32 devices in a mesh: event: 4 (over x, core), row: 2 (over y), col: 4 (over z).
Axes of the slice: x: 2, y: 2, z: 4, core: 2. Of those that a mesh axis runs over, the one named last changes fastest.
Arguments:
- depth_states: float32 [8, 3, 128, 4096], P('event', None, 'row', 'col'), may hold values from 0.8 to 1.2
- wet_mask: int32 [8, 128, 4096], P('event', 'row', 'col'), may hold values 0 or 1
- bed: float32 [128, 4096], P('row', 'col'), may hold values from -0.5 to 0.5
- log_manning: float32 [128, 4096], P('row', 'col'), may hold values from -0.4 to 0.4
- direction: float32 [128, 4096], P('row', 'col'), may hold values from -12 to 12
- gauge_cells: int32 [8, 2, 4, 1024], P('event', 'row', 'col'), may hold values from 0 to 65535
Outputs:
- hess_product: float32 [128, 4096], P('row', 'col')
- curvature: float32 [], replicated
The draws below stay inside these ranges and needn't reach their ends.
All inputs are finite; a program needn't handle non-finite values. No bound on the sum of `wet_mask` on one device may be relied on, other than what follows from the above.
Results may differ from the reference program's by a relative error of at most 0.0003.
Values sent between devices are 32-bit elements; how exact they have to be, the bound alone decides.
No kernel may reach another device: no remote copies, remote signals or barrier semaphores. Data moves between devices by JAX's collectives and lax.ppermute only.
A program may use at most 128 MiB of HBM per device.

```python
import jax
import jax.numpy as jnp
from jax import lax

STEPS = 3
TR = 64
TC = 1024
EVENTS = 8
NR = 128
NC = 4096
BLOCK_ROWS = 2
BLOCK_COLS = 4
GT = 1024
N_ROW = 2
N_COL = 4


def draw_direction(key, part):
    height = jnp.arange(NR, dtype=jnp.float32)[:, None] / NR
    base = jnp.clip(jax.random.normal(key, (NR, NC), jnp.float32), -4.0, 4.0)
    ramp = 1.0 + 2.0 * height
    return (base * ramp).astype(jnp.float32)


def with_ends(entries, stream_key, smallest, top_value):
    extent = entries.shape
    index_at = [jax.random.randint(jax.random.fold_in(stream_key, axis), (), 0, extent[axis]) for axis in range(len(extent))]
    entries = entries.at[tuple(index_at)].set(smallest)
    longest = extent.index(max(extent))
    index_at[longest] = (index_at[longest] + 1) % extent[longest]
    return entries.at[tuple(index_at)].set(top_value)


def level_of(stream_key, shape, split, least, top_value):
    gain, own = 1.0, jax.random.fold_in(stream_key, 6)
    for axis_at, shards_of in split:
        heights = jnp.exp(jax.random.uniform(jax.random.fold_in(own, axis_at), (shards_of,), jnp.float32, least / len(split), top_value / len(split)))
        gain = gain * jnp.repeat(heights, shape[axis_at] // shards_of).reshape([-1 if axis == axis_at else 1 for axis in range(len(shape))])
    return gain


def scatter_about(key, dims, scale, bound, split=(), kind=jnp.bfloat16):
    entries = jax.random.normal(key, dims, jnp.float32) * scale
    if len(split) > 0:
        entries = level_of(key, dims, split, -0.22, 0.18) * entries
    return jnp.clip(entries, min=-bound, max=bound).astype(kind)


def setup_inputs(seed: int = 0) -> dict:
    keys = jax.random.split(jax.random.key(seed), 7)
    return {
        "depth_states": jnp.clip(0.8 + 0.40000004 * jax.random.uniform(keys[0], (EVENTS, STEPS, NR, NC), jnp.float32) ** level_of(keys[0], (EVENTS, STEPS, NR, NC), ((0, 4), (2, 2), (3, 4)), -0.2, 0.2), 0.8, 1.2),
        "wet_mask": with_ends((jax.random.randint(keys[1], (EVENTS, NR, NC), 0, 8) < 7).astype(jnp.int32), jax.random.fold_in(keys[1], 1), 0, 1),
        "bed": scatter_about(keys[2], (NR, NC), 0.1, 0.5, ((0, 2), (1, 4)), jnp.float32),
        "log_manning": jnp.clip(jax.random.uniform(keys[3], (NR, NC), jnp.float32, -0.4, 0.4) * level_of(keys[3], (NR, NC), ((0, 2), (1, 4)), -0.4, 0.0), -0.4, 0.4),
        "direction": draw_direction(jax.random.fold_in(keys[6], 71), 0),
        "gauge_cells": with_ends(jax.random.randint(keys[5], (EVENTS, BLOCK_ROWS, BLOCK_COLS, GT), 0, TR * TC), jax.random.fold_in(keys[5], 1), 0, (TR * TC) - 1).astype(jnp.int32),
    }


time_step = 0.035
slope_floor = 0.01
gauge_weight = 100.0

def advance(depth_pad, wet_pad, bed_pad, rough_pad):
    surface = depth_pad + bed_pad
    manning = jnp.exp(rough_pad)

    def inner(array, down, right):
        height = array.shape[-2] - 2
        width = array.shape[-1] - 2
        return array[..., 1 + down:1 + down + height, 1 + right:1 + right + width]
    depth_here = inner(depth_pad, 0, 0)
    wet_here = inner(wet_pad, 0, 0)
    surface_here = inner(surface, 0, 0)
    manning_here = inner(manning, 0, 0)
    inflow = jnp.zeros(depth_here.shape, jnp.float32)
    for down, right in ((-1, 0), (1, 0), (0, -1), (0, 1)):
        face_depth = 0.5 * (depth_here + inner(depth_pad, down, right))
        face_rough = 0.5 * (manning_here + inner(manning, down, right))
        slope = inner(surface, down, right) - surface_here
        conduct = wet_here * inner(wet_pad, down, right) * face_depth ** (5.0 / 3.0) / face_rough
        inflow = inflow + conduct * slope * (slope * slope + slope_floor) ** (-0.25)
    return depth_here + time_step * inflow

def padded(array):
    return jnp.pad(array, ((1, 1), (1, 1)))

def reference(depth_states, wet_mask, bed, log_manning, direction, gauge_cells):
    bed_pad = padded(bed)
    rough_pad = padded(log_manning)
    direction_pad = padded(direction)
    block_row = jnp.arange(N_ROW, dtype=jnp.int32)[:, None, None] * TR
    block_col = jnp.arange(N_COL, dtype=jnp.int32)[None, :, None] * TC

    def one_event(total, inputs):
        states, wet_flags, gauges = inputs
        wet_pad = padded(wet_flags.astype(jnp.float32))
        tangent = jax.jvp(lambda rough: advance(padded(states[0]), wet_pad, bed_pad, rough), (rough_pad,), (direction_pad,))[1]
        for moment in range(1, STEPS):
            tangent = jax.jvp(lambda depth, rough: advance(depth, wet_pad, bed_pad, rough), (padded(states[moment]), rough_pad), (padded(tangent), direction_pad))[1]
        gauge_rows = block_row + gauges // TC
        gauge_cols = block_col + gauges % TC
        observed = tangent[gauge_rows, gauge_cols]
        adjoint = jnp.zeros((NR, NC), jnp.float32).at[gauge_rows, gauge_cols].add(gauge_weight * observed)
        gradient = jnp.zeros((NR, NC), jnp.float32)
        for moment in range(STEPS - 1, -1, -1):
            _, pull = jax.vjp(lambda depth, rough: advance(padded(depth), wet_pad, bed_pad, padded(rough)), states[moment], log_manning)
            depth_back, rough_back = pull(adjoint)
            gradient = gradient + rough_back
            adjoint = depth_back
        return (total + gradient, None)
    hess_product = lax.scan(one_event, jnp.zeros((NR, NC), jnp.float32), (depth_states, wet_mask, gauge_cells))[0]
    curvature = jnp.sum(direction * hess_product)
    return (hess_product, curvature)
```

```python
import functools

import jax
import jax.numpy as jnp
from jax import lax
from jax.experimental import pallas as pl
from jax.experimental.pallas import tpu as pltpu
from jax.sharding import PartitionSpec as P

time_step = 0.035
slope_floor = 0.01
gauge_weight = 100.0
REACH = 6
LANES = 128
SUB = 8


def pairs(count, first):
    out = []
    for i in range(first, count - 1, 2):
        out += [(i, i + 1), (i + 1, i)]
    return out


def exchange(x, axis, first):
    perm = pairs(lax.axis_size(axis), first)
    return lax.ppermute(x, axis, perm) if perm else None


def lanes_of(shape):
    return lax.broadcasted_iota(jnp.int32, shape, 1)


def gauge_kernel(par, g_ref, da, wa, ba, ra, va, db, wb, bb, rb, vb, cnt, pay_a, pay_b):
    events, rows, cols = cnt.shape
    gauges = g_ref.shape[-1]
    tall = rows * cols // 256
    which = lax.broadcasted_iota(jnp.int32, (tall, gauges), 0)
    low = lax.broadcasted_iota(jnp.int32, (256, gauges), 0)
    one = lambda hit: jnp.where(hit, 1.0, 0.0).astype(jnp.bfloat16)
    steps = da.shape[1]
    edge_a = pl.multiple_of((par[0] * (rows // SUB - 1)) * SUB, SUB)
    edge_b = pl.multiple_of((rows - SUB) - edge_a, SUB)
    for e in range(events):
        g = g_ref[e]
        row, col = g // cols, g % cols
        high = (col // 256) * rows + row
        tally = lax.dot_general(
            one(which == high),
            one(low == col % 256),
            (((1,), (1,)), ((), ())),
            preferred_element_type=jnp.float32,
        )
        for b in range(cols // 256):
            cnt[e, :, b * 256 : (b + 1) * 256] = tally[b * rows : (b + 1) * rows]
    for pay, d, w, b, r, v, edge in (
        (pay_a, da, wa, ba, ra, va, edge_a),
        (pay_b, db, wb, bb, rb, vb, edge_b),
    ):
        for e in range(events):
            for t in range(steps):
                pay[e * steps + t] = d[e, t]
            pay[events * steps + e] = w[e].astype(jnp.float32)
            pay[events * (steps + 1) + 3 + e] = cnt[e, pl.ds(edge, SUB), :]
        base = events * (steps + 1)
        pay[base], pay[base + 1], pay[base + 2] = b[...], r[...], v[...]


def gauges_and_rows(par, cells, depth, wet, bed, rough, direction):
    events, steps, rows, cols = depth.shape
    top = rows // SUB - 1
    fields = events * (steps + 2) + 3

    def edges(flip):
        at = lambda p: (1 - p[0] if flip else p[0]) * top
        return [
            pl.BlockSpec((events, steps, SUB, cols), lambda i, p: (0, 0, at(p), 0)),
            pl.BlockSpec((events, SUB, cols), lambda i, p: (0, at(p), 0)),
        ] + [pl.BlockSpec((SUB, cols), lambda i, p: (at(p), 0))] * 3

    whole = lambda shape: pl.BlockSpec(shape, lambda i, p: (0,) * len(shape))
    return pl.pallas_call(
        gauge_kernel,
        grid_spec=pltpu.PrefetchScalarGridSpec(
            num_scalar_prefetch=1,
            grid=(1,),
            in_specs=[whole(cells.shape)] + edges(False) + edges(True),
            out_specs=[whole((events, rows, cols))] + [whole((fields, SUB, cols))] * 2,
        ),
        out_shape=[jax.ShapeDtypeStruct((events, rows, cols), jnp.float32)]
        + [jax.ShapeDtypeStruct((fields, SUB, cols), jnp.float32)] * 2,
        name="gauges_and_rows",
    )(par, cells, *(depth, wet, bed, rough, direction) * 2)


def column_kernel(par, *refs):
    sides = (refs[0:6], refs[6:12])
    rims = refs[12:16]
    pay_a, pay_b = refs[16:18]
    events, steps, rows, _ = sides[0][0].shape
    even_row = par[0] == 1
    even_col = par[1] == 1
    packs = []
    for side in range(2):
        d, w, b, r, v, c = sides[side]
        rim_a, rim_b = rims[2 * side], rims[2 * side + 1]
        lane = lanes_of((rows + 2 * SUB, LANES))
        pack = jnp.zeros((rows + 2 * SUB, LANES), jnp.float32)
        own = [d[e, t] for e in range(events) for t in range(steps)]
        own += [w[e].astype(jnp.float32) for e in range(events)]
        own += [b[...], r[...], v[...]]
        own += [c[e] for e in range(events)]
        for f, x in enumerate(own):
            top = jnp.where(even_row, rim_b[f], rim_a[f])
            bottom = jnp.where(even_row, rim_a[f], rim_b[f])
            x = jnp.concatenate([top, x, bottom], axis=0)
            place = f * REACH
            shift = (place + REACH if side == 1 else place) % LANES
            if shift:
                x = pltpu.roll(x, shift, 1)
            pack = jnp.where((lane >= place) & (lane < place + REACH), x, pack)
        packs.append(pack)
    pay_a[...] = jnp.where(even_col, packs[1], packs[0])
    pay_b[...] = jnp.where(even_col, packs[0], packs[1])


def edge_columns(par, depth, wet, bed, rough, direction, counts, rim_a, rim_b):
    events, steps, rows, cols = depth.shape
    fields = rim_a.shape[0]
    last = cols // LANES - 1

    def side(j):
        return [
            pl.BlockSpec((events, steps, rows, LANES), lambda i, p: (0, 0, 0, j)),
            pl.BlockSpec((events, rows, LANES), lambda i, p: (0, 0, j)),
            pl.BlockSpec((rows, LANES), lambda i, p: (0, j)),
            pl.BlockSpec((rows, LANES), lambda i, p: (0, j)),
            pl.BlockSpec((rows, LANES), lambda i, p: (0, j)),
            pl.BlockSpec((events, rows, LANES), lambda i, p: (0, 0, j)),
        ]

    rim = lambda j: [pl.BlockSpec((fields, SUB, LANES), lambda i, p: (0, 0, j))] * 2
    tall = (rows + 2 * SUB, LANES)
    own = (depth, wet, bed, rough, direction, counts)
    return pl.pallas_call(
        column_kernel,
        grid_spec=pltpu.PrefetchScalarGridSpec(
            num_scalar_prefetch=1,
            grid=(1,),
            in_specs=side(0) + side(last) + rim(0) + rim(last),
            out_specs=[pl.BlockSpec(tall, lambda i, p: (0, 0))] * 2,
        ),
        out_shape=[jax.ShapeDtypeStruct(tall, jnp.float32)] * 2,
        name="edge_columns",
    )(par, *own, *own, rim_a, rim_b, rim_a, rim_b)


def model_kernel(
    par, depth, wet, bed, rough, direction, counts, rim_a, rim_b, side_a, side_b,
    grad_ref, curve_ref,
    hx, wx, bx, mx, qx, cx, inv_x, inv_y, sum_x, sum_y,
    a_x, b_x, c_x, a_y, b_y, c_y, state, work, flow, g_x, g_y,
):
    events, steps, rows, cols = depth.shape
    tall = rows + 2 * SUB
    tiles = cols // LANES
    count = tiles + 1
    even_row = par[0] == 1
    even_col = par[1] == 1
    lane = lanes_of((tall, LANES))
    right_rim = jnp.where(even_col, side_a[...], side_b[...])
    left_rim = jnp.where(even_col, side_b[...], side_a[...])

    def assemble(f, own, put):
        top = jnp.where(even_row, rim_b[f], rim_a[f])
        bottom = jnp.where(even_row, rim_a[f], rim_b[f])
        put(slice(0, SUB), slice(0, cols), top)
        put(slice(SUB, SUB + rows), slice(0, cols), own)
        put(slice(SUB + rows, tall), slice(0, cols), bottom)
        place = f * REACH
        r = pltpu.roll(right_rim, (LANES - place) % LANES, 1) if place else right_rim
        l = pltpu.roll(left_rim, (LANES - REACH - place) % LANES, 1)
        extra = jnp.where(lane < REACH, r, jnp.where(lane >= LANES - REACH, l, 0.0))
        put(slice(0, tall), slice(cols, cols + LANES), extra)

    def into(ref, *lead):
        def put(rs, cs, x):
            ref[(*lead, rs, cs)] = x

        return put

    for e in range(events):
        for t in range(steps):
            assemble(e * steps + t, depth[e, t], into(hx, e, t))
        assemble(events * steps + e, wet[e].astype(jnp.float32), into(wx, e))
        assemble(events * (steps + 1) + 3 + e, counts[e], into(cx, e))
    base = events * (steps + 1)
    assemble(base, bed[...], into(bx))
    assemble(base + 1, rough[...], into(mx))
    assemble(base + 2, direction[...], into(qx))

    def at(j):
        return pl.ds(pl.multiple_of(j * LANES, LANES), LANES)

    def after(j):
        return jnp.where(j == count - 1, 0, j + 1)

    def before(j):
        return jnp.where(j == 0, count - 1, j - 1)

    below = lambda x: pltpu.roll(x, tall - 1, 0)
    above = lambda x: pltpu.roll(x, 1, 0)

    def right(x, nxt):
        return jnp.where(lane == LANES - 1, pltpu.roll(nxt, LANES - 1, 1), pltpu.roll(x, LANES - 1, 1))

    def left(x, prv):
        return jnp.where(lane == 0, pltpu.roll(prv, 1, 1), pltpu.roll(x, 1, 1))

    @pl.loop(0, count)
    def _(j):
        m = jnp.exp(mx[:, at(j)])
        mx[:, at(j)] = m
        qx[:, at(j)] = m * qx[:, at(j)]

    scale = time_step * 2.0 ** (-2.0 / 3.0)

    @pl.loop(0, count)
    def _(j):
        n = after(j)
        m, q = mx[:, at(j)], qx[:, at(j)]
        inv_x[:, at(j)] = 1.0 / (m + right(m, mx[:, at(n)]))
        inv_y[:, at(j)] = 1.0 / (m + below(m))
        sum_x[:, at(j)] = q + right(q, qx[:, at(n)])
        sum_y[:, at(j)] = q + below(q)
        g_x[:, at(j)] = jnp.zeros((tall, LANES), jnp.float32)
        g_y[:, at(j)] = jnp.zeros((tall, LANES), jnp.float32)

    def face(h, h_k, s, cond, inv):
        hs = h + h_k
        x = s * s + slope_floor
        lx = jnp.log(x)
        p = cond * jnp.exp((2.0 / 3.0) * jnp.log(hs) - 0.25 * lx)
        t = p * hs
        return (
            (5.0 / 3.0) * (p * s),
            t * (0.5 + (0.5 * slope_floor) * jnp.exp(-lx)),
            -(t * s) * inv,
        )

    curve_ref[...] = jnp.zeros(curve_ref.shape, jnp.float32)

    @pl.loop(0, events)
    def _(e):
        for t in range(steps):

            @pl.loop(0, count)
            def _(j):
                n = after(j)
                h, b = hx[e, t, :, at(j)], bx[:, at(j)]
                w = wx[e, :, at(j)]
                h_n = hx[e, t, :, at(n)]
                surface = h + b
                inv = inv_x[:, at(j)]
                A, B, C = face(
                    h,
                    right(h, h_n),
                    right(surface, h_n + bx[:, at(n)]) - surface,
                    (scale * inv) * (w * right(w, wx[e, :, at(n)])),
                    inv,
                )
                inv = inv_y[:, at(j)]
                A2, B2, C2 = face(
                    h,
                    below(h),
                    below(surface) - surface,
                    (scale * inv) * (w * below(w)),
                    inv,
                )
                c_x[t, :, at(j)] = C
                c_y[t, :, at(j)] = C2
                fx = C * sum_x[:, at(j)]
                fy = C2 * sum_y[:, at(j)]
                if t:
                    a_x[t - 1, :, at(j)] = A
                    b_x[t - 1, :, at(j)] = B
                    a_y[t - 1, :, at(j)] = A2
                    b_y[t - 1, :, at(j)] = B2
                    d = state[:, at(j)]
                    k = right(d, state[:, at(n)])
                    fx += A * (d + k) + B * (k - d)
                    k = below(d)
                    fy += A2 * (d + k) + B2 * (k - d)
                    work[:, at(j)] = d + fx + (fy - above(fy))
                else:
                    work[:, at(j)] = fx + (fy - above(fy))
                flow[:, at(j)] = fx

            @pl.loop(0, count)
            def _(j):
                r = work[:, at(j)] - left(flow[:, at(j)], flow[:, at(before(j))])
                if t == steps - 1:
                    c = cx[e, :, at(j)] * gauge_weight
                    s = c * r

                    @pl.when(j < tiles)
                    def _():
                        own = (s * r)[SUB : SUB + rows]
                        total = own[0:SUB]
                        for i in range(1, rows // SUB):
                            total += own[i * SUB : (i + 1) * SUB]
                        curve_ref[...] += total

                    r = s
                state[:, at(j)] = r

        for t in range(steps - 1, -1, -1):

            @pl.loop(0, count)
            def _(j):
                n = after(j)
                l = state[:, at(j)]
                px = l - right(l, state[:, at(n)])
                py = l - below(l)
                g_x[:, at(j)] += c_x[t, :, at(j)] * px
                g_y[:, at(j)] += c_y[t, :, at(j)] * py
                if t:
                    u, v = a_x[t - 1, :, at(j)] * px, b_x[t - 1, :, at(j)] * px
                    u2, v2 = a_y[t - 1, :, at(j)] * py, b_y[t - 1, :, at(j)] * py
                    work[:, at(j)] = l + (u - v) + (u2 - v2) + above(u2 + v2)
                    flow[:, at(j)] = u + v

            if t:

                @pl.loop(0, count)
                def _(j):
                    state[:, at(j)] = work[:, at(j)] + left(
                        flow[:, at(j)], flow[:, at(before(j))]
                    )

    @pl.loop(0, tiles)
    def _(j):
        x, y = g_x[:, at(j)], g_y[:, at(j)]
        g = mx[:, at(j)] * ((x + left(x, g_x[:, at(before(j))])) + (y + above(y)))
        grad_ref[:, at(j)] = g[SUB : SUB + rows]


def model(par, depth, wet, bed, rough, direction, counts, rim_a, rim_b, side_a, side_b):
    events, steps, rows, cols = depth.shape
    tall, wide = rows + 2 * SUB, cols + LANES
    f32 = functools.partial(pltpu.VMEM, dtype=jnp.float32)
    vm = lambda *lead: pltpu.VMEM((*lead, tall, wide), jnp.float32)
    vmem = pl.BlockSpec(memory_space=pltpu.VMEM)
    return pl.pallas_call(
        model_kernel,
        in_specs=[pl.BlockSpec(memory_space=pltpu.SMEM)] + [vmem] * 10,
        out_specs=[vmem] * 2,
        out_shape=[
            jax.ShapeDtypeStruct((rows, cols), jnp.float32),
            jax.ShapeDtypeStruct((SUB, LANES), jnp.float32),
        ],
        scratch_shapes=[vm(events, steps), vm(events), vm(), vm(), vm(), vm(events)]
        + [vm()] * 4
        + [vm(steps - 1), vm(steps - 1), vm(steps)] * 2
        + [vm()] * 5,
        compiler_params=pltpu.CompilerParams(vmem_limit_bytes=56 * 1024 * 1024),
        name="model",
    )(par, depth, wet, bed, rough, direction, counts, rim_a, rim_b, side_a, side_b)


def total_over(x, axis):
    count = lax.axis_size(axis)
    hop = 1
    while hop < count:
        x = x + lax.ppermute(x, axis, [(i, i ^ hop) for i in range(count)])
        hop *= 2
    return x


def local(depth, wet, bed, rough, direction, gauge_cells):
    events, steps, rows, cols = depth.shape
    cells = gauge_cells.reshape(events, 1, -1)
    par = jnp.stack([1 - lax.axis_index("row") % 2, 1 - lax.axis_index("col") % 2]).astype(jnp.int32)
    counts, pay_a, pay_b = gauges_and_rows(par, cells, depth, wet, bed, rough, direction)
    rim_a = exchange(pay_a, "row", 0)
    rim_b = exchange(pay_b, "row", 1)
    if rim_b is None:
        rim_b = jnp.zeros_like(rim_a)
    send_a, send_b = edge_columns(par, depth, wet, bed, rough, direction, counts, rim_a, rim_b)
    side_a = exchange(send_a, "col", 0)
    side_b = exchange(send_b, "col", 1)
    grad, curve = model(par, depth, wet, bed, rough, direction, counts, rim_a, rim_b, side_a, side_b)
    hess_product = total_over(grad, "event")
    c = total_over(total_over(total_over(curve, "event"), "row"), "col")
    return (hess_product, jnp.sum(c))


def solution(mesh):
    placed = (
        P("event", None, "row", "col"),
        P("event", "row", "col"),
        P("row", "col"),
        P("row", "col"),
        P("row", "col"),
        P("event", "row", "col", None),
    )
    return jax.shard_map(
        local, mesh=mesh, in_specs=placed, out_specs=(P("row", "col"), P()), check_vma=False
    )
```

```python
import functools

import jax
import jax.numpy as jnp
from jax import lax
from jax.experimental import pallas as pl
from jax.experimental.pallas import tpu as pltpu
from jax.sharding import PartitionSpec as P

time_step = 0.035
slope_floor = 0.01
gauge_weight = 100.0
REACH = 6
LANES = 128
LN2 = 0.6931471805599453
SUB = 8


def pairs(count, first):
    out = []
    for i in range(first, count - 1, 2):
        out += [(i, i + 1), (i + 1, i)]
    return out


def exchange(x, axis, first):
    perm = pairs(lax.axis_size(axis), first)
    return lax.ppermute(x, axis, perm) if perm else None


def lanes_of(shape):
    return lax.broadcasted_iota(jnp.int32, shape, 1)


def gauge_kernel(par, g_ref, da, wa, ba, ra, va, db, wb, bb, rb, vb, cnt, pay_a, pay_b):
    events, rows, cols = cnt.shape
    gauges = g_ref.shape[-1]
    tall = rows * cols // 256
    which = lax.broadcasted_iota(jnp.int32, (tall, gauges), 0)
    low = lax.broadcasted_iota(jnp.int32, (256, gauges), 0)
    one = lambda hit: jnp.where(hit, 1.0, 0.0).astype(jnp.bfloat16)
    steps = da.shape[1]
    edge_a = pl.multiple_of((par[0] * (rows // SUB - 1)) * SUB, SUB)
    edge_b = pl.multiple_of((rows - SUB) - edge_a, SUB)
    for e in range(events):
        g = g_ref[e]
        row, col = g // cols, g % cols
        high = (col // 256) * rows + row
        tally = lax.dot_general(
            one(which == high),
            one(low == col % 256),
            (((1,), (1,)), ((), ())),
            preferred_element_type=jnp.float32,
        )
        for b in range(cols // 256):
            cnt[e, :, b * 256 : (b + 1) * 256] = tally[b * rows : (b + 1) * rows]
    for pay, d, w, b, r, v, edge in (
        (pay_a, da, wa, ba, ra, va, edge_a),
        (pay_b, db, wb, bb, rb, vb, edge_b),
    ):
        for e in range(events):
            for t in range(steps):
                pay[e * steps + t] = d[e, t]
            pay[events * steps + e] = w[e].astype(jnp.float32)
            pay[events * (steps + 1) + 3 + e] = cnt[e, pl.ds(edge, SUB), :]
        base = events * (steps + 1)
        pay[base], pay[base + 1], pay[base + 2] = b[...], r[...], v[...]


def gauges_and_rows(par, cells, depth, wet, bed, rough, direction):
    events, steps, rows, cols = depth.shape
    top = rows // SUB - 1
    fields = events * (steps + 2) + 3

    def edges(flip):
        at = lambda p: (1 - p[0] if flip else p[0]) * top
        return [
            pl.BlockSpec((events, steps, SUB, cols), lambda i, p: (0, 0, at(p), 0)),
            pl.BlockSpec((events, SUB, cols), lambda i, p: (0, at(p), 0)),
        ] + [pl.BlockSpec((SUB, cols), lambda i, p: (at(p), 0))] * 3

    whole = lambda shape: pl.BlockSpec(shape, lambda i, p: (0,) * len(shape))
    return pl.pallas_call(
        gauge_kernel,
        grid_spec=pltpu.PrefetchScalarGridSpec(
            num_scalar_prefetch=1,
            grid=(1,),
            in_specs=[whole(cells.shape)] + edges(False) + edges(True),
            out_specs=[whole((events, rows, cols))] + [whole((fields, SUB, cols))] * 2,
        ),
        out_shape=[jax.ShapeDtypeStruct((events, rows, cols), jnp.float32)]
        + [jax.ShapeDtypeStruct((fields, SUB, cols), jnp.float32)] * 2,
        compiler_params=pltpu.CompilerParams(vmem_limit_bytes=56 * 1024 * 1024),
        name="gauges_and_rows",
    )(par, cells, *(depth, wet, bed, rough, direction) * 2)


def column_kernel(par, *refs):
    sides = (refs[0:6], refs[6:12])
    rims = refs[12:16]
    pay_a, pay_b = refs[16:18]
    events, steps, rows, _ = sides[0][0].shape
    even_row = par[0] == 1
    even_col = par[1] == 1
    packs = []
    for side in range(2):
        d, w, b, r, v, c = sides[side]
        rim_a, rim_b = rims[2 * side], rims[2 * side + 1]
        lane = lanes_of((rows + 2 * SUB, LANES))
        pack = jnp.zeros((rows + 2 * SUB, LANES), jnp.float32)
        own = [d[e, t] for e in range(events) for t in range(steps)]
        own += [w[e].astype(jnp.float32) for e in range(events)]
        own += [b[...], r[...], v[...]]
        own += [c[e] for e in range(events)]
        for f, x in enumerate(own):
            top = jnp.where(even_row, rim_b[f], rim_a[f])
            bottom = jnp.where(even_row, rim_a[f], rim_b[f])
            x = jnp.concatenate([top, x, bottom], axis=0)
            place = f * REACH
            shift = (place + REACH if side == 1 else place) % LANES
            if shift:
                x = pltpu.roll(x, shift, 1)
            pack = jnp.where((lane >= place) & (lane < place + REACH), x, pack)
        packs.append(pack)
    pay_a[...] = jnp.where(even_col, packs[1], packs[0])
    pay_b[...] = jnp.where(even_col, packs[0], packs[1])


def edge_columns(par, depth, wet, bed, rough, direction, counts, rim_a, rim_b):
    events, steps, rows, cols = depth.shape
    fields = rim_a.shape[0]
    last = cols // LANES - 1

    def side(j):
        return [
            pl.BlockSpec((events, steps, rows, LANES), lambda i, p: (0, 0, 0, j)),
            pl.BlockSpec((events, rows, LANES), lambda i, p: (0, 0, j)),
            pl.BlockSpec((rows, LANES), lambda i, p: (0, j)),
            pl.BlockSpec((rows, LANES), lambda i, p: (0, j)),
            pl.BlockSpec((rows, LANES), lambda i, p: (0, j)),
            pl.BlockSpec((events, rows, LANES), lambda i, p: (0, 0, j)),
        ]

    rim = lambda j: [pl.BlockSpec((fields, SUB, LANES), lambda i, p: (0, 0, j))] * 2
    tall = (rows + 2 * SUB, LANES)
    own = (depth, wet, bed, rough, direction, counts)
    return pl.pallas_call(
        column_kernel,
        grid_spec=pltpu.PrefetchScalarGridSpec(
            num_scalar_prefetch=1,
            grid=(1,),
            in_specs=side(0) + side(last) + rim(0) + rim(last),
            out_specs=[pl.BlockSpec(tall, lambda i, p: (0, 0))] * 2,
        ),
        out_shape=[jax.ShapeDtypeStruct(tall, jnp.float32)] * 2,
        compiler_params=pltpu.CompilerParams(vmem_limit_bytes=12 * 1024 * 1024),
        name="edge_columns",
    )(par, *own, *own, rim_a, rim_b, rim_a, rim_b)


def model_kernel(
    par, depth, wet, bed, rough, direction, counts, rim_a, rim_b, side_a, side_b,
    grad_ref, curve_ref,
    nat, hx, sb_x, sb_y, m_c, q_x, q_y, inv_x, inv_y, cond_x, cond_y, cnt,
    a_x, b_x, c_x, a_y, b_y, c_y, tan_a, tan_b, flow, g_x, g_y, tmp,
):
    events, steps, rows, cols = depth.shape
    tall = rows + 2 * SUB
    deep = tall // SUB
    tiles = cols // LANES
    count = tiles + 1
    even_row = par[0] == 1
    even_col = par[1] == 1
    lane_t = lanes_of((tall, LANES))
    lane = lanes_of((SUB, LANES))
    sub = lax.broadcasted_iota(jnp.int32, (SUB, LANES), 0)
    last_lane, first_lane = lane == LANES - 1, lane == 0
    right_rim = jnp.where(even_col, side_a[...], side_b[...])
    left_rim = jnp.where(even_col, side_b[...], side_a[...])
    J = [slice(j * LANES, (j + 1) * LANES) for j in range(count)]
    zero = jnp.zeros((SUB, LANES), jnp.float32)

    def assemble(f, own, k):
        top = jnp.where(even_row, rim_b[f], rim_a[f])
        bottom = jnp.where(even_row, rim_a[f], rim_b[f])
        for j in range(tiles):
            nat[k, j, 0:SUB, :] = top[:, J[j]]
            nat[k, j, SUB : SUB + rows, :] = own[:, J[j]]
            nat[k, j, SUB + rows : tall, :] = bottom[:, J[j]]
        place = f * REACH
        r = pltpu.roll(right_rim, (LANES - place) % LANES, 1) if place else right_rim
        l = pltpu.roll(left_rim, (LANES - REACH - place) % LANES, 1)
        extra = jnp.where(lane_t < REACH, r, jnp.where(lane_t >= LANES - REACH, l, 0.0))
        nat[k, tiles] = extra

    def spread(k, i):
        return [nat[k, j, pl.ds(i, SUB, stride=deep), :] for j in range(count)]

    up = lambda x: pltpu.roll(x, SUB - 1, 0)
    down = lambda x: pltpu.roll(x, 1, 0)
    to_left = lambda x: pltpu.roll(x, LANES - 1, 1)
    to_right = lambda x: pltpu.roll(x, 1, 1)

    def right(xs):
        r = [to_left(x) for x in xs]
        return [jnp.where(last_lane, r[(j + 1) % count], r[j]) for j in range(count)]

    def left(xs):
        r = [to_right(x) for x in xs]
        return [jnp.where(first_lane, r[j - 1], r[j]) for j in range(count)]

    def get(ref, *at):
        return [ref[(*at, slice(None), J[j])] for j in range(count)]

    def put(xs, ref, *at):
        for j in range(count):
            ref[(*at, slice(None), J[j])] = xs[j]

    def wrap(ref, *at):
        put([up(x) for x in get(ref, *at, 0)], ref, *at, deep)

    base = events * (steps + 1)
    for k, (f, x) in enumerate(((base, bed), (base + 1, rough), (base + 2, direction))):
        assemble(f, x[...], k)
    for e in range(events):
        assemble(events * steps + e, wet[e].astype(jnp.float32), 3 + e)
        assemble(base + 3 + e, counts[e], 3 + events + e)
        for t in range(steps):
            assemble(e * steps + t, depth[e, t], 3 + 2 * events + e * steps + t)

    @pl.loop(0, deep, unroll=5)
    def _(i):
        m = [jnp.exp(x) for x in spread(1, i)]
        put(spread(0, i), tmp, 0, i)
        put(m, tmp, 1, i)
        put(m, m_c, i)
        put([x * y for x, y in zip(m, spread(2, i))], tmp, 2, i)
        for e in range(events):
            put(spread(3 + e, i), tmp, 3 + e, i)
            put(spread(3 + events + e, i), cnt, e, i)
            for t in range(steps):
                put(spread(3 + 2 * events + e * steps + t, i), hx, e, t, i)

    for k in range(3 + events):
        wrap(tmp, k)
    for e in range(events):
        for t in range(steps):
            wrap(hx, e, t)

    scale = time_step * 2.0 ** (-2.0 / 3.0)

    @pl.loop(0, deep, unroll=5)
    def _(i):
        b, m, q = (get(tmp, k, i) for k in range(3))
        put([y - x for x, y in zip(b, right(b))], sb_x, i)
        put([y - x for x, y in zip(b, get(tmp, 0, i + 1))], sb_y, i)
        ix = [1.0 / (x + y) for x, y in zip(m, right(m))]
        iy = [1.0 / (x + y) for x, y in zip(m, get(tmp, 1, i + 1))]
        put([-x for x in ix], inv_x, i)
        put([-x for x in iy], inv_y, i)
        put([x + y for x, y in zip(q, right(q))], q_x, i)
        put([x + y for x, y in zip(q, get(tmp, 2, i + 1))], q_y, i)
        for e in range(events):
            w = get(tmp, 3 + e, i)
            put([(scale * z) * (x * y) for x, y, z in zip(w, right(w), ix)], cond_x, e, i)
            put([(scale * z) * (x * y) for x, y, z in zip(w, get(tmp, 3 + e, i + 1), iy)], cond_y, e, i)
        put([zero] * count, g_x, i)
        put([zero] * count, g_y, i)

    def face(h, h_k, sb, cond, inv):
        hs = h + h_k
        s = (h_k - h) + sb
        x = s * s + slope_floor
        y = lax.rsqrt(x)
        p = cond * (jnp.exp2((2.0 / 3.0 / LN2) * jnp.log(hs)) * (y * lax.rsqrt(y)))
        ps = p * s
        t = p * hs
        A = (5.0 / 3.0) * ps
        B = t * (0.5 + (0.5 * slope_floor) * (y * y))
        return A - B, A + B, (ps * hs) * inv

    curve_ref[...] = jnp.zeros(curve_ref.shape, jnp.float32)
    put([zero] * count, flow, 0)

    @pl.loop(0, events)
    def _(e):
        for t in range(steps):
            old, new = (tan_a, tan_b) if t % 2 else (tan_b, tan_a)

            @pl.loop(0, deep, unroll=5)
            def _(i):
                h = get(hx, e, t, i)
                h_r, h_d = right(h), get(hx, e, t, i + 1)
                if t:
                    d = get(old, i)
                    d_r, d_d = right(d), get(old, i + 1)
                fx, fy = [], []
                for j in range(count):
                    A, B, C = face(h[j], h_r[j], sb_x[i, :, J[j]], cond_x[e, i, :, J[j]], inv_x[i, :, J[j]])
                    f = C * q_x[i, :, J[j]]
                    c_x[t, i, :, J[j]] = C
                    if t:
                        a_x[t - 1, i, :, J[j]] = A
                        b_x[t - 1, i, :, J[j]] = B
                        f += A * d[j] + B * d_r[j]
                    fx.append(f)
                    A, B, C = face(h[j], h_d[j], sb_y[i, :, J[j]], cond_y[e, i, :, J[j]], inv_y[i, :, J[j]])
                    f = C * q_y[i, :, J[j]]
                    c_y[t, i, :, J[j]] = C
                    if t:
                        a_y[t - 1, i, :, J[j]] = A
                        b_y[t - 1, i, :, J[j]] = B
                        f += A * d[j] + B * d_d[j]
                    fy.append(f)
                put(fy, flow, i + 1)
                before = get(flow, i)
                fl = left(fx)
                for j in range(count):
                    r = (fx[j] - fl[j]) + (fy[j] - before[j])
                    new[i, :, J[j]] = d[j] + r if t else r

            for j in range(count):
                new[0, :, J[j]] = new[0, :, J[j]] - down(flow[deep, :, J[j]])
            wrap(new)

        old, new = (tan_a, tan_b) if steps % 2 else (tan_b, tan_a)

        @pl.loop(0, deep, unroll=5)
        def _(i):
            row = sub * deep + i
            own = (row >= SUB) & (row < SUB + rows)
            total = zero
            for j in range(count):
                r = old[i, :, J[j]]
                s = (gauge_weight * cnt[e, i, :, J[j]]) * r
                old[i, :, J[j]] = s
                if j < tiles:
                    total += s * r
            curve_ref[...] += jnp.where(own, total, 0.0)

        wrap(old)

        for t in range(steps - 1, -1, -1):
            back = steps - 1 - t
            old, new = (tan_a, tan_b) if (steps + back) % 2 else (tan_b, tan_a)

            @pl.loop(0, deep, unroll=5)
            def _(i):
                l = get(old, i)
                l_r, l_d = right(l), get(old, i + 1)
                acc, kx, ky = [], [], []
                for j in range(count):
                    p = l[j] - l_r[j]
                    g_x[i, :, J[j]] += c_x[t, i, :, J[j]] * p
                    if t:
                        a = l[j] + a_x[t - 1, i, :, J[j]] * p
                        kx.append(b_x[t - 1, i, :, J[j]] * p)
                    p = l[j] - l_d[j]
                    g_y[i, :, J[j]] += c_y[t, i, :, J[j]] * p
                    if t:
                        acc.append(a + a_y[t - 1, i, :, J[j]] * p)
                        ky.append(b_y[t - 1, i, :, J[j]] * p)
                if t:
                    put(ky, flow, i + 1)
                    before = get(flow, i)
                    kl = left(kx)
                    for j in range(count):
                        new[i, :, J[j]] = acc[j] + (kl[j] + before[j])

            if t:
                for j in range(count):
                    new[0, :, J[j]] = new[0, :, J[j]] + down(flow[deep, :, J[j]])
                wrap(new)

    put([down(x) for x in get(g_y, deep - 1)], flow, 0)

    @pl.loop(0, deep, unroll=5)
    def _(i):
        x, y = get(g_x, i), get(g_y, i)
        put(y, flow, i + 1)
        xl, yl = left(x), get(flow, i)
        for j in range(tiles):
            g = m_c[i, :, J[j]] * ((x[j] + xl[j]) + (y[j] + yl[j]))
            nat[0, j, pl.ds(i, SUB, stride=deep), :] = g

    for j in range(tiles):
        grad_ref[:, J[j]] = nat[0, j, SUB : SUB + rows, :]


def model(par, depth, wet, bed, rough, direction, counts, rim_a, rim_b, side_a, side_b):
    events, steps, rows, cols = depth.shape
    tall, wide = rows + 2 * SUB, cols + LANES
    deep = tall // SUB
    vm = lambda *lead: pltpu.VMEM((*lead, deep, SUB, wide), jnp.float32)
    more = lambda *lead: pltpu.VMEM((*lead, deep + 1, SUB, wide), jnp.float32)
    vmem = pl.BlockSpec(memory_space=pltpu.VMEM)
    fields = 3 + events * (steps + 2)
    return pl.pallas_call(
        model_kernel,
        in_specs=[pl.BlockSpec(memory_space=pltpu.SMEM)] + [vmem] * 10,
        out_specs=[vmem] * 2,
        out_shape=[
            jax.ShapeDtypeStruct((rows, cols), jnp.float32),
            jax.ShapeDtypeStruct((SUB, LANES), jnp.float32),
        ],
        scratch_shapes=[
            pltpu.VMEM((fields, wide // LANES, tall, LANES), jnp.float32),
            more(events, steps),
            *[vm()] * 7,
            *[vm(events)] * 3,
            *[vm(steps - 1), vm(steps - 1), vm(steps)] * 2,
            more(),
            more(),
            more(),
            vm(),
            vm(),
            more(3 + events),
        ],
        compiler_params=pltpu.CompilerParams(vmem_limit_bytes=26 * 1024 * 1024),
        name="model",
    )(par, depth, wet, bed, rough, direction, counts, rim_a, rim_b, side_a, side_b)


def total_over(x, axis):
    count = lax.axis_size(axis)
    hop = 1
    while hop < count:
        x = x + lax.ppermute(x, axis, [(i, i ^ hop) for i in range(count)])
        hop *= 2
    return x


def local(depth, wet, bed, rough, direction, gauge_cells):
    events, steps, rows, cols = depth.shape
    cells = gauge_cells.reshape(events, 1, -1)
    par = jnp.stack([1 - lax.axis_index("row") % 2, 1 - lax.axis_index("col") % 2]).astype(jnp.int32)
    counts, pay_a, pay_b = gauges_and_rows(par, cells, depth, wet, bed, rough, direction)
    rim_a = exchange(pay_a, "row", 0)
    rim_b = exchange(pay_b, "row", 1)
    if rim_b is None:
        rim_b = jnp.zeros_like(rim_a)
    send_a, send_b = edge_columns(par, depth, wet, bed, rough, direction, counts, rim_a, rim_b)
    side_a = exchange(send_a, "col", 0)
    side_b = exchange(send_b, "col", 1)
    grad, curve = model(par, depth, wet, bed, rough, direction, counts, rim_a, rim_b, side_a, side_b)
    hess_product = total_over(grad, "event")
    c = total_over(total_over(total_over(curve, "event"), "row"), "col")
    return (hess_product, jnp.sum(c))


def solution(mesh):
    placed = (
        P("event", None, "row", "col"),
        P("event", "row", "col"),
        P("row", "col"),
        P("row", "col"),
        P("row", "col"),
        P("event", "row", "col", None),
    )
    return jax.shard_map(
        local, mesh=mesh, in_specs=placed, out_specs=(P("row", "col"), P()), check_vma=False
    )
```

```python
import functools

import jax
import jax.numpy as jnp
from jax import lax
from jax.experimental import pallas as pl
from jax.experimental.pallas import tpu as pltpu
from jax.sharding import PartitionSpec as P

time_step = 0.035
slope_floor = 0.01
gauge_weight = 100.0
REACH = 6
LANES = 128
LN2 = 0.6931471805599453
SUB = 8


def pairs(count, first):
    out = []
    for i in range(first, count - 1, 2):
        out += [(i, i + 1), (i + 1, i)]
    return out


def exchange(x, axis, first):
    perm = pairs(lax.axis_size(axis), first)
    return lax.ppermute(x, axis, perm) if perm else None


def lanes_of(shape):
    return lax.broadcasted_iota(jnp.int32, shape, 1)


def plan(events, steps):
    out, slot = [], 0
    for n in [REACH - t for _ in range(events) for t in range(steps)] + [REACH] * (events + 3) + [1] * events:
        out.append((n, slot))
        slot += n
    return out, -(-slot // SUB)


def one_hot(hit):
    return jnp.where(hit, 1.0, 0.0).astype(jnp.bfloat16)


def tally_of(row, col, rows, cols):
    gauges = row.shape[-1]
    tall = rows * (cols // 256)
    inside = (row >= 0) & (row < rows)
    high = jnp.where(inside, (col // 256) * rows + row, -1)
    hits = lax.dot_general(
        one_hot(lax.broadcasted_iota(jnp.int32, (tall, gauges), 0) == high),
        one_hot(lax.broadcasted_iota(jnp.int32, (256, gauges), 0) == col % 256),
        (((1,), (1,)), ((), ())),
        preferred_element_type=jnp.float32,
    )
    return [hits[b * rows : (b + 1) * rows] for b in range(cols // 256)]


def rows_kernel(sides, *refs):
    ins, pays, rest = refs[1:6], refs[6 : 6 + sides], refs[6 + sides :]
    cells, sems = rest[-2:]
    events, steps, rows, cols = ins[0].shape
    even = lax.axis_index("row") % 2 == 0
    slots, count = plan(events, steps)
    sub = lax.broadcasted_iota(jnp.int32, (SUB, cols), 0)
    copies = [pltpu.make_async_copy(refs[0], cells, sems.at[0, 5])]
    copies[0].start()
    for k in range(sides):
        sends_last = even if k == 0 else jnp.logical_not(even)
        edge = pl.multiple_of(jnp.where(sends_last, rows - SUB, 0), SUB)
        for i, x in enumerate(ins):
            lead = (slice(None),) * (len(x.shape) - 2)
            copy = pltpu.make_async_copy(
                x.at[(*lead, pl.ds(edge, SUB), slice(None))], rest[5 * k + i], sems.at[k, i]
            )
            copy.start()
            copies.append(copy)
    for copy in copies:
        copy.wait()
    for k, pay in enumerate(pays):
        d, w, b, r, v = rest[5 * k : 5 * k + 5]
        sends_last = even if k == 0 else jnp.logical_not(even)
        fields = [d[e, t] for e in range(events) for t in range(steps)]
        fields += [w[e].astype(jnp.float32) for e in range(events)] + [b[...], r[...], v[...]]
        fields += [jnp.broadcast_to(cells[e].astype(jnp.float32), (SUB, cols)) for e in range(events)]
        tiles = [jnp.zeros((SUB, cols), jnp.float32)] * count
        for x, (n, slot) in zip(fields, slots):
            if 1 < n < SUB:
                x = jnp.where(sends_last, pltpu.roll(x, n, 0), x)
            for i in range(slot // SUB, (slot + n - 1) // SUB + 1):
                low, high = slot - i * SUB, slot + n - i * SUB
                y = pltpu.roll(x, low % SUB, 0) if low % SUB else x
                tiles[i] = jnp.where((sub >= low) & (sub < high), y, tiles[i])
        for i in range(count):
            pay[i * SUB : (i + 1) * SUB] = tiles[i]


def edge_rows(cells, depth, wet, bed, rough, direction):
    events, steps, _, cols = depth.shape
    sides = 2 if lax.axis_size("row") > 2 else 1
    _, count = plan(events, steps)
    vmem, anywhere = pl.BlockSpec(memory_space=pltpu.VMEM), pl.BlockSpec(memory_space=pl.ANY)
    ins = (depth, wet, bed, rough, direction)
    return pl.pallas_call(
        functools.partial(rows_kernel, sides),
        in_specs=[anywhere] * 6,
        out_specs=[vmem] * sides,
        out_shape=[jax.ShapeDtypeStruct((count * SUB, cols), jnp.float32)] * sides,
        scratch_shapes=[pltpu.VMEM((*x.shape[:-2], SUB, cols), x.dtype) for x in ins] * sides
        + [pltpu.VMEM(cells.shape, cells.dtype), pltpu.SemaphoreType.DMA((sides, 6))],
        compiler_params=pltpu.CompilerParams(vmem_limit_bytes=58 * 1024 * 1024),
        name="edge_rows",
    )(cells, *ins)


def gauge_kernel(cells, cnt):
    events, rows, cols = cnt.shape
    for e in range(events):
        g = cells[e]
        for b, x in enumerate(tally_of(g // cols, g % cols, rows, cols)):
            cnt[e, :, b * 256 : (b + 1) * 256] = x


def gauges(cells, rows, cols):
    vmem = pl.BlockSpec(memory_space=pltpu.VMEM)
    return pl.pallas_call(
        gauge_kernel,
        in_specs=[vmem],
        out_specs=vmem,
        out_shape=jax.ShapeDtypeStruct((cells.shape[0], rows, cols), jnp.float32),
        compiler_params=pltpu.CompilerParams(vmem_limit_bytes=12 * 1024 * 1024),
        cost_estimate=pl.CostEstimate(flops=20000000, bytes_accessed=4000000, transcendentals=0),
        name="gauges",
    )(cells)


def column_kernel(sides, *refs):
    rims_in, own = refs[:sides], (refs[sides : sides + 6], refs[sides + 6 : sides + 12])
    rim_top, rim_bottom, pay_a, pay_b = refs[sides + 12 :]
    events, steps, rows, _ = own[0][0].shape
    cols = rim_top.shape[-1]
    even_row = lax.axis_index("row") % 2 == 0
    even_col = lax.axis_index("col") % 2 == 0
    sub = lax.broadcasted_iota(jnp.int32, (SUB, cols), 0)
    slots, _ = plan(events, steps)
    base = events * (steps + 1) + 3
    nothing = jnp.zeros((SUB, cols), jnp.float32)

    def field(ref, n, slot):
        x = nothing
        for i in range(slot // SUB, (slot + n - 1) // SUB + 1):
            low, high = slot - i * SUB, slot + n - i * SUB
            y = ref[i * SUB : (i + 1) * SUB]
            y = pltpu.roll(y, -low % SUB, 0) if low % SUB else y
            x = jnp.where((sub >= -low) & (sub < min(n, SUB - low)) & (sub >= max(0, -low)), y, x)
        return x

    for f in range(base):
        n, slot = slots[f]
        x = field(rims_in[0], n, slot)
        y = field(rims_in[1], n, slot) if sides > 1 else nothing
        rim_bottom[f] = jnp.where(even_row, x, y)
        rim_top[f] = pltpu.roll(jnp.where(even_row, y, x), SUB - n, 0)
    for e in range(events):
        slot = slots[base + e][1]
        for k in range(2):
            lower = even_row if k == 0 else jnp.logical_not(even_row)
            if k < sides:
                g = rims_in[k][slot : slot + 1].astype(jnp.int32)
                row = g // cols - jnp.where(lower, 0, rows - SUB)
                hits = jnp.concatenate(tally_of(row, g % cols, SUB, cols), axis=1)
            else:
                hits = nothing
            if k == 0:
                first = hits
        rim_bottom[base + e] = jnp.where(even_row, first, hits)
        rim_top[base + e] = jnp.where(even_row, hits, first)

    lane = lanes_of((rows + 2 * SUB, LANES))
    packs = []
    for side in range(2):
        d, w, b, r, v, c = own[side]
        place_of = slice(0, LANES) if side == 0 else slice(cols - LANES, cols)
        pack = jnp.zeros((rows + 2 * SUB, LANES), jnp.float32)
        xs = [d[e, t] for e in range(events) for t in range(steps)]
        xs += [w[e].astype(jnp.float32) for e in range(events)]
        xs += [b[...], r[...], v[...]]
        xs += [c[e] for e in range(events)]
        for f, x in enumerate(xs):
            x = jnp.concatenate([rim_top[f, :, place_of], x, rim_bottom[f, :, place_of]], axis=0)
            place = f * REACH
            shift = (place + REACH if side == 1 else place) % LANES
            if shift:
                x = pltpu.roll(x, shift, 1)
            pack = jnp.where((lane >= place) & (lane < place + REACH), x, pack)
        packs.append(pack)
    pay_a[...] = jnp.where(even_col, packs[1], packs[0])
    pay_b[...] = jnp.where(even_col, packs[0], packs[1])


def rims_and_columns(rims, depth, wet, bed, rough, direction, counts):
    events, steps, rows, cols = depth.shape
    last = cols // LANES - 1

    def side(j):
        return [
            pl.BlockSpec((events, steps, rows, LANES), lambda i: (0, 0, 0, j)),
            pl.BlockSpec((events, rows, LANES), lambda i: (0, 0, j)),
            pl.BlockSpec((rows, LANES), lambda i: (0, j)),
            pl.BlockSpec((rows, LANES), lambda i: (0, j)),
            pl.BlockSpec((rows, LANES), lambda i: (0, j)),
            pl.BlockSpec((events, rows, LANES), lambda i: (0, 0, j)),
        ]

    whole = lambda shape: pl.BlockSpec(shape, lambda i: (0,) * len(shape))
    tall = (rows + 2 * SUB, LANES)
    rim = (events * (steps + 2) + 3, SUB, cols)
    own = (depth, wet, bed, rough, direction, counts)
    return pl.pallas_call(
        functools.partial(column_kernel, len(rims)),
        grid=(1,),
        in_specs=[whole(r.shape) for r in rims] + side(0) + side(last),
        out_specs=[whole(rim)] * 2 + [whole(tall)] * 2,
        out_shape=[jax.ShapeDtypeStruct(rim, jnp.float32)] * 2 + [jax.ShapeDtypeStruct(tall, jnp.float32)] * 2,
        compiler_params=pltpu.CompilerParams(vmem_limit_bytes=12 * 1024 * 1024),
        name="rims_and_columns",
    )(*rims, *own, *own)


def up(x):
    return pltpu.roll(x, SUB - 1, 0)


def down(x):
    return pltpu.roll(x, 1, 0)


def right(xs):
    last = lanes_of((SUB, LANES)) == LANES - 1
    r = [pltpu.roll(x, LANES - 1, 1) for x in xs]
    return [jnp.where(last, r[(j + 1) % len(xs)], r[j]) for j in range(len(xs))]


def left(xs):
    first = lanes_of((SUB, LANES)) == 0
    r = [pltpu.roll(x, 1, 1) for x in xs]
    return [jnp.where(first, r[j - 1], r[j]) for j in range(len(xs))]


def at_lanes(j):
    return slice(j * LANES, (j + 1) * LANES)


def get(ref, *at):
    return [ref[(*at, slice(None), at_lanes(j))] for j in range(ref.shape[-1] // LANES)]


def put(xs, ref, *at):
    for j, x in enumerate(xs):
        ref[(*at, slice(None), at_lanes(j))] = x


def wrap(ref, *at):
    deep = ref.shape[-3] - 1
    put([up(x) for x in get(ref, *at, 0)], ref, *at, deep)


def tangent_kernel(
    depth, wet, bed, rough, direction, counts, rim_top, rim_bottom, side_a, side_b,
    curve_ref, m_c, source, a_x, b_x, c_x, a_y, b_y, c_y,
    nat, hx, sb_x, sb_y, q_x, q_y, inv_x, inv_y, cond_x, cond_y, cnt,
    tan_a, tan_b, flow, tmp,
):
    events, steps, rows, cols = depth.shape
    tall = rows + 2 * SUB
    deep = tall // SUB
    tiles = cols // LANES
    count = tiles + 1
    even_col = lax.axis_index("col") % 2 == 0
    lane_t = lanes_of((tall, LANES))
    sub = lax.broadcasted_iota(jnp.int32, (SUB, LANES), 0)
    right_rim = jnp.where(even_col, side_a[...], side_b[...])
    left_rim = jnp.where(even_col, side_b[...], side_a[...])
    J = [slice(j * LANES, (j + 1) * LANES) for j in range(count)]
    zero = jnp.zeros((SUB, LANES), jnp.float32)

    def assemble(f, own, k):
        for j in range(tiles):
            nat[k, j, 0:SUB, :] = rim_top[f, :, J[j]]
            nat[k, j, SUB : SUB + rows, :] = own[:, J[j]]
            nat[k, j, SUB + rows : tall, :] = rim_bottom[f, :, J[j]]
        place = f * REACH
        r = pltpu.roll(right_rim, (LANES - place) % LANES, 1) if place else right_rim
        l = pltpu.roll(left_rim, (LANES - REACH - place) % LANES, 1)
        extra = jnp.where(lane_t < REACH, r, jnp.where(lane_t >= LANES - REACH, l, 0.0))
        nat[k, tiles] = extra

    def spread(k, i):
        return [nat[k, j, pl.ds(i, SUB, stride=deep), :] for j in range(count)]

    base = events * (steps + 1)
    for k, (f, x) in enumerate(((base, bed), (base + 1, rough), (base + 2, direction))):
        assemble(f, x[...], k)
    for e in range(events):
        assemble(events * steps + e, wet[e].astype(jnp.float32), 3 + e)
        assemble(base + 3 + e, counts[e], 3 + events + e)
        for t in range(steps):
            assemble(e * steps + t, depth[e, t], 3 + 2 * events + e * steps + t)

    @pl.loop(0, deep, unroll=5)
    def _(i):
        m = [jnp.exp(x) for x in spread(1, i)]
        put(spread(0, i), tmp, 0, i)
        put(m, tmp, 1, i)
        put(m, m_c, i)
        put([x * y for x, y in zip(m, spread(2, i))], tmp, 2, i)
        for e in range(events):
            put(spread(3 + e, i), tmp, 3 + e, i)
            put(spread(3 + events + e, i), cnt, e, i)
            for t in range(steps):
                put(spread(3 + 2 * events + e * steps + t, i), hx, e, t, i)

    for k in range(3 + events):
        wrap(tmp, k)
    for e in range(events):
        for t in range(steps):
            wrap(hx, e, t)

    scale = time_step * 2.0 ** (-2.0 / 3.0)

    @pl.loop(0, deep, unroll=5)
    def _(i):
        b, m, q = (get(tmp, k, i) for k in range(3))
        put([y - x for x, y in zip(b, right(b))], sb_x, i)
        put([y - x for x, y in zip(b, get(tmp, 0, i + 1))], sb_y, i)
        ix = [1.0 / (x + y) for x, y in zip(m, right(m))]
        iy = [1.0 / (x + y) for x, y in zip(m, get(tmp, 1, i + 1))]
        put([-x for x in ix], inv_x, i)
        put([-x for x in iy], inv_y, i)
        put([x + y for x, y in zip(q, right(q))], q_x, i)
        put([x + y for x, y in zip(q, get(tmp, 2, i + 1))], q_y, i)
        for e in range(events):
            w = get(tmp, 3 + e, i)
            put([(scale * z) * (x * y) for x, y, z in zip(w, right(w), ix)], cond_x, e, i)
            put([(scale * z) * (x * y) for x, y, z in zip(w, get(tmp, 3 + e, i + 1), iy)], cond_y, e, i)

    def face(h, h_k, sb, cond, inv):
        hs = h + h_k
        s = (h_k - h) + sb
        x = s * s + slope_floor
        y = lax.rsqrt(x)
        p = cond * (jnp.exp2((2.0 / 3.0 / LN2) * jnp.log(hs)) * (y * lax.rsqrt(y)))
        ps = p * s
        t = p * hs
        A = (5.0 / 3.0) * ps
        B = t * (0.5 + (0.5 * slope_floor) * (y * y))
        return A - B, A + B, (ps * hs) * inv

    curve_ref[...] = jnp.zeros(curve_ref.shape, jnp.float32)
    put([zero] * count, flow, 0)

    @pl.loop(0, events)
    def _(e):
        for t in range(steps):
            old, new = (tan_a, tan_b) if t % 2 else (tan_b, tan_a)

            @pl.loop(0, deep, unroll=5)
            def _(i):
                h = get(hx, e, t, i)
                h_r, h_d = right(h), get(hx, e, t, i + 1)
                if t:
                    d = get(old, i)
                    d_r, d_d = right(d), get(old, i + 1)
                fx, fy = [], []
                for j in range(count):
                    A, B, C = face(h[j], h_r[j], sb_x[i, :, J[j]], cond_x[e, i, :, J[j]], inv_x[i, :, J[j]])
                    f = C * q_x[i, :, J[j]]
                    c_x[e, t, i, :, J[j]] = C
                    if t:
                        a_x[e, t - 1, i, :, J[j]] = A
                        b_x[e, t - 1, i, :, J[j]] = B
                        f += A * d[j] + B * d_r[j]
                    fx.append(f)
                    A, B, C = face(h[j], h_d[j], sb_y[i, :, J[j]], cond_y[e, i, :, J[j]], inv_y[i, :, J[j]])
                    f = C * q_y[i, :, J[j]]
                    c_y[e, t, i, :, J[j]] = C
                    if t:
                        a_y[e, t - 1, i, :, J[j]] = A
                        b_y[e, t - 1, i, :, J[j]] = B
                        f += A * d[j] + B * d_d[j]
                    fy.append(f)
                put(fy, flow, i + 1)
                before = get(flow, i)
                fl = left(fx)
                for j in range(count):
                    r = (fx[j] - fl[j]) + (fy[j] - before[j])
                    new[i, :, J[j]] = d[j] + r if t else r

            for j in range(count):
                new[0, :, J[j]] = new[0, :, J[j]] - down(flow[deep, :, J[j]])
            wrap(new)

        old = tan_a if steps % 2 else tan_b

        @pl.loop(0, deep, unroll=5)
        def _(i):
            row = sub * deep + i
            own = (row >= SUB) & (row < SUB + rows)
            total = zero
            for j in range(count):
                r = old[i, :, J[j]]
                s = (gauge_weight * cnt[e, i, :, J[j]]) * r
                source[e, i, :, J[j]] = s
                if j < tiles:
                    total += s * r
            curve_ref[...] += jnp.where(own, total, 0.0)

        wrap(source, e)


def adjoint_kernel(first_event, last_event, m_c, source, a_x, b_x, c_x, a_y, b_y, c_y, *refs):
    sums = () if first_event else refs[:2]
    outs = refs[len(sums) : len(sums) + (1 if last_event else 2)]
    nat, adj_a, adj_b, flow, *own = refs[len(sums) + len(outs) :]
    g_x, g_y = own if last_event else outs
    steps, deep, _, wide = c_x.shape
    count = wide // LANES
    J = [at_lanes(j) for j in range(count)]
    zero = jnp.zeros((SUB, LANES), jnp.float32)
    put([zero] * count, flow, 0)

    for t in range(steps - 1, -1, -1):
        old, new = (adj_a, adj_b) if t % 2 else (adj_b, adj_a)
        if t == steps - 1:
            old = source
            base_x, base_y = sums if sums else (None, None)
        else:
            base_x, base_y = g_x, g_y

        @pl.loop(0, deep, unroll=5)
        def _(i):
            l = get(old, i)
            l_r, l_d = right(l), get(old, i + 1)
            acc, kx, ky = [], [], []
            for j in range(count):
                p = l[j] - l_r[j]
                g = c_x[t, i, :, J[j]] * p
                g_x[i, :, J[j]] = g + base_x[i, :, J[j]] if base_x is not None else g
                if t:
                    a = l[j] + a_x[t - 1, i, :, J[j]] * p
                    kx.append(b_x[t - 1, i, :, J[j]] * p)
                p = l[j] - l_d[j]
                g = c_y[t, i, :, J[j]] * p
                g_y[i, :, J[j]] = g + base_y[i, :, J[j]] if base_y is not None else g
                if t:
                    acc.append(a + a_y[t - 1, i, :, J[j]] * p)
                    ky.append(b_y[t - 1, i, :, J[j]] * p)
            if t:
                put(ky, flow, i + 1)
                before = get(flow, i)
                kl = left(kx)
                for j in range(count):
                    new[i, :, J[j]] = acc[j] + (kl[j] + before[j])

        if t:
            for j in range(count):
                new[0, :, J[j]] = new[0, :, J[j]] + down(flow[deep, :, J[j]])
            wrap(new)

    if last_event:
        (grad_ref,) = outs
        rows, cols = grad_ref.shape
        tiles = cols // LANES
        put([down(x) for x in get(g_y, deep - 1)], flow, 0)

        @pl.loop(0, deep, unroll=5)
        def _(i):
            x, y = get(g_x, i), get(g_y, i)
            put(y, flow, i + 1)
            xl, yl = left(x), get(flow, i)
            for j in range(tiles):
                g = m_c[i, :, J[j]] * ((x[j] + xl[j]) + (y[j] + yl[j]))
                nat[j, pl.ds(i, SUB, stride=deep), :] = g

        for j in range(tiles):
            grad_ref[:, J[j]] = nat[j, SUB : SUB + rows, :]


def tangents(depth, wet, bed, rough, direction, counts, rim_top, rim_bottom, side_a, side_b):
    events, steps, rows, cols = depth.shape
    tall, wide = rows + 2 * SUB, cols + LANES
    deep = tall // SUB
    shape = lambda *lead: (*lead, deep, SUB, wide)
    vm = lambda *lead: pltpu.VMEM(shape(*lead), jnp.float32)
    more = lambda *lead: pltpu.VMEM((*lead, deep + 1, SUB, wide), jnp.float32)
    out = lambda *lead: jax.ShapeDtypeStruct(shape(*lead), jnp.float32)
    vmem = pl.BlockSpec(memory_space=pltpu.VMEM)
    fields = 3 + events * (steps + 2)
    return pl.pallas_call(
        tangent_kernel,
        in_specs=[vmem] * 10,
        out_specs=[vmem] * 9,
        out_shape=[
            jax.ShapeDtypeStruct((SUB, LANES), jnp.float32),
            out(),
            jax.ShapeDtypeStruct((events, deep + 1, SUB, wide), jnp.float32),
            *[out(events, steps - 1), out(events, steps - 1), out(events, steps)] * 2,
        ],
        scratch_shapes=[
            pltpu.VMEM((fields, wide // LANES, tall, LANES), jnp.float32),
            more(events, steps),
            *[vm()] * 6,
            *[vm(events)] * 3,
            *[more()] * 3,
            more(3 + events),
        ],
        compiler_params=pltpu.CompilerParams(vmem_limit_bytes=20 * 1024 * 1024),
        name="tangents",
    )(depth, wet, bed, rough, direction, counts, rim_top, rim_bottom, side_a, side_b)


def gradient(e, rows, cols, sums, m_c, source, *coefficients):
    events, _, _, wide = source.shape
    deep = m_c.shape[0]
    first, last = e == 0, e == events - 1
    vm = (deep, SUB, wide)
    more = pltpu.VMEM((deep + 1, SUB, wide), jnp.float32)
    vmem = pl.BlockSpec(memory_space=pltpu.VMEM)
    own = lambda x: pl.BlockSpec((None, *x.shape[1:]), lambda i: (e,) + (0,) * (x.ndim - 1))
    whole = lambda shape: pl.BlockSpec(shape, lambda i: (0,) * len(shape))
    return pl.pallas_call(
        functools.partial(adjoint_kernel, first, last),
        grid=(1,),
        in_specs=[whole(m_c.shape), own(source)] + [own(x) for x in coefficients] + [whole(vm)] * len(sums),
        out_specs=whole((rows, cols)) if last else [whole(vm)] * 2,
        out_shape=jax.ShapeDtypeStruct((rows, cols), jnp.float32)
        if last
        else [jax.ShapeDtypeStruct(vm, jnp.float32)] * 2,
        scratch_shapes=[pltpu.VMEM((cols // LANES, deep * SUB, LANES), jnp.float32), more, more, more]
        + [pltpu.VMEM(vm, jnp.float32)] * (2 if last else 0),
        compiler_params=pltpu.CompilerParams(vmem_limit_bytes=16 * 1024 * 1024),
        cost_estimate=pl.CostEstimate(flops=40000000, bytes_accessed=12000000, transcendentals=0),
        name="gradient",
    )(m_c, source, *coefficients, *sums)


def hops_over(axis):
    count, hop, out = lax.axis_size(axis), 1, []
    while hop < count:
        out.append((axis, hop))
        hop *= 2
    return out


def hop_sum(x, axis, hop):
    return x + lax.ppermute(x, axis, [(i, i ^ hop) for i in range(lax.axis_size(axis))])


def local(depth, wet, bed, rough, direction, gauge_cells):
    events, steps, rows, cols = depth.shape
    cells = gauge_cells.reshape(events, 1, -1)
    pays = edge_rows(cells, depth, wet, bed, rough, direction)
    rims = [exchange(x, "row", k) for k, x in enumerate(pays)]
    counts = gauges(cells, rows, cols)
    rim_top, rim_bottom, send_a, send_b = rims_and_columns(
        rims, depth, wet, bed, rough, direction, counts
    )
    side_b = exchange(send_b, "col", 1)
    side_a = exchange(send_a, "col", 0)
    curve, *coefficients = tangents(
        depth, wet, bed, rough, direction, counts, rim_top, rim_bottom, side_a, side_b
    )
    hops = hops_over("event") + hops_over("row") + hops_over("col")
    sums = ()
    for e in range(events):
        sums = gradient(e, rows, cols, sums, *coefficients)
        if hops:
            curve = hop_sum(curve, *hops.pop(0))
            sums, curve = lax.optimization_barrier((sums, curve))
    grad = sums
    for axis, hop in hops_over("event"):
        grad = hop_sum(grad, axis, hop)
    for axis, hop in hops:
        curve = hop_sum(curve, axis, hop)
    return (grad, jnp.sum(curve))


def solution(mesh):
    placed = (
        P("event", None, "row", "col"),
        P("event", "row", "col"),
        P("row", "col"),
        P("row", "col"),
        P("row", "col"),
        P("event", "row", "col", None),
    )
    return jax.shard_map(
        local, mesh=mesh, in_specs=placed, out_specs=(P("row", "col"), P()), check_vma=False
    )
```

```python
import functools

import jax
import jax.numpy as jnp
from jax import lax
from jax.experimental import pallas as pl
from jax.experimental.pallas import tpu as pltpu
from jax.sharding import PartitionSpec as P

time_step = 0.035
slope_floor = 0.01
gauge_weight = 100.0
REACH = 6
LANES = 128
LN2 = 0.6931471805599453
SUB = 8


def pairs(count, first):
    out = []
    for i in range(first, count - 1, 2):
        out += [(i, i + 1), (i + 1, i)]
    return out


def exchange(x, axis, first):
    perm = pairs(lax.axis_size(axis), first)
    return lax.ppermute(x, axis, perm) if perm else None


def lanes_of(shape):
    return lax.broadcasted_iota(jnp.int32, shape, 1)


def plan(events, steps):
    out, slot = [], 0
    for n in [REACH - t for _ in range(events) for t in range(steps)] + [REACH] * (events + 3) + [1] * events:
        out.append((n, slot))
        slot += n
    return out, -(-slot // SUB)


def one_hot(hit):
    return jnp.where(hit, 1.0, 0.0).astype(jnp.bfloat16)


def tally_of(row, col, rows, cols):
    gauges = row.shape[-1]
    tall = rows * (cols // 256)
    inside = (row >= 0) & (row < rows)
    high = jnp.where(inside, (col // 256) * rows + row, -1)
    hits = lax.dot_general(
        one_hot(lax.broadcasted_iota(jnp.int32, (tall, gauges), 0) == high),
        one_hot(lax.broadcasted_iota(jnp.int32, (256, gauges), 0) == col % 256),
        (((1,), (1,)), ((), ())),
        preferred_element_type=jnp.float32,
    )
    return [hits[b * rows : (b + 1) * rows] for b in range(cols // 256)]


def rows_kernel(sides, *refs):
    ins, pays, rest = refs[1:6], refs[6 : 6 + sides], refs[6 + sides :]
    cells, sems = rest[-2:]
    events, steps, rows, cols = ins[0].shape
    even = lax.axis_index("row") % 2 == 0
    slots, count = plan(events, steps)
    sub = lax.broadcasted_iota(jnp.int32, (SUB, cols), 0)
    copies = [pltpu.make_async_copy(refs[0], cells, sems.at[0, 5])]
    copies[0].start()
    for k in range(sides):
        sends_last = even if k == 0 else jnp.logical_not(even)
        edge = pl.multiple_of(jnp.where(sends_last, rows - SUB, 0), SUB)
        for i, x in enumerate(ins):
            lead = (slice(None),) * (len(x.shape) - 2)
            copy = pltpu.make_async_copy(
                x.at[(*lead, pl.ds(edge, SUB), slice(None))], rest[5 * k + i], sems.at[k, i]
            )
            copy.start()
            copies.append(copy)
    for copy in copies:
        copy.wait()
    for k, pay in enumerate(pays):
        d, w, b, r, v = rest[5 * k : 5 * k + 5]
        sends_last = even if k == 0 else jnp.logical_not(even)
        fields = [d[e, t] for e in range(events) for t in range(steps)]
        fields += [w[e].astype(jnp.float32) for e in range(events)] + [b[...], r[...], v[...]]
        fields += [jnp.broadcast_to(cells[e].astype(jnp.float32), (SUB, cols)) for e in range(events)]
        tiles = [jnp.zeros((SUB, cols), jnp.float32)] * count
        for x, (n, slot) in zip(fields, slots):
            if 1 < n < SUB:
                x = jnp.where(sends_last, pltpu.roll(x, n, 0), x)
            for i in range(slot // SUB, (slot + n - 1) // SUB + 1):
                low, high = slot - i * SUB, slot + n - i * SUB
                y = pltpu.roll(x, low % SUB, 0) if low % SUB else x
                tiles[i] = jnp.where((sub >= low) & (sub < high), y, tiles[i])
        for i in range(count):
            pay[i * SUB : (i + 1) * SUB] = tiles[i]


def edge_rows(cells, depth, wet, bed, rough, direction):
    events, steps, _, cols = depth.shape
    sides = 2 if lax.axis_size("row") > 2 else 1
    _, count = plan(events, steps)
    vmem, anywhere = pl.BlockSpec(memory_space=pltpu.VMEM), pl.BlockSpec(memory_space=pl.ANY)
    ins = (depth, wet, bed, rough, direction)
    return pl.pallas_call(
        functools.partial(rows_kernel, sides),
        in_specs=[anywhere] * 6,
        out_specs=[vmem] * sides,
        out_shape=[jax.ShapeDtypeStruct((count * SUB, cols), jnp.float32)] * sides,
        scratch_shapes=[pltpu.VMEM((*x.shape[:-2], SUB, cols), x.dtype) for x in ins] * sides
        + [pltpu.VMEM(cells.shape, cells.dtype), pltpu.SemaphoreType.DMA((sides, 6))],
        compiler_params=pltpu.CompilerParams(vmem_limit_bytes=58 * 1024 * 1024),
        name="edge_rows",
    )(cells, *ins)


def gauge_kernel(cells, cnt):
    events, rows, cols = cnt.shape
    for e in range(events):
        g = cells[e]
        for b, x in enumerate(tally_of(g // cols, g % cols, rows, cols)):
            cnt[e, :, b * 256 : (b + 1) * 256] = x


def gauges(cells, rows, cols):
    vmem = pl.BlockSpec(memory_space=pltpu.VMEM)
    return pl.pallas_call(
        gauge_kernel,
        in_specs=[vmem],
        out_specs=vmem,
        out_shape=jax.ShapeDtypeStruct((cells.shape[0], rows, cols), jnp.float32),
        compiler_params=pltpu.CompilerParams(vmem_limit_bytes=12 * 1024 * 1024),
        cost_estimate=pl.CostEstimate(flops=20000000, bytes_accessed=4000000, transcendentals=0),
        name="gauges",
    )(cells)


def column_kernel(sides, *refs):
    rims_in, own = refs[:sides], (refs[sides : sides + 6], refs[sides + 6 : sides + 12])
    rim_top, rim_bottom, pay_b, pay_a = refs[sides + 12 :]
    events, steps, rows, _ = own[0][0].shape
    cols = rim_top.shape[-1]
    even_row = lax.axis_index("row") % 2 == 0
    even_col = lax.axis_index("col") % 2 == 0
    sub = lax.broadcasted_iota(jnp.int32, (SUB, cols), 0)
    slots, _ = plan(events, steps)
    base = events * (steps + 1) + 3
    nothing = jnp.zeros((SUB, cols), jnp.float32)

    def field(ref, n, slot):
        x = nothing
        for i in range(slot // SUB, (slot + n - 1) // SUB + 1):
            low, high = slot - i * SUB, slot + n - i * SUB
            y = ref[i * SUB : (i + 1) * SUB]
            y = pltpu.roll(y, -low % SUB, 0) if low % SUB else y
            x = jnp.where((sub >= -low) & (sub < min(n, SUB - low)) & (sub >= max(0, -low)), y, x)
        return x

    for f in range(base):
        n, slot = slots[f]
        x = field(rims_in[0], n, slot)
        y = field(rims_in[1], n, slot) if sides > 1 else nothing
        rim_bottom[f] = jnp.where(even_row, x, y)
        rim_top[f] = pltpu.roll(jnp.where(even_row, y, x), SUB - n, 0)
    for e in range(events):
        slot = slots[base + e][1]
        for k in range(2):
            lower = even_row if k == 0 else jnp.logical_not(even_row)
            if k < sides:
                g = rims_in[k][slot : slot + 1].astype(jnp.int32)
                row = g // cols - jnp.where(lower, 0, rows - SUB)
                hits = jnp.concatenate(tally_of(row, g % cols, SUB, cols), axis=1)
            else:
                hits = nothing
            if k == 0:
                first = hits
        rim_bottom[base + e] = jnp.where(even_row, first, hits)
        rim_top[base + e] = jnp.where(even_row, hits, first)

    lane = lanes_of((rows + 2 * SUB, LANES))
    packs = []
    for side in range(2):
        d, w, b, r, v, c = own[side]
        place_of = slice(0, LANES) if side == 0 else slice(cols - LANES, cols)
        pack = jnp.zeros((rows + 2 * SUB, LANES), jnp.float32)
        xs = [d[e, t] for e in range(events) for t in range(steps)]
        xs += [w[e].astype(jnp.float32) for e in range(events)]
        xs += [b[...], r[...], v[...]]
        xs += [c[e] for e in range(events)]
        for f, x in enumerate(xs):
            x = jnp.concatenate([rim_top[f, :, place_of], x, rim_bottom[f, :, place_of]], axis=0)
            place = f * REACH
            shift = (place + REACH if side == 1 else place) % LANES
            if shift:
                x = pltpu.roll(x, shift, 1)
            pack = jnp.where((lane >= place) & (lane < place + REACH), x, pack)
        packs.append(pack)
    pay_a[...] = jnp.where(even_col, packs[1], packs[0])
    pay_b[...] = jnp.where(even_col, packs[0], packs[1])


def rims_and_columns(rims, depth, wet, bed, rough, direction, counts):
    events, steps, rows, cols = depth.shape
    last = cols // LANES - 1

    def side(j):
        return [
            pl.BlockSpec((events, steps, rows, LANES), lambda i: (0, 0, 0, j)),
            pl.BlockSpec((events, rows, LANES), lambda i: (0, 0, j)),
            pl.BlockSpec((rows, LANES), lambda i: (0, j)),
            pl.BlockSpec((rows, LANES), lambda i: (0, j)),
            pl.BlockSpec((rows, LANES), lambda i: (0, j)),
            pl.BlockSpec((events, rows, LANES), lambda i: (0, 0, j)),
        ]

    whole = lambda shape: pl.BlockSpec(shape, lambda i: (0,) * len(shape))
    tall = (rows + 2 * SUB, LANES)
    rim = (events * (steps + 2) + 3, SUB, cols)
    own = (depth, wet, bed, rough, direction, counts)
    return pl.pallas_call(
        functools.partial(column_kernel, len(rims)),
        grid=(1,),
        in_specs=[whole(r.shape) for r in rims] + side(0) + side(last),
        out_specs=[whole(rim)] * 2 + [whole(tall)] * 2,
        out_shape=[jax.ShapeDtypeStruct(rim, jnp.float32)] * 2 + [jax.ShapeDtypeStruct(tall, jnp.float32)] * 2,
        compiler_params=pltpu.CompilerParams(vmem_limit_bytes=12 * 1024 * 1024),
        name="rims_and_columns",
    )(*rims, *own, *own)


def up(x):
    return pltpu.roll(x, SUB - 1, 0)


def down(x):
    return pltpu.roll(x, 1, 0)


def right(xs):
    last = lanes_of((SUB, LANES)) == LANES - 1
    r = [pltpu.roll(x, LANES - 1, 1) for x in xs]
    return [jnp.where(last, r[(j + 1) % len(xs)], r[j]) for j in range(len(xs))]


def left(xs):
    first = lanes_of((SUB, LANES)) == 0
    r = [pltpu.roll(x, 1, 1) for x in xs]
    return [jnp.where(first, r[j - 1], r[j]) for j in range(len(xs))]


def at_lanes(j):
    return slice(j * LANES, (j + 1) * LANES)


def get(ref, *at):
    return [ref[(*at, slice(None), at_lanes(j))] for j in range(ref.shape[-1] // LANES)]


def put(xs, ref, *at):
    for j, x in enumerate(xs):
        ref[(*at, slice(None), at_lanes(j))] = x


def wrap(ref, *at):
    deep = ref.shape[-3] - 1
    put([up(x) for x in get(ref, *at, 0)], ref, *at, deep)


def tangent_kernel(
    depth, wet, bed, rough, direction, counts, rim_top, rim_bottom, side_b, side_a,
    curve_ref, m_c, source, a_x, b_x, c_x, a_y, b_y, c_y,
    nat, hx, sb_x, sb_y, q_x, q_y, inv_x, inv_y, cond_x, cond_y, cnt,
    tan_a, tan_b, flow, tmp,
):
    events, steps, rows, cols = depth.shape
    tall = rows + 2 * SUB
    deep = tall // SUB
    tiles = cols // LANES
    count = tiles + 1
    even_col = lax.axis_index("col") % 2 == 0
    lane_t = lanes_of((tall, LANES))
    sub = lax.broadcasted_iota(jnp.int32, (SUB, LANES), 0)
    right_rim = jnp.where(even_col, side_a[...], side_b[...])
    left_rim = jnp.where(even_col, side_b[...], side_a[...])
    J = [slice(j * LANES, (j + 1) * LANES) for j in range(count)]
    zero = jnp.zeros((SUB, LANES), jnp.float32)

    def assemble(f, own, k):
        for j in range(tiles):
            nat[k, j, 0:SUB, :] = rim_top[f, :, J[j]]
            nat[k, j, SUB : SUB + rows, :] = own[:, J[j]]
            nat[k, j, SUB + rows : tall, :] = rim_bottom[f, :, J[j]]
        place = f * REACH
        r = pltpu.roll(right_rim, (LANES - place) % LANES, 1) if place else right_rim
        l = pltpu.roll(left_rim, (LANES - REACH - place) % LANES, 1)
        extra = jnp.where(lane_t < REACH, r, jnp.where(lane_t >= LANES - REACH, l, 0.0))
        nat[k, tiles] = extra

    def spread(k, i):
        return [nat[k, j, pl.ds(i, SUB, stride=deep), :] for j in range(count)]

    base = events * (steps + 1)
    for k, (f, x) in enumerate(((base, bed), (base + 1, rough), (base + 2, direction))):
        assemble(f, x[...], k)
    for e in range(events):
        assemble(events * steps + e, wet[e].astype(jnp.float32), 3 + e)
        assemble(base + 3 + e, counts[e], 3 + events + e)
        for t in range(steps):
            assemble(e * steps + t, depth[e, t], 3 + 2 * events + e * steps + t)

    @pl.loop(0, deep, unroll=5)
    def _(i):
        m = [jnp.exp(x) for x in spread(1, i)]
        put(spread(0, i), tmp, 0, i)
        put(m, tmp, 1, i)
        put(m, m_c, i)
        put([x * y for x, y in zip(m, spread(2, i))], tmp, 2, i)
        for e in range(events):
            put(spread(3 + e, i), tmp, 3 + e, i)
            put(spread(3 + events + e, i), cnt, e, i)
            for t in range(steps):
                put(spread(3 + 2 * events + e * steps + t, i), hx, e, t, i)

    for k in range(3 + events):
        wrap(tmp, k)
    for e in range(events):
        for t in range(steps):
            wrap(hx, e, t)

    scale = time_step * 2.0 ** (-2.0 / 3.0)

    @pl.loop(0, deep, unroll=5)
    def _(i):
        b, m, q = (get(tmp, k, i) for k in range(3))
        put([y - x for x, y in zip(b, right(b))], sb_x, i)
        put([y - x for x, y in zip(b, get(tmp, 0, i + 1))], sb_y, i)
        ix = [1.0 / (x + y) for x, y in zip(m, right(m))]
        iy = [1.0 / (x + y) for x, y in zip(m, get(tmp, 1, i + 1))]
        put([-x for x in ix], inv_x, i)
        put([-x for x in iy], inv_y, i)
        put([x + y for x, y in zip(q, right(q))], q_x, i)
        put([x + y for x, y in zip(q, get(tmp, 2, i + 1))], q_y, i)
        for e in range(events):
            w = get(tmp, 3 + e, i)
            put([(scale * z) * (x * y) for x, y, z in zip(w, right(w), ix)], cond_x, e, i)
            put([(scale * z) * (x * y) for x, y, z in zip(w, get(tmp, 3 + e, i + 1), iy)], cond_y, e, i)

    def face(h, h_k, sb, cond, inv):
        hs = h + h_k
        s = (h_k - h) + sb
        x = s * s + slope_floor
        y = lax.rsqrt(x)
        p = cond * (jnp.exp2((2.0 / 3.0 / LN2) * jnp.log(hs)) * (y * lax.rsqrt(y)))
        ps = p * s
        t = p * hs
        A = (5.0 / 3.0) * ps
        B = t * (0.5 + (0.5 * slope_floor) * (y * y))
        return A - B, A + B, (ps * hs) * inv

    curve_ref[...] = jnp.zeros(curve_ref.shape, jnp.float32)
    put([zero] * count, flow, 0)

    @pl.loop(0, events)
    def _(e):
        for t in range(steps):
            old, new = (tan_a, tan_b) if t % 2 else (tan_b, tan_a)

            @pl.loop(0, deep, unroll=5)
            def _(i):
                h = get(hx, e, t, i)
                h_r, h_d = right(h), get(hx, e, t, i + 1)
                if t:
                    d = get(old, i)
                    d_r, d_d = right(d), get(old, i + 1)
                fx, fy = [], []
                for j in range(count):
                    A, B, C = face(h[j], h_r[j], sb_x[i, :, J[j]], cond_x[e, i, :, J[j]], inv_x[i, :, J[j]])
                    f = C * q_x[i, :, J[j]]
                    c_x[e, t, i, :, J[j]] = C
                    if t:
                        a_x[e, t - 1, i, :, J[j]] = A
                        b_x[e, t - 1, i, :, J[j]] = B
                        f += A * d[j] + B * d_r[j]
                    fx.append(f)
                    A, B, C = face(h[j], h_d[j], sb_y[i, :, J[j]], cond_y[e, i, :, J[j]], inv_y[i, :, J[j]])
                    f = C * q_y[i, :, J[j]]
                    c_y[e, t, i, :, J[j]] = C
                    if t:
                        a_y[e, t - 1, i, :, J[j]] = A
                        b_y[e, t - 1, i, :, J[j]] = B
                        f += A * d[j] + B * d_d[j]
                    fy.append(f)
                put(fy, flow, i + 1)
                before = get(flow, i)
                fl = left(fx)
                for j in range(count):
                    r = (fx[j] - fl[j]) + (fy[j] - before[j])
                    new[i, :, J[j]] = d[j] + r if t else r

            for j in range(count):
                new[0, :, J[j]] = new[0, :, J[j]] - down(flow[deep, :, J[j]])
            wrap(new)

        old = tan_a if steps % 2 else tan_b

        @pl.loop(0, deep, unroll=5)
        def _(i):
            row = sub * deep + i
            own = (row >= SUB) & (row < SUB + rows)
            total = zero
            for j in range(count):
                r = old[i, :, J[j]]
                s = (gauge_weight * cnt[e, i, :, J[j]]) * r
                source[e, i, :, J[j]] = s
                if j < tiles:
                    total += s * r
            curve_ref[...] += jnp.where(own, total, 0.0)

        wrap(source, e)


def adjoint_kernel(first_event, last_event, m_c, source, a_x, b_x, c_x, a_y, b_y, c_y, *refs):
    sums = () if first_event else refs[:2]
    outs = refs[len(sums) : len(sums) + (1 if last_event else 2)]
    nat, adj_a, adj_b, flow, *own = refs[len(sums) + len(outs) :]
    g_x, g_y = own if last_event else outs
    steps, deep, _, wide = c_x.shape
    count = wide // LANES
    J = [at_lanes(j) for j in range(count)]
    zero = jnp.zeros((SUB, LANES), jnp.float32)
    put([zero] * count, flow, 0)

    for t in range(steps - 1, -1, -1):
        old, new = (adj_a, adj_b) if t % 2 else (adj_b, adj_a)
        if t == steps - 1:
            old = source
            base_x, base_y = sums if sums else (None, None)
        else:
            base_x, base_y = g_x, g_y

        @pl.loop(0, deep, unroll=5)
        def _(i):
            l = get(old, i)
            l_r, l_d = right(l), get(old, i + 1)
            acc, kx, ky = [], [], []
            for j in range(count):
                p = l[j] - l_r[j]
                g = c_x[t, i, :, J[j]] * p
                g_x[i, :, J[j]] = g + base_x[i, :, J[j]] if base_x is not None else g
                if t:
                    a = l[j] + a_x[t - 1, i, :, J[j]] * p
                    kx.append(b_x[t - 1, i, :, J[j]] * p)
                p = l[j] - l_d[j]
                g = c_y[t, i, :, J[j]] * p
                g_y[i, :, J[j]] = g + base_y[i, :, J[j]] if base_y is not None else g
                if t:
                    acc.append(a + a_y[t - 1, i, :, J[j]] * p)
                    ky.append(b_y[t - 1, i, :, J[j]] * p)
            if t:
                put(ky, flow, i + 1)
                before = get(flow, i)
                kl = left(kx)
                for j in range(count):
                    new[i, :, J[j]] = acc[j] + (kl[j] + before[j])

        if t:
            for j in range(count):
                new[0, :, J[j]] = new[0, :, J[j]] + down(flow[deep, :, J[j]])
            wrap(new)

    if last_event:
        (grad_ref,) = outs
        rows, cols = grad_ref.shape
        tiles = cols // LANES
        put([down(x) for x in get(g_y, deep - 1)], flow, 0)

        @pl.loop(0, deep, unroll=5)
        def _(i):
            x, y = get(g_x, i), get(g_y, i)
            put(y, flow, i + 1)
            xl, yl = left(x), get(flow, i)
            for j in range(tiles):
                g = m_c[i, :, J[j]] * ((x[j] + xl[j]) + (y[j] + yl[j]))
                nat[j, pl.ds(i, SUB, stride=deep), :] = g

        for j in range(tiles):
            grad_ref[:, J[j]] = nat[j, SUB : SUB + rows, :]


def tangents(depth, wet, bed, rough, direction, counts, rim_top, rim_bottom, side_b, side_a):
    events, steps, rows, cols = depth.shape
    tall, wide = rows + 2 * SUB, cols + LANES
    deep = tall // SUB
    shape = lambda *lead: (*lead, deep, SUB, wide)
    vm = lambda *lead: pltpu.VMEM(shape(*lead), jnp.float32)
    more = lambda *lead: pltpu.VMEM((*lead, deep + 1, SUB, wide), jnp.float32)
    out = lambda *lead: jax.ShapeDtypeStruct(shape(*lead), jnp.float32)
    vmem = pl.BlockSpec(memory_space=pltpu.VMEM)
    fields = 3 + events * (steps + 2)
    return pl.pallas_call(
        tangent_kernel,
        in_specs=[vmem] * 10,
        out_specs=[vmem] * 9,
        out_shape=[
            jax.ShapeDtypeStruct((SUB, LANES), jnp.float32),
            out(),
            jax.ShapeDtypeStruct((events, deep + 1, SUB, wide), jnp.float32),
            *[out(events, steps - 1), out(events, steps - 1), out(events, steps)] * 2,
        ],
        scratch_shapes=[
            pltpu.VMEM((fields, wide // LANES, tall, LANES), jnp.float32),
            more(events, steps),
            *[vm()] * 6,
            *[vm(events)] * 3,
            *[more()] * 3,
            more(3 + events),
        ],
        compiler_params=pltpu.CompilerParams(vmem_limit_bytes=20 * 1024 * 1024),
        name="tangents",
    )(depth, wet, bed, rough, direction, counts, rim_top, rim_bottom, side_b, side_a)


def gradient(e, rows, cols, sums, m_c, source, *coefficients):
    events, _, _, wide = source.shape
    deep = m_c.shape[0]
    first, last = e == 0, e == events - 1
    vm = (deep, SUB, wide)
    more = pltpu.VMEM((deep + 1, SUB, wide), jnp.float32)
    vmem = pl.BlockSpec(memory_space=pltpu.VMEM)
    own = lambda x: pl.BlockSpec((None, *x.shape[1:]), lambda i: (e,) + (0,) * (x.ndim - 1))
    whole = lambda shape: pl.BlockSpec(shape, lambda i: (0,) * len(shape))
    return pl.pallas_call(
        functools.partial(adjoint_kernel, first, last),
        grid=(1,),
        in_specs=[whole(m_c.shape), own(source)] + [own(x) for x in coefficients] + [whole(vm)] * len(sums),
        out_specs=whole((rows, cols)) if last else [whole(vm)] * 2,
        out_shape=jax.ShapeDtypeStruct((rows, cols), jnp.float32)
        if last
        else [jax.ShapeDtypeStruct(vm, jnp.float32)] * 2,
        scratch_shapes=[pltpu.VMEM((cols // LANES, deep * SUB, LANES), jnp.float32), more, more, more]
        + [pltpu.VMEM(vm, jnp.float32)] * (2 if last else 0),
        compiler_params=pltpu.CompilerParams(vmem_limit_bytes=16 * 1024 * 1024),
        cost_estimate=pl.CostEstimate(flops=40000000, bytes_accessed=12000000, transcendentals=0),
        name="gradient",
    )(m_c, source, *coefficients, *sums)


def hops_over(axis):
    count, hop, out = lax.axis_size(axis), 1, []
    while hop < count:
        out.append((axis, hop))
        hop *= 2
    return out


def from_hop(x, axis, hop):
    return lax.ppermute(x, axis, [(i, i ^ hop) for i in range(lax.axis_size(axis))])


def hop_sum(x, axis, hop):
    return x + from_hop(x, axis, hop)


def finish_kernel(grad, arrived, curve, curve_arrived, hess, total):
    hess[...] = grad[...] + arrived[...]
    total[...] = jnp.sum(curve[...] + curve_arrived[...], keepdims=True)


def finish(grad, arrived, curve, curve_arrived):
    vmem = pl.BlockSpec(memory_space=pltpu.VMEM)
    hess, total = pl.pallas_call(
        finish_kernel,
        in_specs=[vmem] * 4,
        out_specs=[vmem] * 2,
        out_shape=[jax.ShapeDtypeStruct(grad.shape, grad.dtype), jax.ShapeDtypeStruct((1, 1), curve.dtype)],
        compiler_params=pltpu.CompilerParams(vmem_limit_bytes=4 * 1024 * 1024),
        name="finish",
    )(grad, arrived, curve, curve_arrived)
    return (hess, total.reshape(()))


def local(depth, wet, bed, rough, direction, gauge_cells):
    events, steps, rows, cols = depth.shape
    cells = gauge_cells.reshape(events, 1, -1)
    pays = edge_rows(cells, depth, wet, bed, rough, direction)
    rims = [exchange(x, "row", k) for k, x in enumerate(pays)]
    counts = gauges(cells, rows, cols)
    rim_top, rim_bottom, send_b, send_a = rims_and_columns(
        rims, depth, wet, bed, rough, direction, counts
    )
    side_b = exchange(send_b, "col", 1)
    side_a = exchange(send_a, "col", 0)
    curve, *coefficients = tangents(
        depth, wet, bed, rough, direction, counts, rim_top, rim_bottom, side_b, side_a
    )
    hops = hops_over("event") + hops_over("row") + hops_over("col")
    sums = ()
    for e in range(events):
        sums = gradient(e, rows, cols, sums, *coefficients)
        if hops:
            curve = hop_sum(curve, *hops.pop(0))
            sums, curve = lax.optimization_barrier((sums, curve))
    grad, arrived = sums, None
    for axis, hop in hops_over("event"):
        if arrived is not None:
            grad = grad + arrived
            if hops:
                curve = hop_sum(curve, *hops.pop(0))
                grad, curve = lax.optimization_barrier((grad, curve))
        arrived = from_hop(grad, axis, hop)
    while len(hops) > 1:
        curve = hop_sum(curve, *hops.pop(0))
    return finish(grad, arrived, curve, from_hop(curve, *hops[0]))


def solution(mesh):
    placed = (
        P("event", None, "row", "col"),
        P("event", "row", "col"),
        P("row", "col"),
        P("row", "col"),
        P("row", "col"),
        P("event", "row", "col", None),
    )
    return jax.shard_map(
        local, mesh=mesh, in_specs=placed, out_specs=(P("row", "col"), P()), check_vma=False
    )
```

```python
import functools

import jax
import jax.numpy as jnp
from jax import lax
from jax.experimental import pallas as pl
from jax.experimental.pallas import tpu as pltpu
from jax.sharding import PartitionSpec as P

time_step = 0.035
slope_floor = 0.01
gauge_weight = 100.0
REACH = 6
LANES = 128
LN2 = 0.6931471805599453
SUB = 8


def pairs(count, first):
    out = []
    for i in range(first, count - 1, 2):
        out += [(i, i + 1), (i + 1, i)]
    return out


def exchange(x, axis, first):
    perm = pairs(lax.axis_size(axis), first)
    return lax.ppermute(x, axis, perm) if perm else None


def lanes_of(shape):
    return lax.broadcasted_iota(jnp.int32, shape, 1)


def plan(events, steps):
    out, slot = [], 0
    for n in [REACH - t for _ in range(events) for t in range(steps)] + [REACH] * (events + 3) + [1] * events:
        out.append((n, slot))
        slot += n
    return out, -(-slot // SUB)


def one_hot(hit):
    return jnp.where(hit, 1.0, 0.0).astype(jnp.bfloat16)


def tally_of(row, col, rows, cols):
    gauges = row.shape[-1]
    tall = rows * (cols // 256)
    inside = (row >= 0) & (row < rows)
    high = jnp.where(inside, (col // 256) * rows + row, -1)
    hits = lax.dot_general(
        one_hot(lax.broadcasted_iota(jnp.int32, (tall, gauges), 0) == high),
        one_hot(lax.broadcasted_iota(jnp.int32, (256, gauges), 0) == col % 256),
        (((1,), (1,)), ((), ())),
        preferred_element_type=jnp.float32,
    )
    return [hits[b * rows : (b + 1) * rows] for b in range(cols // 256)]


def rows_kernel(sides, *refs):
    ins, pays, rest = refs[1:6], refs[6 : 6 + sides], refs[6 + sides :]
    cells, sems = rest[-2:]
    events, steps, rows, cols = ins[0].shape
    even = lax.axis_index("row") % 2 == 0
    slots, count = plan(events, steps)
    sub = lax.broadcasted_iota(jnp.int32, (SUB, cols), 0)
    copies = [pltpu.make_async_copy(refs[0], cells, sems.at[0, 5])]
    copies[0].start()
    for k in range(sides):
        sends_last = even if k == 0 else jnp.logical_not(even)
        edge = pl.multiple_of(jnp.where(sends_last, rows - SUB, 0), SUB)
        for i, x in enumerate(ins):
            lead = (slice(None),) * (len(x.shape) - 2)
            copy = pltpu.make_async_copy(
                x.at[(*lead, pl.ds(edge, SUB), slice(None))], rest[5 * k + i], sems.at[k, i]
            )
            copy.start()
            copies.append(copy)
    for copy in copies:
        copy.wait()
    for k, pay in enumerate(pays):
        d, w, b, r, v = rest[5 * k : 5 * k + 5]
        sends_last = even if k == 0 else jnp.logical_not(even)
        fields = [d[e, t] for e in range(events) for t in range(steps)]
        fields += [w[e].astype(jnp.float32) for e in range(events)] + [b[...], r[...], v[...]]
        fields += [jnp.broadcast_to(cells[e].astype(jnp.float32), (SUB, cols)) for e in range(events)]
        tiles = [jnp.zeros((SUB, cols), jnp.float32)] * count
        for x, (n, slot) in zip(fields, slots):
            if 1 < n < SUB:
                x = jnp.where(sends_last, pltpu.roll(x, n, 0), x)
            for i in range(slot // SUB, (slot + n - 1) // SUB + 1):
                low, high = slot - i * SUB, slot + n - i * SUB
                y = pltpu.roll(x, low % SUB, 0) if low % SUB else x
                tiles[i] = jnp.where((sub >= low) & (sub < high), y, tiles[i])
        for i in range(count):
            pay[i * SUB : (i + 1) * SUB] = tiles[i]


def edge_rows(cells, depth, wet, bed, rough, direction):
    events, steps, _, cols = depth.shape
    sides = 2 if lax.axis_size("row") > 2 else 1
    _, count = plan(events, steps)
    vmem, anywhere = pl.BlockSpec(memory_space=pltpu.VMEM), pl.BlockSpec(memory_space=pl.ANY)
    ins = (depth, wet, bed, rough, direction)
    return pl.pallas_call(
        functools.partial(rows_kernel, sides),
        in_specs=[anywhere] * 6,
        out_specs=[vmem] * sides,
        out_shape=[jax.ShapeDtypeStruct((count * SUB, cols), jnp.float32)] * sides,
        scratch_shapes=[pltpu.VMEM((*x.shape[:-2], SUB, cols), x.dtype) for x in ins] * sides
        + [pltpu.VMEM(cells.shape, cells.dtype), pltpu.SemaphoreType.DMA((sides, 6))],
        compiler_params=pltpu.CompilerParams(vmem_limit_bytes=58 * 1024 * 1024),
        name="edge_rows",
    )(cells, *ins)


def gauge_kernel(cells, cnt):
    events, rows, cols = cnt.shape
    for e in range(events):
        g = cells[e]
        for b, x in enumerate(tally_of(g // cols, g % cols, rows, cols)):
            cnt[e, :, b * 256 : (b + 1) * 256] = x


def gauges(cells, rows, cols):
    vmem = pl.BlockSpec(memory_space=pltpu.VMEM)
    return pl.pallas_call(
        gauge_kernel,
        in_specs=[vmem],
        out_specs=vmem,
        out_shape=jax.ShapeDtypeStruct((cells.shape[0], rows, cols), jnp.float32),
        compiler_params=pltpu.CompilerParams(vmem_limit_bytes=12 * 1024 * 1024),
        cost_estimate=pl.CostEstimate(flops=20000000, bytes_accessed=4000000, transcendentals=0),
        name="gauges",
    )(cells)


def column_kernel(sides, *refs):
    rims_in, own = refs[:sides], (refs[sides : sides + 6], refs[sides + 6 : sides + 12])
    rim_top, rim_bottom, pay_b, pay_a = refs[sides + 12 :]
    events, steps, rows, _ = own[0][0].shape
    cols = rim_top.shape[-1]
    even_row = lax.axis_index("row") % 2 == 0
    even_col = lax.axis_index("col") % 2 == 0
    sub = lax.broadcasted_iota(jnp.int32, (SUB, cols), 0)
    slots, _ = plan(events, steps)
    base = events * (steps + 1) + 3
    nothing = jnp.zeros((SUB, cols), jnp.float32)

    def field(ref, n, slot):
        x = nothing
        for i in range(slot // SUB, (slot + n - 1) // SUB + 1):
            low, high = slot - i * SUB, slot + n - i * SUB
            y = ref[i * SUB : (i + 1) * SUB]
            y = pltpu.roll(y, -low % SUB, 0) if low % SUB else y
            x = jnp.where((sub >= -low) & (sub < min(n, SUB - low)) & (sub >= max(0, -low)), y, x)
        return x

    for f in range(base):
        n, slot = slots[f]
        x = field(rims_in[0], n, slot)
        y = field(rims_in[1], n, slot) if sides > 1 else nothing
        rim_bottom[f] = jnp.where(even_row, x, y)
        rim_top[f] = pltpu.roll(jnp.where(even_row, y, x), SUB - n, 0)
    for e in range(events):
        slot = slots[base + e][1]
        for k in range(2):
            lower = even_row if k == 0 else jnp.logical_not(even_row)
            if k < sides:
                g = rims_in[k][slot : slot + 1].astype(jnp.int32)
                row = g // cols - jnp.where(lower, 0, rows - SUB)
                hits = jnp.concatenate(tally_of(row, g % cols, SUB, cols), axis=1)
            else:
                hits = nothing
            if k == 0:
                first = hits
        rim_bottom[base + e] = jnp.where(even_row, first, hits)
        rim_top[base + e] = jnp.where(even_row, hits, first)

    lane = lanes_of((rows + 2 * SUB, LANES))
    packs = []
    for side in range(2):
        d, w, b, r, v, c = own[side]
        place_of = slice(0, LANES) if side == 0 else slice(cols - LANES, cols)
        pack = jnp.zeros((rows + 2 * SUB, LANES), jnp.float32)
        xs = [d[e, t] for e in range(events) for t in range(steps)]
        xs += [w[e].astype(jnp.float32) for e in range(events)]
        xs += [b[...], r[...], v[...]]
        xs += [c[e] for e in range(events)]
        for f, x in enumerate(xs):
            x = jnp.concatenate([rim_top[f, :, place_of], x, rim_bottom[f, :, place_of]], axis=0)
            place = f * REACH
            shift = (place + REACH if side == 1 else place) % LANES
            if shift:
                x = pltpu.roll(x, shift, 1)
            pack = jnp.where((lane >= place) & (lane < place + REACH), x, pack)
        packs.append(pack)
    pay_a[...] = jnp.where(even_col, packs[1], packs[0])
    pay_b[...] = jnp.where(even_col, packs[0], packs[1])


def rims_and_columns(rims, depth, wet, bed, rough, direction, counts):
    events, steps, rows, cols = depth.shape
    last = cols // LANES - 1

    def side(j):
        return [
            pl.BlockSpec((events, steps, rows, LANES), lambda i: (0, 0, 0, j)),
            pl.BlockSpec((events, rows, LANES), lambda i: (0, 0, j)),
            pl.BlockSpec((rows, LANES), lambda i: (0, j)),
            pl.BlockSpec((rows, LANES), lambda i: (0, j)),
            pl.BlockSpec((rows, LANES), lambda i: (0, j)),
            pl.BlockSpec((events, rows, LANES), lambda i: (0, 0, j)),
        ]

    whole = lambda shape: pl.BlockSpec(shape, lambda i: (0,) * len(shape))
    tall = (rows + 2 * SUB, LANES)
    rim = (events * (steps + 2) + 3, SUB, cols)
    own = (depth, wet, bed, rough, direction, counts)
    return pl.pallas_call(
        functools.partial(column_kernel, len(rims)),
        grid=(1,),
        in_specs=[whole(r.shape) for r in rims] + side(0) + side(last),
        out_specs=[whole(rim)] * 2 + [whole(tall)] * 2,
        out_shape=[jax.ShapeDtypeStruct(rim, jnp.float32)] * 2 + [jax.ShapeDtypeStruct(tall, jnp.float32)] * 2,
        compiler_params=pltpu.CompilerParams(vmem_limit_bytes=12 * 1024 * 1024),
        name="rims_and_columns",
    )(*rims, *own, *own)


def up(x):
    return pltpu.roll(x, SUB - 1, 0)


def down(x):
    return pltpu.roll(x, 1, 0)


def right(xs):
    last = lanes_of((SUB, LANES)) == LANES - 1
    r = [pltpu.roll(x, LANES - 1, 1) for x in xs]
    return [jnp.where(last, r[(j + 1) % len(xs)], r[j]) for j in range(len(xs))]


def left(xs):
    first = lanes_of((SUB, LANES)) == 0
    r = [pltpu.roll(x, 1, 1) for x in xs]
    return [jnp.where(first, r[j - 1], r[j]) for j in range(len(xs))]


def at_lanes(j):
    return slice(j * LANES, (j + 1) * LANES)


def get(ref, *at):
    return [ref[(*at, slice(None), at_lanes(j))] for j in range(ref.shape[-1] // LANES)]


def put(xs, ref, *at):
    for j, x in enumerate(xs):
        ref[(*at, slice(None), at_lanes(j))] = x


def wrap(ref, *at):
    deep = ref.shape[-3] - 1
    put([up(x) for x in get(ref, *at, 0)], ref, *at, deep)


def up(x):
    return pltpu.roll(x, SUB - 1, 0)


def down(x):
    return pltpu.roll(x, 1, 0)


def sublanes():
    return lax.broadcasted_iota(jnp.int32, (SUB, LANES), 0)


def to_right(x, nxt):
    last = lanes_of((SUB, LANES)) == LANES - 1
    return jnp.where(last, pltpu.roll(nxt, LANES - 1, 1), pltpu.roll(x, LANES - 1, 1))


def right(xs):
    last = lanes_of((SUB, LANES)) == LANES - 1
    r = [pltpu.roll(x, LANES - 1, 1) for x in xs]
    return [jnp.where(last, r[(j + 1) % len(xs)], r[j]) for j in range(len(xs))]


def left(xs):
    first = lanes_of((SUB, LANES)) == 0
    r = [pltpu.roll(x, 1, 1) for x in xs]
    return [jnp.where(first, r[j - 1], r[j]) for j in range(len(xs))]


def at_lanes(j):
    return slice(j * LANES, (j + 1) * LANES)


def get(ref, *at):
    return [ref[(*at, slice(None), at_lanes(j))] for j in range(ref.shape[-1] // LANES)]


def put(xs, ref, *at):
    for j, x in enumerate(xs):
        ref[(*at, slice(None), at_lanes(j))] = x


def followers(first, below, above):
    last = sublanes() == SUB - 1
    f, b, a = up(first), up(below), up(above)
    return jnp.where(last, b, f), b, jnp.where(last, f, a)


def follow(ref, *at):
    deep = ref.shape[-3] - 5
    sets = zip(get(ref, *at, 0), get(ref, *at, deep), get(ref, *at, deep + 1))
    for k, xs in enumerate(zip(*[followers(*x) for x in sets])):
        put(xs, ref, *at, deep + 2 + k)


def preceding(ref, deep, passed):
    first = sublanes() == 0
    last, below, above = get(ref, deep), get(ref, deep + 1), get(ref, deep + 2)
    return (
        [jnp.where(first, down(a), down(l)) for a, l in zip(above, last)],
        [jnp.where(first, down(l), down(b)) - l for b, l in zip(below, last)],
        [down(a) - b for a, b in zip(above, below)],
    )


def face(h, h_k, sb, cond, inv):
    hs = h + h_k
    s = (h_k - h) + sb
    x = s * s + slope_floor
    y = lax.rsqrt(x)
    p = cond * (jnp.exp2((2.0 / 3.0 / LN2) * jnp.log(hs)) * (y * lax.rsqrt(y)))
    ps = p * s
    t = p * hs
    A = (5.0 / 3.0) * ps
    B = t * (0.5 + (0.5 * slope_floor) * (y * y))
    return A - B, A + B, (ps * hs) * inv


scale = time_step * 2.0 ** (-2.0 / 3.0)


def inner_kernel(
    depth, wet, bed, rough, direction, counts,
    prim, cnt, a_x, b_x, c_x, a_y, b_y, c_y, q_x, q_y,
    nat, sb_x, sb_y, inv_x, inv_y, cond_x, cond_y,
):
    events, steps, rows, cols = depth.shape
    deep, count = rows // SUB, cols // LANES
    fields = [bed, rough, direction] + [wet.at[e] for e in range(events)]
    fields += [depth.at[e, t] for e in range(events) for t in range(steps)]
    fields += [counts.at[e] for e in range(events)]
    for k, x in enumerate(fields):
        for j in range(count):
            nat[k, j] = x[:, at_lanes(j)].astype(jnp.float32)

    @pl.loop(0, deep, unroll=4)
    def _(i):
        spread = lambda k: [nat[k, j, pl.ds(i, SUB, stride=deep), :] for j in range(count)]
        m = [jnp.exp(x) for x in spread(1)]
        put(spread(0), prim, 0, i)
        put(m, prim, 1, i)
        put([x * y for x, y in zip(m, spread(2))], prim, 2, i)
        for k in range(3, 3 + events * (steps + 1)):
            put(spread(k), prim, k, i)
        for e in range(events):
            put(spread(3 + events * (steps + 1) + e), cnt, e, i)

    for k in range(3 + events * (steps + 1)):
        put([up(x) for x in get(prim, k, 0)], prim, k, deep)

    @pl.loop(0, deep, unroll=4)
    def _(i):
        b, m, q = (get(prim, k, i) for k in range(3))
        put([y - x for x, y in zip(b, right(b))], sb_x, i)
        put([y - x for x, y in zip(b, get(prim, 0, i + 1))], sb_y, i)
        ix = [1.0 / (x + y) for x, y in zip(m, right(m))]
        iy = [1.0 / (x + y) for x, y in zip(m, get(prim, 1, i + 1))]
        put([-x for x in ix], inv_x, i)
        put([-x for x in iy], inv_y, i)
        put([x + y for x, y in zip(q, right(q))], q_x, i)
        put([x + y for x, y in zip(q, get(prim, 2, i + 1))], q_y, i)
        for e in range(events):
            w = get(prim, 3 + e, i)
            put([(scale * z) * (x * y) for x, y, z in zip(w, right(w), ix)], cond_x, e, i)
            put([(scale * z) * (x * y) for x, y, z in zip(w, get(prim, 3 + e, i + 1), iy)], cond_y, e, i)

    @pl.loop(0, events)
    def _(e):
        for t in range(steps):

            @pl.loop(0, deep, unroll=4)
            def _(i):
                k = 3 + events + e * steps + t
                h = get(prim, k, i)
                h_r, h_d = right(h), get(prim, k, i + 1)
                for j in range(count):
                    J = at_lanes(j)
                    for h_k, sb, cond, inv, a, b, c in (
                        (h_r, sb_x, cond_x, inv_x, a_x, b_x, c_x),
                        (h_d, sb_y, cond_y, inv_y, a_y, b_y, c_y),
                    ):
                        A, B, C = face(h[j], h_k[j], sb[i, :, J], cond[e, i, :, J], inv[i, :, J])
                        c[e, t, i, :, J] = C
                        if t:
                            a[e, t - 1, i, :, J] = A
                            b[e, t - 1, i, :, J] = B


def inner(depth, wet, bed, rough, direction, counts):
    events, steps, rows, cols = depth.shape
    deep = rows // SUB
    shape = lambda *lead: (*lead, deep, SUB, cols)
    vm = lambda *lead: pltpu.VMEM(shape(*lead), jnp.float32)
    out = lambda *lead: jax.ShapeDtypeStruct(shape(*lead), jnp.float32)
    vmem = pl.BlockSpec(memory_space=pltpu.VMEM)
    fields = 3 + events * (steps + 1)
    return pl.pallas_call(
        inner_kernel,
        in_specs=[vmem] * 6,
        out_specs=[vmem] * 10,
        out_shape=[
            jax.ShapeDtypeStruct((fields, deep + 1, SUB, cols), jnp.float32),
            out(events),
            *[out(events, steps - 1), out(events, steps - 1), out(events, steps)] * 2,
            out(),
            out(),
        ],
        scratch_shapes=[
            pltpu.VMEM((fields + events, cols // LANES, rows, LANES), jnp.float32),
            *[vm()] * 4,
            *[vm(events)] * 2,
        ],
        compiler_params=pltpu.CompilerParams(vmem_limit_bytes=12 * 1024 * 1024),
        cost_estimate=pl.CostEstimate(flops=100000000, bytes_accessed=16000000, transcendentals=0),
        name="inner",
    )(depth, wet, bed, rough, direction, counts)


def tangent_kernel(
    prim, cnt, ia_x, ib_x, ic_x, ia_y, ib_y, ic_y, iq_x, iq_y, rim_top, rim_bottom, side_b, side_a,
    curve_ref, source, a_x, b_x, c_x, a_y, b_y, c_y,
    nat, ext, xcnt, sb_x, sb_y, q_x, q_y, inv_x, inv_y, cond_x, cond_y, tan_a, tan_b, flow,
):
    events, steps, deep, _, cols = ic_x.shape
    rows, tiles = deep * SUB, cols // LANES
    count, tall = tiles + 1, rows + 2 * SUB
    even_col = lax.axis_index("col") % 2 == 0
    lane_t = lanes_of((tall, LANES))
    right_rim = jnp.where(even_col, side_a[...], side_b[...])
    left_rim = jnp.where(even_col, side_b[...], side_a[...])
    J = [at_lanes(j) for j in range(count)]
    zero = jnp.zeros((SUB, LANES), jnp.float32)
    below, above = deep, deep + 1
    fields = prim.shape[0]

    place_in = [events * (steps + 1) + k for k in range(3)]
    place_in += [events * steps + e for e in range(events)]
    place_in += [e * steps + t for e in range(events) for t in range(steps)]
    place_in += [events * (steps + 1) + 3 + e for e in range(events)]
    for k, f in enumerate(place_in):
        place = f * REACH
        r = pltpu.roll(right_rim, (LANES - place) % LANES, 1) if place else right_rim
        l = pltpu.roll(left_rim, (LANES - REACH - place) % LANES, 1)
        x = jnp.where(lane_t < REACH, r, jnp.where(lane_t >= LANES - REACH, l, 0.0))
        if k == 1:
            m_side = x = jnp.exp(x)
        if k == 2:
            x = m_side * x
        nat[k] = x
        to, n = (ext, k) if k < fields else (xcnt, k - fields)
        for i in range(deep):
            to[n, i, :, J[tiles]] = nat[k, pl.ds(SUB + i, SUB, stride=deep), :]
        for i, rim, at in ((below, rim_bottom, SUB + rows), (above, rim_top, 0)):
            xs = get(rim, f)
            if k == 1:
                xs = [jnp.exp(x) for x in xs]
            if k == 2:
                xs = [x * y for x, y in zip(xs, get(ext, 1, i))]
            put(xs, to, n, i)
            to[n, i, :, J[tiles]] = nat[k, at : at + SUB, :]

    def value(k, i, j):
        return ext[k, i, :, J[j]] if j == tiles or (isinstance(i, int) and i >= deep) else prim[k, i, :, J[j]]

    def next_rows(k, j):
        return followers(value(k, 0, j), value(k, below, j), value(k, above, j))

    for k in range(fields):
        ext[k, deep + 2, :, J[tiles]] = next_rows(k, tiles)[0]

    def derive(i, j, along, k_of):
        sb, inv, q, cond = (sb_x, inv_x, q_x, cond_x) if along else (sb_y, inv_y, q_y, cond_y)
        x, y = k_of(0)
        sb[i, :, J[j]] = y - x
        x, y = k_of(1)
        z = 1.0 / (x + y)
        inv[i, :, J[j]] = -z
        x, y = k_of(2)
        q[i, :, J[j]] = x + y
        for e in range(events):
            x, y = k_of(3 + e)
            cond[e, i, :, J[j]] = (scale * z) * (x * y)

    def across(i, j):
        return lambda k: (value(k, i, j), to_right(value(k, i, j), value(k, i, (j + 1) % count)))

    @pl.loop(0, deep, unroll=4)
    def _(i):
        for j in (tiles - 1, tiles):
            derive(i, j, True, across(i, j))
        n = jnp.where(i == deep - 1, deep + 2, i + 1)
        derive(i, tiles, False, lambda k: (value(k, i, tiles), ext[k, n, :, J[tiles]]))

    for i in (below, above):
        for j in range(count):
            derive(i, j, True, across(i, j))
    for n, i in enumerate((deep - 1, below, above)):
        for j in range(tiles if n == 0 else count):
            derive(i, j, False, lambda k: (value(k, i, j), next_rows(k, j)[n]))

    curve_ref[...] = jnp.zeros(curve_ref.shape, jnp.float32)
    put([zero] * count, flow, 0)

    @pl.loop(0, events)
    def _(e):
        for t in range(steps):
            old, new = (tan_a, tan_b) if t % 2 else (tan_b, tan_a)
            k = 3 + events + e * steps + t

            def row(i):
                static = isinstance(i, int)
                rim = static and i >= deep
                nxt = i + 3 if static and i >= deep - 1 else i + 1
                if t:
                    d = get(old, i)
                    d_r, d_d = right(d), get(old, nxt)
                fx, fy = [], []
                here = lambda j: ext[k, i, :, J[j]] if rim or j == tiles else prim[k, i, :, J[j]]
                for j in range(count):
                    inside = not rim and j < tiles - 1
                    if inside:
                        A, B = (ia_x[e, t - 1, i, :, J[j]], ib_x[e, t - 1, i, :, J[j]]) if t else (None, None)
                        C = ic_x[e, t, i, :, J[j]]
                        f = C * iq_x[i, :, J[j]]
                    else:
                        h = here(j)
                        A, B, C = face(
                            h, to_right(h, here((j + 1) % count)),
                            sb_x[i, :, J[j]], cond_x[e, i, :, J[j]], inv_x[i, :, J[j]],
                        )
                        f = C * q_x[i, :, J[j]]
                    c_x[e, t, i, :, J[j]] = C
                    if t:
                        a_x[e, t - 1, i, :, J[j]] = A
                        b_x[e, t - 1, i, :, J[j]] = B
                        f += A * d[j] + B * d_r[j]
                    fx.append(f)
                    inside = not (static and i >= deep - 1) and j < tiles
                    if inside:
                        A, B = (ia_y[e, t - 1, i, :, J[j]], ib_y[e, t - 1, i, :, J[j]]) if t else (None, None)
                        C = ic_y[e, t, i, :, J[j]]
                        f = C * iq_y[i, :, J[j]]
                    else:
                        h = here(j)
                        if static and i >= deep - 1:
                            first = ext[k, 0, :, J[j]] if j == tiles else prim[k, 0, :, J[j]]
                            h_d = followers(first, ext[k, below, :, J[j]], ext[k, above, :, J[j]])[i - deep + 1]
                        else:
                            h_d = ext[k, i + 1, :, J[j]]
                        A, B, C = face(h, h_d, sb_y[i, :, J[j]], cond_y[e, i, :, J[j]], inv_y[i, :, J[j]])
                        f = C * q_y[i, :, J[j]]
                    c_y[e, t, i, :, J[j]] = C
                    if t:
                        a_y[e, t - 1, i, :, J[j]] = A
                        b_y[e, t - 1, i, :, J[j]] = B
                        f += A * d[j] + B * d_d[j]
                    fy.append(f)
                put(fy, flow, i + 1)
                before = get(flow, i)
                fl = left(fx)
                for j in range(count):
                    r = (fx[j] - fl[j]) + (fy[j] - before[j])
                    new[i, :, J[j]] = d[j] + r if t else r

            main = deep - 2
            pl.loop(0, main, unroll=3 if main % 3 == 0 else 1)(row)
            for i in range(main, deep + 2):
                row(i)
            for i, lack in zip((0, below, above), preceding(flow, deep, zero)):
                put([x - y for x, y in zip(get(new, i), lack)], new, i)
            follow(new)

        old = tan_a if steps % 2 else tan_b
        total = zero
        for i in range(deep + 2):
            for j in range(count):
                own = i < deep and j < tiles
                n = cnt[e, i, :, J[j]] if own else xcnt[e, i, :, J[j]]
                r = old[i, :, J[j]]
                s = (gauge_weight * n) * r
                source[e, i, :, J[j]] = s
                if own:
                    total += s * r
        curve_ref[...] += total
        follow(source, e)


def tangents(prim, cnt, *more_inputs):
    fields, _, _, cols = prim.shape
    events, deep = cnt.shape[:2]
    steps = more_inputs[2].shape[1]
    wide = cols + LANES
    regs = deep + 2
    vm = lambda *lead: pltpu.VMEM((*lead, regs, SUB, wide), jnp.float32)
    more = lambda *lead: pltpu.VMEM((*lead, regs + 3, SUB, wide), jnp.float32)
    out = lambda *lead: jax.ShapeDtypeStruct((*lead, regs, SUB, wide), jnp.float32)
    vmem = pl.BlockSpec(memory_space=pltpu.VMEM)
    return pl.pallas_call(
        tangent_kernel,
        in_specs=[vmem] * (2 + len(more_inputs)),
        out_specs=[vmem] * 8,
        out_shape=[
            jax.ShapeDtypeStruct((SUB, LANES), jnp.float32),
            jax.ShapeDtypeStruct((events, regs + 3, SUB, wide), jnp.float32),
            *[out(events, steps - 1), out(events, steps - 1), out(events, steps)] * 2,
        ],
        scratch_shapes=[
            pltpu.VMEM((fields + events, deep * SUB + 2 * SUB, LANES), jnp.float32),
            more(fields),
            vm(events),
            *[vm()] * 6,
            *[vm(events)] * 2,
            *[more()] * 3,
        ],
        compiler_params=pltpu.CompilerParams(vmem_limit_bytes=16 * 1024 * 1024),
        name="tangents",
    )(prim, cnt, *more_inputs)


def adjoint_kernel(first_event, last_event, m_c, source, a_x, b_x, c_x, a_y, b_y, c_y, *refs):
    sums = () if first_event else refs[:2]
    outs = refs[len(sums) : len(sums) + (1 if last_event else 2)]
    nat, adj_a, adj_b, flow, *own = refs[len(sums) + len(outs) :]
    g_x, g_y = own if last_event else outs
    steps, regs, _, wide = c_x.shape
    deep = regs - 2
    count = wide // LANES
    J = [at_lanes(j) for j in range(count)]
    zero = jnp.zeros((SUB, LANES), jnp.float32)
    put([zero] * count, flow, 0)

    for t in range(steps - 1, -1, -1):
        old, new = (adj_a, adj_b) if t % 2 else (adj_b, adj_a)
        if t == steps - 1:
            old = source
            base_x, base_y = sums if sums else (None, None)
        else:
            base_x, base_y = g_x, g_y

        @pl.loop(0, regs, unroll=5 if regs % 5 == 0 else 1)
        def _(i):
            l = get(old, i)
            l_r, l_d = right(l), get(old, jnp.where(i < deep - 1, i + 1, i + 3))
            acc, kx, ky = [], [], []
            for j in range(count):
                p = l[j] - l_r[j]
                g = c_x[t, i, :, J[j]] * p
                g_x[i, :, J[j]] = g + base_x[i, :, J[j]] if base_x is not None else g
                if t:
                    a = l[j] + a_x[t - 1, i, :, J[j]] * p
                    kx.append(b_x[t - 1, i, :, J[j]] * p)
                p = l[j] - l_d[j]
                g = c_y[t, i, :, J[j]] * p
                g_y[i, :, J[j]] = g + base_y[i, :, J[j]] if base_y is not None else g
                if t:
                    acc.append(a + a_y[t - 1, i, :, J[j]] * p)
                    ky.append(b_y[t - 1, i, :, J[j]] * p)
            if t:
                put(ky, flow, i + 1)
                before = get(flow, i)
                kl = left(kx)
                for j in range(count):
                    new[i, :, J[j]] = acc[j] + (kl[j] + before[j])

        if t:
            for i, lack in zip((0, deep, deep + 1), preceding(flow, deep, zero)):
                put([x + y for x, y in zip(get(new, i), lack)], new, i)
            follow(new)

    if last_event:
        (grad_ref,) = outs
        tiles = grad_ref.shape[-1] // LANES
        first = sublanes() == 0
        put(
            [jnp.where(first, down(a), down(l)) for a, l in zip(get(g_y, deep + 1), get(g_y, deep - 1))],
            flow,
            0,
        )

        @pl.loop(0, deep, unroll=4)
        def _(i):
            x, y = get(g_x, i), get(g_y, i)
            put(y, flow, i + 1)
            xl, yl = left(x), get(flow, i)
            for j in range(tiles):
                g = m_c[i, :, J[j]] * ((x[j] + xl[j]) + (y[j] + yl[j]))
                nat[j, pl.ds(i, SUB, stride=deep), :] = g

        for j in range(tiles):
            grad_ref[:, J[j]] = nat[j]


def gradient(e, sums, prim, source, *coefficients):
    events, entries, _, wide = source.shape
    cols, regs = prim.shape[-1], entries - 3
    rows = (regs - 2) * SUB
    first, last = e == 0, e == events - 1
    vm = (regs, SUB, wide)
    more = pltpu.VMEM((entries, SUB, wide), jnp.float32)
    own = lambda x: pl.BlockSpec((None, *x.shape[1:]), lambda i: (e,) + (0,) * (x.ndim - 1))
    whole = lambda shape: pl.BlockSpec(shape, lambda i: (0,) * len(shape))
    return pl.pallas_call(
        functools.partial(adjoint_kernel, first, last),
        grid=(1,),
        in_specs=[pl.BlockSpec((None, *prim.shape[1:]), lambda i: (1, 0, 0, 0)), own(source)]
        + [own(x) for x in coefficients]
        + [whole(vm)] * len(sums),
        out_specs=whole((rows, cols)) if last else [whole(vm)] * 2,
        out_shape=jax.ShapeDtypeStruct((rows, cols), jnp.float32)
        if last
        else [jax.ShapeDtypeStruct(vm, jnp.float32)] * 2,
        scratch_shapes=[pltpu.VMEM((cols // LANES, rows, LANES), jnp.float32), more, more, more]
        + [pltpu.VMEM(vm, jnp.float32)] * (2 if last else 0),
        compiler_params=pltpu.CompilerParams(vmem_limit_bytes=16 * 1024 * 1024),
        cost_estimate=pl.CostEstimate(flops=40000000, bytes_accessed=12000000, transcendentals=0),
        name="gradient",
    )(prim, source, *coefficients, *sums)


def hops_over(axis):
    count, hop, out = lax.axis_size(axis), 1, []
    while hop < count:
        out.append((axis, hop))
        hop *= 2
    return out


def from_hop(x, axis, hop):
    return lax.ppermute(x, axis, [(i, i ^ hop) for i in range(lax.axis_size(axis))])


def hop_sum(x, axis, hop):
    return x + from_hop(x, axis, hop)


def finish_kernel(grad, arrived, curve, curve_arrived, hess, total):
    hess[...] = grad[...] + arrived[...]
    total[...] = jnp.sum(curve[...] + curve_arrived[...], keepdims=True)


def finish(grad, arrived, curve, curve_arrived):
    vmem = pl.BlockSpec(memory_space=pltpu.VMEM)
    hess, total = pl.pallas_call(
        finish_kernel,
        in_specs=[vmem] * 4,
        out_specs=[vmem] * 2,
        out_shape=[jax.ShapeDtypeStruct(grad.shape, grad.dtype), jax.ShapeDtypeStruct((1, 1), curve.dtype)],
        compiler_params=pltpu.CompilerParams(vmem_limit_bytes=4 * 1024 * 1024),
        name="finish",
    )(grad, arrived, curve, curve_arrived)
    return (hess, total.reshape(()))


def local(depth, wet, bed, rough, direction, gauge_cells):
    events, steps, rows, cols = depth.shape
    cells = gauge_cells.reshape(events, 1, -1)
    pays = edge_rows(cells, depth, wet, bed, rough, direction)
    rims = [exchange(x, "row", k) for k, x in enumerate(pays)]
    counts = gauges(cells, rows, cols)
    block = inner(depth, wet, bed, rough, direction, counts)
    rims, block = lax.optimization_barrier((rims, block))
    rim_top, rim_bottom, send_b, send_a = rims_and_columns(
        rims, depth, wet, bed, rough, direction, counts
    )
    side_b = exchange(send_b, "col", 1)
    side_a = exchange(send_a, "col", 0)
    curve, *coefficients = tangents(*block, rim_top, rim_bottom, side_b, side_a)
    hops = hops_over("event") + hops_over("row") + hops_over("col")
    sums = ()
    for e in range(events):
        sums = gradient(e, sums, block[0], *coefficients)
        if hops:
            curve = hop_sum(curve, *hops.pop(0))
            sums, curve = lax.optimization_barrier((sums, curve))
    grad, arrived = sums, None
    for axis, hop in hops_over("event"):
        if arrived is not None:
            grad = grad + arrived
            if hops:
                curve = hop_sum(curve, *hops.pop(0))
                grad, curve = lax.optimization_barrier((grad, curve))
        arrived = from_hop(grad, axis, hop)
    while len(hops) > 1:
        curve = hop_sum(curve, *hops.pop(0))
    return finish(grad, arrived, curve, from_hop(curve, *hops[0]))


def solution(mesh):
    placed = (
        P("event", None, "row", "col"),
        P("event", "row", "col"),
        P("row", "col"),
        P("row", "col"),
        P("row", "col"),
        P("event", "row", "col", None),
    )
    return jax.shard_map(
        local, mesh=mesh, in_specs=placed, out_specs=(P("row", "col"), P()), check_vma=False
    )
```

```python
import functools

import jax
import jax.numpy as jnp
from jax import lax
from jax.experimental import pallas as pl
from jax.experimental.pallas import tpu as pltpu
from jax.sharding import PartitionSpec as P

time_step = 0.035
slope_floor = 0.01
gauge_weight = 100.0
REACH = 6
LANES = 128
LN2 = 0.6931471805599453
SUB = 8


def pairs(count, first):
    out = []
    for i in range(first, count - 1, 2):
        out += [(i, i + 1), (i + 1, i)]
    return out


def exchange(x, axis, first):
    perm = pairs(lax.axis_size(axis), first)
    return lax.ppermute(x, axis, perm) if perm else None


def lanes_of(shape):
    return lax.broadcasted_iota(jnp.int32, shape, 1)


def plan(events, steps):
    out, slot = [], 0
    for n in [REACH - t for _ in range(events) for t in range(steps)] + [REACH] * (events + 3) + [1] * events:
        out.append((n, slot))
        slot += n
    return out, -(-slot // SUB)


def one_hot(hit):
    return jnp.where(hit, 1.0, 0.0).astype(jnp.bfloat16)


def tally_of(row, col, rows, cols):
    gauges = row.shape[-1]
    tall = rows * (cols // 256)
    inside = (row >= 0) & (row < rows)
    high = jnp.where(inside, (col // 256) * rows + row, -1)
    hits = lax.dot_general(
        one_hot(lax.broadcasted_iota(jnp.int32, (tall, gauges), 0) == high),
        one_hot(lax.broadcasted_iota(jnp.int32, (256, gauges), 0) == col % 256),
        (((1,), (1,)), ((), ())),
        preferred_element_type=jnp.float32,
    )
    return [hits[b * rows : (b + 1) * rows] for b in range(cols // 256)]


def edge_kernel(sides, *refs):
    ins, outs, rest = refs[1:6], refs[6 : 9 + 3 * sides], refs[9 + 3 * sides :]
    cnt, pay_a, pay_b, *more = outs
    pays, corners = more[:sides], more[sides:]
    cells, sems = rest[-2:]
    events, steps, rows, cols = ins[0].shape
    even = lax.axis_index("row") % 2 == 0
    even_col = lax.axis_index("col") % 2 == 0
    slots, count = plan(events, steps)
    sub = lax.broadcasted_iota(jnp.int32, (SUB, cols), 0)
    copies = [pltpu.make_async_copy(refs[0], cells, sems.at[0, 5])]
    edges = []
    for k in range(sides):
        sends_last = even if k == 0 else jnp.logical_not(even)
        edge = pl.multiple_of(jnp.where(sends_last, rows - SUB, 0), SUB)
        edges.append((sends_last, edge))
        for i, x in enumerate(ins):
            lead = (slice(None),) * (len(x.shape) - 2)
            at = x.at[(*lead, pl.ds(edge, SUB), slice(None))]
            copies.append(pltpu.make_async_copy(at, rest[5 * k + i], sems.at[k, i]))
    columns = (rest[5 * sides : 5 * sides + 5], rest[5 * sides + 5 : 5 * sides + 10])
    for k in range(2):
        for i, x in enumerate(ins):
            lead = (slice(None),) * (len(x.shape) - 1)
            at = x.at[(*lead, slice(0, LANES) if k == 0 else slice(cols - LANES, cols))]
            copies.append(pltpu.make_async_copy(at, columns[k][i], sems.at[sides + k, i]))
    for copy in copies:
        copy.start()
    copies[0].wait()
    for e in range(events):
        g = cells[e]
        for b, x in enumerate(tally_of(g // cols, g % cols, rows, cols)):
            for j in range(256 // LANES):
                cnt[e, b * (256 // LANES) + j] = x[:, j * LANES : (j + 1) * LANES]
    for copy in copies[1:]:
        copy.wait()

    for k, pay in enumerate(pays):
        d, w, b, r, v = rest[5 * k : 5 * k + 5]
        fields = [d[e, t] for e in range(events) for t in range(steps)]
        fields += [w[e].astype(jnp.float32) for e in range(events)] + [b[...], r[...], v[...]]
        fields += [jnp.broadcast_to(cells[e].astype(jnp.float32), (SUB, cols)) for e in range(events)]
        tiles = [jnp.zeros((SUB, cols), jnp.float32)] * count
        for x, (n, slot) in zip(fields, slots):
            if 1 < n < SUB:
                x = jnp.where(edges[k][0], pltpu.roll(x, n, 0), x)
            for i in range(slot // SUB, (slot + n - 1) // SUB + 1):
                low, high = slot - i * SUB, slot + n - i * SUB
                y = pltpu.roll(x, low % SUB, 0) if low % SUB else x
                tiles[i] = jnp.where((sub >= low) & (sub < high), y, tiles[i])
        for i in range(count):
            pay[i * SUB : (i + 1) * SUB] = tiles[i]

    lane = lanes_of((rows, LANES))
    packs = []
    for side in range(2):
        d, w, b, r, v = columns[side]
        pack = jnp.zeros((rows, LANES), jnp.float32)
        xs = [d[e, t] for e in range(events) for t in range(steps)]
        xs += [w[e].astype(jnp.float32) for e in range(events)]
        xs += [b[...], r[...], v[...]]
        xs += [cnt[e, 0 if side == 0 else cols // LANES - 1] for e in range(events)]
        for f, x in enumerate(xs):
            place = f * REACH
            shift = (place + REACH if side == 1 else place) % LANES
            if shift:
                x = pltpu.roll(x, shift, 1)
            pack = jnp.where((lane >= place) & (lane < place + REACH), x, pack)
        packs.append(pack)
    pay_a[...] = jnp.where(even_col, packs[1], packs[0])
    pay_b[...] = jnp.where(even_col, packs[0], packs[1])
    for k in range(sides):
        corners[2 * k][...] = pay_a[pl.ds(edges[k][1], SUB), :]
        corners[2 * k + 1][...] = pay_b[pl.ds(edges[k][1], SUB), :]


def edges_and_gauges(cells, depth, wet, bed, rough, direction):
    events, steps, rows, cols = depth.shape
    sides = 2 if lax.axis_size("row") > 2 else 1
    _, count = plan(events, steps)
    vmem, anywhere = pl.BlockSpec(memory_space=pltpu.VMEM), pl.BlockSpec(memory_space=pl.ANY)
    ins = (depth, wet, bed, rough, direction)
    shapes = [(events, cols // LANES, rows, LANES)] + [(rows, LANES)] * 2
    shapes += [(count * SUB, cols)] * sides + [(SUB, LANES)] * (2 * sides)
    return pl.pallas_call(
        functools.partial(edge_kernel, sides),
        in_specs=[anywhere] * 6,
        out_specs=[vmem] * len(shapes),
        out_shape=[jax.ShapeDtypeStruct(x, jnp.float32) for x in shapes],
        scratch_shapes=[pltpu.VMEM((*x.shape[:-2], SUB, cols), x.dtype) for x in ins] * sides
        + [pltpu.VMEM((*x.shape[:-1], LANES), x.dtype) for x in ins] * 2
        + [pltpu.VMEM(cells.shape, cells.dtype), pltpu.SemaphoreType.DMA((sides + 2, 6))],
        compiler_params=pltpu.CompilerParams(vmem_limit_bytes=58 * 1024 * 1024),
        name="edges",
    )(cells, *ins)


def diagonal(x, first_row, first_col):
    count = lax.axis_size("col")
    perm = [
        (a * count + c, b * count + d)
        for a, b in pairs(lax.axis_size("row"), first_row)
        for c, d in pairs(count, first_col)
    ]
    return lax.ppermute(x, ("row", "col"), perm)


def rim_kernel(sides, events, steps, rows, *refs):
    rims_in = refs[:sides]
    rim_top, rim_bottom = refs[sides:]
    cols = rim_top.shape[-1]
    even_row = lax.axis_index("row") % 2 == 0
    sub = lax.broadcasted_iota(jnp.int32, (SUB, cols), 0)
    slots, _ = plan(events, steps)
    base = events * (steps + 1) + 3
    nothing = jnp.zeros((SUB, cols), jnp.float32)

    def field(ref, n, slot):
        x = nothing
        for i in range(slot // SUB, (slot + n - 1) // SUB + 1):
            low, high = slot - i * SUB, slot + n - i * SUB
            y = ref[i * SUB : (i + 1) * SUB]
            y = pltpu.roll(y, -low % SUB, 0) if low % SUB else y
            x = jnp.where((sub >= -low) & (sub < min(n, SUB - low)) & (sub >= max(0, -low)), y, x)
        return x

    for f in range(base):
        n, slot = slots[f]
        x = field(rims_in[0], n, slot)
        y = field(rims_in[1], n, slot) if sides > 1 else nothing
        rim_bottom[f] = jnp.where(even_row, x, y)
        rim_top[f] = pltpu.roll(jnp.where(even_row, y, x), SUB - n, 0)
    for e in range(events):
        slot = slots[base + e][1]
        for k in range(2):
            lower = even_row if k == 0 else jnp.logical_not(even_row)
            if k < sides:
                g = rims_in[k][slot : slot + 1].astype(jnp.int32)
                row = g // cols - jnp.where(lower, 0, rows - SUB)
                hits = jnp.concatenate(tally_of(row, g % cols, SUB, cols), axis=1)
            else:
                hits = nothing
            if k == 0:
                first = hits
        rim_bottom[base + e] = jnp.where(even_row, first, hits)
        rim_top[base + e] = jnp.where(even_row, hits, first)


def row_rims(rims, events, steps, rows):
    vmem = pl.BlockSpec(memory_space=pltpu.VMEM)
    rim = jax.ShapeDtypeStruct((events * (steps + 2) + 3, SUB, rims[0].shape[-1]), jnp.float32)
    return pl.pallas_call(
        functools.partial(rim_kernel, len(rims), events, steps, rows),
        in_specs=[vmem] * len(rims),
        out_specs=[vmem] * 2,
        out_shape=[rim] * 2,
        compiler_params=pltpu.CompilerParams(vmem_limit_bytes=4 * 1024 * 1024),
        name="row_rims",
    )(*rims)


def up(x):
    return pltpu.roll(x, SUB - 1, 0)


def down(x):
    return pltpu.roll(x, 1, 0)


def sublanes():
    return lax.broadcasted_iota(jnp.int32, (SUB, LANES), 0)


def to_right(x, nxt):
    last = lanes_of((SUB, LANES)) == LANES - 1
    return jnp.where(last, pltpu.roll(nxt, LANES - 1, 1), pltpu.roll(x, LANES - 1, 1))


def right(xs):
    last = lanes_of((SUB, LANES)) == LANES - 1
    r = [pltpu.roll(x, LANES - 1, 1) for x in xs]
    return [jnp.where(last, r[(j + 1) % len(xs)], r[j]) for j in range(len(xs))]


def left(xs):
    first = lanes_of((SUB, LANES)) == 0
    r = [pltpu.roll(x, 1, 1) for x in xs]
    return [jnp.where(first, r[j - 1], r[j]) for j in range(len(xs))]


def at_lanes(j):
    return slice(j * LANES, (j + 1) * LANES)


def get(ref, *at):
    return [ref[(*at, slice(None), at_lanes(j))] for j in range(ref.shape[-1] // LANES)]


def put(xs, ref, *at):
    for j, x in enumerate(xs):
        ref[(*at, slice(None), at_lanes(j))] = x


def followers(first, below, above):
    last = sublanes() == SUB - 1
    f, b, a = up(first), up(below), up(above)
    return jnp.where(last, b, f), b, jnp.where(last, f, a)


def follow(ref, *at):
    deep = ref.shape[-3] - 5
    sets = zip(get(ref, *at, 0), get(ref, *at, deep), get(ref, *at, deep + 1))
    for k, xs in enumerate(zip(*[followers(*x) for x in sets])):
        put(xs, ref, *at, deep + 2 + k)


def preceding(ref, deep, passed):
    first = sublanes() == 0
    last, below, above = get(ref, deep), get(ref, deep + 1), get(ref, deep + 2)
    return (
        [jnp.where(first, down(a), down(l)) for a, l in zip(above, last)],
        [jnp.where(first, down(l), down(b)) - l for b, l in zip(below, last)],
        [down(a) - b for a, b in zip(above, below)],
    )


def face(h, h_k, sb, cond, inv):
    hs = h + h_k
    s = (h_k - h) + sb
    x = s * s + slope_floor
    y = lax.rsqrt(x)
    p = cond * (jnp.exp2((2.0 / 3.0 / LN2) * jnp.log(hs)) * (y * lax.rsqrt(y)))
    ps = p * s
    t = p * hs
    A = (5.0 / 3.0) * ps
    B = t * (0.5 + (0.5 * slope_floor) * (y * y))
    return A - B, A + B, (ps * hs) * inv


scale = time_step * 2.0 ** (-2.0 / 3.0)


def inner_kernel(
    depth, wet, bed, rough, direction,
    prim, a_x, b_x, c_x, a_y, b_y, c_y, q_x, q_y,
    nat, sb_x, sb_y, inv_x, inv_y, cond_x, cond_y,
):
    events, steps, rows, cols = depth.shape
    deep, count = rows // SUB, cols // LANES
    fields = [bed, rough, direction] + [wet.at[e] for e in range(events)]
    fields += [depth.at[e, t] for e in range(events) for t in range(steps)]
    for k, x in enumerate(fields):
        for j in range(count):
            nat[k, j] = x[:, at_lanes(j)].astype(jnp.float32)

    @pl.loop(0, deep, unroll=4)
    def _(i):
        spread = lambda k: [nat[k, j, pl.ds(i, SUB, stride=deep), :] for j in range(count)]
        m = [jnp.exp(x) for x in spread(1)]
        put(spread(0), prim, 0, i)
        put(m, prim, 1, i)
        put([x * y for x, y in zip(m, spread(2))], prim, 2, i)
        for k in range(3, 3 + events * (steps + 1)):
            put(spread(k), prim, k, i)

    for k in range(3 + events * (steps + 1)):
        put([up(x) for x in get(prim, k, 0)], prim, k, deep)

    @pl.loop(0, deep, unroll=4)
    def _(i):
        b, m, q = (get(prim, k, i) for k in range(3))
        put([y - x for x, y in zip(b, right(b))], sb_x, i)
        put([y - x for x, y in zip(b, get(prim, 0, i + 1))], sb_y, i)
        ix = [1.0 / (x + y) for x, y in zip(m, right(m))]
        iy = [1.0 / (x + y) for x, y in zip(m, get(prim, 1, i + 1))]
        put([-x for x in ix], inv_x, i)
        put([-x for x in iy], inv_y, i)
        put([x + y for x, y in zip(q, right(q))], q_x, i)
        put([x + y for x, y in zip(q, get(prim, 2, i + 1))], q_y, i)
        for e in range(events):
            w = get(prim, 3 + e, i)
            put([(scale * z) * (x * y) for x, y, z in zip(w, right(w), ix)], cond_x, e, i)
            put([(scale * z) * (x * y) for x, y, z in zip(w, get(prim, 3 + e, i + 1), iy)], cond_y, e, i)

    @pl.loop(0, events)
    def _(e):
        for t in range(steps):

            @pl.loop(0, deep, unroll=4)
            def _(i):
                k = 3 + events + e * steps + t
                h = get(prim, k, i)
                h_r, h_d = right(h), get(prim, k, i + 1)
                for j in range(count):
                    J = at_lanes(j)
                    for h_k, sb, cond, inv, a, b, c in (
                        (h_r, sb_x, cond_x, inv_x, a_x, b_x, c_x),
                        (h_d, sb_y, cond_y, inv_y, a_y, b_y, c_y),
                    ):
                        A, B, C = face(h[j], h_k[j], sb[i, :, J], cond[e, i, :, J], inv[i, :, J])
                        c[e, t, i, :, J] = C
                        if t:
                            a[e, t - 1, i, :, J] = A
                            b[e, t - 1, i, :, J] = B


def inner(depth, wet, bed, rough, direction):
    events, steps, rows, cols = depth.shape
    deep = rows // SUB
    shape = lambda *lead: (*lead, deep, SUB, cols)
    vm = lambda *lead: pltpu.VMEM(shape(*lead), jnp.float32)
    out = lambda *lead: jax.ShapeDtypeStruct(shape(*lead), jnp.float32)
    vmem = pl.BlockSpec(memory_space=pltpu.VMEM)
    fields = 3 + events * (steps + 1)
    return pl.pallas_call(
        inner_kernel,
        in_specs=[vmem] * 5,
        out_specs=[vmem] * 9,
        out_shape=[
            jax.ShapeDtypeStruct((fields, deep + 1, SUB, cols), jnp.float32),
            *[out(events, steps - 1), out(events, steps - 1), out(events, steps)] * 2,
            out(),
            out(),
        ],
        scratch_shapes=[
            pltpu.VMEM((fields, cols // LANES, rows, LANES), jnp.float32),
            *[vm()] * 4,
            *[vm(events)] * 2,
        ],
        compiler_params=pltpu.CompilerParams(vmem_limit_bytes=12 * 1024 * 1024),
        cost_estimate=pl.CostEstimate(flops=100000000, bytes_accessed=16000000, transcendentals=0),
        name="inner",
    )(depth, wet, bed, rough, direction)


def tangent_kernel(
    prim, cnt, ia_x, ib_x, ic_x, ia_y, ib_y, ic_y, iq_x, iq_y, rim_top, rim_bottom, side_a, side_b,
    corner_aa, corner_ab, corner_ba, corner_bb, curve_ref, source, a_x, b_x, c_x, a_y, b_y, c_y,
    nat, ext, xcnt, sb_x, sb_y, q_x, q_y, inv_x, inv_y, cond_x, cond_y, tan_a, tan_b, flow,
):
    events, steps, deep, _, cols = ic_x.shape
    rows, tiles = deep * SUB, cols // LANES
    count, tall = tiles + 1, rows + 2 * SUB
    even_col = lax.axis_index("col") % 2 == 0
    lane_t = lanes_of((tall, LANES))
    even_row = lax.axis_index("row") % 2 == 0

    def whole_side(side, corner_a, corner_b):
        above = jnp.where(even_row, corner_b[...], corner_a[...])
        below = jnp.where(even_row, corner_a[...], corner_b[...])
        return jnp.concatenate([above, side[...], below], axis=0)

    full_a, full_b = whole_side(side_a, corner_aa, corner_ba), whole_side(side_b, corner_ab, corner_bb)
    right_rim = jnp.where(even_col, full_a, full_b)
    left_rim = jnp.where(even_col, full_b, full_a)
    J = [at_lanes(j) for j in range(count)]
    zero = jnp.zeros((SUB, LANES), jnp.float32)
    below, above = deep, deep + 1
    fields = prim.shape[0]

    place_in = [events * (steps + 1) + k for k in range(3)]
    place_in += [events * steps + e for e in range(events)]
    place_in += [e * steps + t for e in range(events) for t in range(steps)]
    place_in += [events * (steps + 1) + 3 + e for e in range(events)]
    for k, f in enumerate(place_in):
        place = f * REACH
        r = pltpu.roll(right_rim, (LANES - place) % LANES, 1) if place else right_rim
        l = pltpu.roll(left_rim, (LANES - REACH - place) % LANES, 1)
        x = jnp.where(lane_t < REACH, r, jnp.where(lane_t >= LANES - REACH, l, 0.0))
        if k == 1:
            m_side = x = jnp.exp(x)
        if k == 2:
            x = m_side * x
        nat[k] = x
        to, n = (ext, k) if k < fields else (xcnt, k - fields)
        for i in range(deep):
            to[n, i, :, J[tiles]] = nat[k, pl.ds(SUB + i, SUB, stride=deep), :]
        for i, rim, at in ((below, rim_bottom, SUB + rows), (above, rim_top, 0)):
            xs = get(rim, f)
            if k == 1:
                xs = [jnp.exp(x) for x in xs]
            if k == 2:
                xs = [x * y for x, y in zip(xs, get(ext, 1, i))]
            put(xs, to, n, i)
            to[n, i, :, J[tiles]] = nat[k, at : at + SUB, :]

    def value(k, i, j):
        return ext[k, i, :, J[j]] if j == tiles or (isinstance(i, int) and i >= deep) else prim[k, i, :, J[j]]

    def next_rows(k, j):
        return followers(value(k, 0, j), value(k, below, j), value(k, above, j))

    for k in range(fields):
        ext[k, deep + 2, :, J[tiles]] = next_rows(k, tiles)[0]

    def derive(i, j, along, k_of):
        sb, inv, q, cond = (sb_x, inv_x, q_x, cond_x) if along else (sb_y, inv_y, q_y, cond_y)
        x, y = k_of(0)
        sb[i, :, J[j]] = y - x
        x, y = k_of(1)
        z = 1.0 / (x + y)
        inv[i, :, J[j]] = -z
        x, y = k_of(2)
        q[i, :, J[j]] = x + y
        for e in range(events):
            x, y = k_of(3 + e)
            cond[e, i, :, J[j]] = (scale * z) * (x * y)

    def across(i, j):
        return lambda k: (value(k, i, j), to_right(value(k, i, j), value(k, i, (j + 1) % count)))

    @pl.loop(0, deep, unroll=4)
    def _(i):
        for j in (tiles - 1, tiles):
            derive(i, j, True, across(i, j))
        n = jnp.where(i == deep - 1, deep + 2, i + 1)
        derive(i, tiles, False, lambda k: (value(k, i, tiles), ext[k, n, :, J[tiles]]))

    for i in (below, above):
        for j in range(count):
            derive(i, j, True, across(i, j))
    for n, i in enumerate((deep - 1, below, above)):
        for j in range(tiles if n == 0 else count):
            derive(i, j, False, lambda k: (value(k, i, j), next_rows(k, j)[n]))

    curve_ref[...] = jnp.zeros(curve_ref.shape, jnp.float32)
    put([zero] * count, flow, 0)

    @pl.loop(0, events)
    def _(e):
        for t in range(steps):
            old, new = (tan_a, tan_b) if t % 2 else (tan_b, tan_a)
            k = 3 + events + e * steps + t

            def row(i):
                static = isinstance(i, int)
                rim = static and i >= deep
                nxt = i + 3 if static and i >= deep - 1 else i + 1
                if t:
                    d = get(old, i)
                    d_r, d_d = right(d), get(old, nxt)
                fx, fy = [], []
                here = lambda j: ext[k, i, :, J[j]] if rim or j == tiles else prim[k, i, :, J[j]]
                for j in range(count):
                    inside = not rim and j < tiles - 1
                    if inside:
                        A, B = (ia_x[e, t - 1, i, :, J[j]], ib_x[e, t - 1, i, :, J[j]]) if t else (None, None)
                        C = ic_x[e, t, i, :, J[j]]
                        f = C * iq_x[i, :, J[j]]
                    else:
                        h = here(j)
                        A, B, C = face(
                            h, to_right(h, here((j + 1) % count)),
                            sb_x[i, :, J[j]], cond_x[e, i, :, J[j]], inv_x[i, :, J[j]],
                        )
                        f = C * q_x[i, :, J[j]]
                    c_x[e, t, i, :, J[j]] = C
                    if t:
                        a_x[e, t - 1, i, :, J[j]] = A
                        b_x[e, t - 1, i, :, J[j]] = B
                        f += A * d[j] + B * d_r[j]
                    fx.append(f)
                    inside = not (static and i >= deep - 1) and j < tiles
                    if inside:
                        A, B = (ia_y[e, t - 1, i, :, J[j]], ib_y[e, t - 1, i, :, J[j]]) if t else (None, None)
                        C = ic_y[e, t, i, :, J[j]]
                        f = C * iq_y[i, :, J[j]]
                    else:
                        h = here(j)
                        if static and i >= deep - 1:
                            first = ext[k, 0, :, J[j]] if j == tiles else prim[k, 0, :, J[j]]
                            h_d = followers(first, ext[k, below, :, J[j]], ext[k, above, :, J[j]])[i - deep + 1]
                        else:
                            h_d = ext[k, i + 1, :, J[j]]
                        A, B, C = face(h, h_d, sb_y[i, :, J[j]], cond_y[e, i, :, J[j]], inv_y[i, :, J[j]])
                        f = C * q_y[i, :, J[j]]
                    c_y[e, t, i, :, J[j]] = C
                    if t:
                        a_y[e, t - 1, i, :, J[j]] = A
                        b_y[e, t - 1, i, :, J[j]] = B
                        f += A * d[j] + B * d_d[j]
                    fy.append(f)
                put(fy, flow, i + 1)
                before = get(flow, i)
                fl = left(fx)
                for j in range(count):
                    r = (fx[j] - fl[j]) + (fy[j] - before[j])
                    new[i, :, J[j]] = d[j] + r if t else r

            main = deep - 2
            pl.loop(0, main, unroll=3 if main % 3 == 0 else 1)(row)
            for i in range(main, deep + 2):
                row(i)
            for i, lack in zip((0, below, above), preceding(flow, deep, zero)):
                put([x - y for x, y in zip(get(new, i), lack)], new, i)
            follow(new)

        old = tan_a if steps % 2 else tan_b
        total = zero
        for i in range(deep + 2):
            for j in range(count):
                own = i < deep and j < tiles
                n = cnt[e, j, pl.ds(i, SUB, stride=deep), :] if own else xcnt[e, i, :, J[j]]
                r = old[i, :, J[j]]
                s = (gauge_weight * n) * r
                source[e, i, :, J[j]] = s
                if own:
                    total += s * r
        curve_ref[...] += total
        follow(source, e)


def tangents(prim, cnt, *more_inputs):
    fields, _, _, cols = prim.shape
    events, deep = cnt.shape[0], prim.shape[1] - 1
    steps = more_inputs[2].shape[1]
    wide = cols + LANES
    regs = deep + 2
    vm = lambda *lead: pltpu.VMEM((*lead, regs, SUB, wide), jnp.float32)
    more = lambda *lead: pltpu.VMEM((*lead, regs + 3, SUB, wide), jnp.float32)
    out = lambda *lead: jax.ShapeDtypeStruct((*lead, regs, SUB, wide), jnp.float32)
    vmem = pl.BlockSpec(memory_space=pltpu.VMEM)
    return pl.pallas_call(
        tangent_kernel,
        in_specs=[vmem] * (2 + len(more_inputs)),
        out_specs=[vmem] * 8,
        out_shape=[
            jax.ShapeDtypeStruct((SUB, LANES), jnp.float32),
            jax.ShapeDtypeStruct((events, regs + 3, SUB, wide), jnp.float32),
            *[out(events, steps - 1), out(events, steps - 1), out(events, steps)] * 2,
        ],
        scratch_shapes=[
            pltpu.VMEM((fields + events, deep * SUB + 2 * SUB, LANES), jnp.float32),
            more(fields),
            vm(events),
            *[vm()] * 6,
            *[vm(events)] * 2,
            *[more()] * 3,
        ],
        compiler_params=pltpu.CompilerParams(vmem_limit_bytes=16 * 1024 * 1024),
        name="tangents",
    )(prim, cnt, *more_inputs)


def adjoint_kernel(first_event, last_event, m_c, source, a_x, b_x, c_x, a_y, b_y, c_y, *refs):
    sums = () if first_event else refs[:2]
    outs = refs[len(sums) : len(sums) + (1 if last_event else 2)]
    nat, adj_a, adj_b, flow, *own = refs[len(sums) + len(outs) :]
    g_x, g_y = own if last_event else outs
    steps, regs, _, wide = c_x.shape
    deep = regs - 2
    count = wide // LANES
    J = [at_lanes(j) for j in range(count)]
    zero = jnp.zeros((SUB, LANES), jnp.float32)
    put([zero] * count, flow, 0)

    for t in range(steps - 1, -1, -1):
        old, new = (adj_a, adj_b) if t % 2 else (adj_b, adj_a)
        if t == steps - 1:
            old = source
            base_x, base_y = sums if sums else (None, None)
        else:
            base_x, base_y = g_x, g_y

        @pl.loop(0, regs, unroll=5 if regs % 5 == 0 else 1)
        def _(i):
            l = get(old, i)
            l_r, l_d = right(l), get(old, jnp.where(i < deep - 1, i + 1, i + 3))
            acc, kx, ky = [], [], []
            for j in range(count):
                p = l[j] - l_r[j]
                g = c_x[t, i, :, J[j]] * p
                g_x[i, :, J[j]] = g + base_x[i, :, J[j]] if base_x is not None else g
                if t:
                    a = l[j] + a_x[t - 1, i, :, J[j]] * p
                    kx.append(b_x[t - 1, i, :, J[j]] * p)
                p = l[j] - l_d[j]
                g = c_y[t, i, :, J[j]] * p
                g_y[i, :, J[j]] = g + base_y[i, :, J[j]] if base_y is not None else g
                if t:
                    acc.append(a + a_y[t - 1, i, :, J[j]] * p)
                    ky.append(b_y[t - 1, i, :, J[j]] * p)
            if t:
                put(ky, flow, i + 1)
                before = get(flow, i)
                kl = left(kx)
                for j in range(count):
                    new[i, :, J[j]] = acc[j] + (kl[j] + before[j])

        if t:
            for i, lack in zip((0, deep, deep + 1), preceding(flow, deep, zero)):
                put([x + y for x, y in zip(get(new, i), lack)], new, i)
            follow(new)

    if last_event:
        (grad_ref,) = outs
        tiles = grad_ref.shape[-1] // LANES
        first = sublanes() == 0
        put(
            [jnp.where(first, down(a), down(l)) for a, l in zip(get(g_y, deep + 1), get(g_y, deep - 1))],
            flow,
            0,
        )

        @pl.loop(0, deep, unroll=4)
        def _(i):
            x, y = get(g_x, i), get(g_y, i)
            put(y, flow, i + 1)
            xl, yl = left(x), get(flow, i)
            for j in range(tiles):
                g = m_c[i, :, J[j]] * ((x[j] + xl[j]) + (y[j] + yl[j]))
                nat[j, pl.ds(i, SUB, stride=deep), :] = g

        for j in range(tiles):
            grad_ref[:, J[j]] = nat[j]


def gradient(e, sums, prim, source, *coefficients):
    events, entries, _, wide = source.shape
    cols, regs = prim.shape[-1], entries - 3
    rows = (regs - 2) * SUB
    first, last = e == 0, e == events - 1
    vm = (regs, SUB, wide)
    more = pltpu.VMEM((entries, SUB, wide), jnp.float32)
    own = lambda x: pl.BlockSpec((None, *x.shape[1:]), lambda i: (e,) + (0,) * (x.ndim - 1))
    whole = lambda shape: pl.BlockSpec(shape, lambda i: (0,) * len(shape))
    return pl.pallas_call(
        functools.partial(adjoint_kernel, first, last),
        grid=(1,),
        in_specs=[pl.BlockSpec((None, *prim.shape[1:]), lambda i: (1, 0, 0, 0)), own(source)]
        + [own(x) for x in coefficients]
        + [whole(vm)] * len(sums),
        out_specs=whole((rows, cols)) if last else [whole(vm)] * 2,
        out_shape=jax.ShapeDtypeStruct((rows, cols), jnp.float32)
        if last
        else [jax.ShapeDtypeStruct(vm, jnp.float32)] * 2,
        scratch_shapes=[pltpu.VMEM((cols // LANES, rows, LANES), jnp.float32), more, more, more]
        + [pltpu.VMEM(vm, jnp.float32)] * (2 if last else 0),
        compiler_params=pltpu.CompilerParams(vmem_limit_bytes=16 * 1024 * 1024),
        cost_estimate=pl.CostEstimate(flops=40000000, bytes_accessed=12000000, transcendentals=0),
        name="gradient",
    )(prim, source, *coefficients, *sums)


def hops_over(axis):
    count, hop, out = lax.axis_size(axis), 1, []
    while hop < count:
        out.append((axis, hop))
        hop *= 2
    return out


def from_hop(x, axis, hop):
    return lax.ppermute(x, axis, [(i, i ^ hop) for i in range(lax.axis_size(axis))])


def hop_sum(x, axis, hop):
    return x + from_hop(x, axis, hop)


def finish_kernel(grad, arrived, curve, curve_arrived, hess, total):
    hess[...] = grad[...] + arrived[...]
    total[...] = jnp.sum(curve[...] + curve_arrived[...], keepdims=True)


def finish(grad, arrived, curve, curve_arrived):
    vmem = pl.BlockSpec(memory_space=pltpu.VMEM)
    hess, total = pl.pallas_call(
        finish_kernel,
        in_specs=[vmem] * 4,
        out_specs=[vmem] * 2,
        out_shape=[jax.ShapeDtypeStruct(grad.shape, grad.dtype), jax.ShapeDtypeStruct((1, 1), curve.dtype)],
        compiler_params=pltpu.CompilerParams(vmem_limit_bytes=4 * 1024 * 1024),
        name="finish",
    )(grad, arrived, curve, curve_arrived)
    return (hess, total.reshape(()))


def local(depth, wet, bed, rough, direction, gauge_cells):
    events, steps, rows, cols = depth.shape
    cells = gauge_cells.reshape(events, 1, -1)
    sides = 2 if lax.axis_size("row") > 2 else 1
    counts, send_a, send_b, *more = edges_and_gauges(cells, depth, wet, bed, rough, direction)
    rims = [exchange(x, "row", k) for k, x in enumerate(more[:sides])]
    side_a = exchange(send_a, "col", 0)
    side_b = exchange(send_b, "col", 1)
    corners = [diagonal(x, k // 2, k % 2) for k, x in enumerate(more[sides:])]
    block = inner(depth, wet, bed, rough, direction)
    rims, side_a, side_b, corners, block = lax.optimization_barrier((rims, side_a, side_b, corners, block))
    if sides == 1:
        corners = corners + [jnp.zeros_like(x) for x in corners]
    rim_top, rim_bottom = row_rims(rims, events, steps, rows)
    curve, *coefficients = tangents(block[0], counts, *block[1:], rim_top, rim_bottom, side_a, side_b, *corners)
    hops = hops_over("event") + hops_over("row") + hops_over("col")
    sums = ()
    for e in range(events):
        sums = gradient(e, sums, block[0], *coefficients)
        if hops:
            curve = hop_sum(curve, *hops.pop(0))
            sums, curve = lax.optimization_barrier((sums, curve))
    grad, arrived = sums, None
    for axis, hop in hops_over("event"):
        if arrived is not None:
            grad = grad + arrived
            if hops:
                curve = hop_sum(curve, *hops.pop(0))
                grad, curve = lax.optimization_barrier((grad, curve))
        arrived = from_hop(grad, axis, hop)
    while len(hops) > 1:
        curve = hop_sum(curve, *hops.pop(0))
    return finish(grad, arrived, curve, from_hop(curve, *hops[0]))


def solution(mesh):
    placed = (
        P("event", None, "row", "col"),
        P("event", "row", "col"),
        P("row", "col"),
        P("row", "col"),
        P("row", "col"),
        P("event", "row", "col", None),
    )
    return jax.shard_map(
        local, mesh=mesh, in_specs=placed, out_specs=(P("row", "col"), P()), check_vma=False
    )
```

```python
import functools

import jax
import jax.numpy as jnp
from jax import lax
from jax.experimental import pallas as pl
from jax.experimental.pallas import tpu as pltpu
from jax.sharding import PartitionSpec as P

time_step = 0.035
slope_floor = 0.01
gauge_weight = 100.0
REACH = 6
LANES = 128
LN2 = 0.6931471805599453
SUB = 8


def pairs(count, first):
    out = []
    for i in range(first, count - 1, 2):
        out += [(i, i + 1), (i + 1, i)]
    return out


def exchange(x, axis, first):
    perm = pairs(lax.axis_size(axis), first)
    return lax.ppermute(x, axis, perm) if perm else None


def lanes_of(shape):
    return lax.broadcasted_iota(jnp.int32, shape, 1)


def plan(events, steps):
    out, slot = [], 0
    for n in [REACH - t for _ in range(events) for t in range(steps)] + [REACH] * (events + 3) + [REACH // 2] * events:
        out.append((n, slot))
        slot += n
    return out, -(-slot // SUB)


def one_hot(hit):
    return jnp.where(hit, 1.0, 0.0).astype(jnp.bfloat16)


def tally_of(row, col, rows, cols):
    gauges = row.shape[-1]
    tall = rows * (cols // 256)
    inside = (row >= 0) & (row < rows)
    high = jnp.where(inside, (col // 256) * rows + row, -1)
    hits = lax.dot_general(
        one_hot(lax.broadcasted_iota(jnp.int32, (tall, gauges), 0) == high),
        one_hot(lax.broadcasted_iota(jnp.int32, (256, gauges), 0) == col % 256),
        (((1,), (1,)), ((), ())),
        preferred_element_type=jnp.float32,
    )
    return [hits[b * rows : (b + 1) * rows] for b in range(cols // 256)]


def edge_kernel(sides, *refs):
    ins, outs, rest = refs[1:6], refs[6 : 9 + 3 * sides], refs[9 + 3 * sides :]
    cnt, pay_a, pay_b, *more = outs
    pays, corners = more[:sides], more[sides:]
    cells, sems = rest[-2:]
    events, steps, rows, cols = ins[0].shape
    even = lax.axis_index("row") % 2 == 0
    even_col = lax.axis_index("col") % 2 == 0
    slots, count = plan(events, steps)
    sub = lax.broadcasted_iota(jnp.int32, (SUB, cols), 0)
    copies = [pltpu.make_async_copy(refs[0], cells, sems.at[0, 5])]
    edges = []
    for k in range(sides):
        sends_last = even if k == 0 else jnp.logical_not(even)
        edge = pl.multiple_of(jnp.where(sends_last, rows - SUB, 0), SUB)
        edges.append((sends_last, edge))
        for i, x in enumerate(ins):
            lead = (slice(None),) * (len(x.shape) - 2)
            at = x.at[(*lead, pl.ds(edge, SUB), slice(None))]
            copies.append(pltpu.make_async_copy(at, rest[5 * k + i], sems.at[k, i]))
    columns = (rest[5 * sides : 5 * sides + 5], rest[5 * sides + 5 : 5 * sides + 10])
    for k in range(2):
        for i, x in enumerate(ins):
            lead = (slice(None),) * (len(x.shape) - 1)
            at = x.at[(*lead, slice(0, LANES) if k == 0 else slice(cols - LANES, cols))]
            copies.append(pltpu.make_async_copy(at, columns[k][i], sems.at[sides + k, i]))
    for copy in copies:
        copy.start()
    copies[0].wait()
    for e in range(events):
        g = cells[e]
        for b, x in enumerate(tally_of(g // cols, g % cols, rows, cols)):
            for j in range(256 // LANES):
                cnt[e, b * (256 // LANES) + j] = x[:, j * LANES : (j + 1) * LANES]
    for copy in copies[1:]:
        copy.wait()

    for k, pay in enumerate(pays):
        d, w, b, r, v = rest[5 * k : 5 * k + 5]
        fields = [d[e, t] for e in range(events) for t in range(steps)]
        fields += [w[e].astype(jnp.float32) for e in range(events)] + [b[...], r[...], v[...]]
        fields += [
            jnp.concatenate([cnt[e, j, pl.ds(edges[k][1], SUB), :] for j in range(cols // LANES)], axis=1)
            for e in range(events)
        ]
        tiles = [jnp.zeros((SUB, cols), jnp.float32)] * count
        for x, (n, slot) in zip(fields, slots):
            if 1 < n < SUB:
                x = jnp.where(edges[k][0], pltpu.roll(x, n, 0), x)
            for i in range(slot // SUB, (slot + n - 1) // SUB + 1):
                low, high = slot - i * SUB, slot + n - i * SUB
                y = pltpu.roll(x, low % SUB, 0) if low % SUB else x
                tiles[i] = jnp.where((sub >= low) & (sub < high), y, tiles[i])
        for i in range(count):
            pay[i * SUB : (i + 1) * SUB] = tiles[i]

    lane = lanes_of((rows, LANES))
    packs = []
    for side in range(2):
        d, w, b, r, v = columns[side]
        pack = jnp.zeros((rows, LANES), jnp.float32)
        xs = [d[e, t] for e in range(events) for t in range(steps)]
        xs += [w[e].astype(jnp.float32) for e in range(events)]
        xs += [b[...], r[...], v[...]]
        xs += [cnt[e, 0 if side == 0 else cols // LANES - 1] for e in range(events)]
        for f, x in enumerate(xs):
            place = f * REACH
            shift = (place + REACH if side == 1 else place) % LANES
            if shift:
                x = pltpu.roll(x, shift, 1)
            pack = jnp.where((lane >= place) & (lane < place + REACH), x, pack)
        packs.append(pack)
    pay_a[...] = jnp.where(even_col, packs[1], packs[0])
    pay_b[...] = jnp.where(even_col, packs[0], packs[1])
    for k in range(sides):
        corners[2 * k][...] = pay_a[pl.ds(edges[k][1], SUB), :]
        corners[2 * k + 1][...] = pay_b[pl.ds(edges[k][1], SUB), :]


def edges_and_gauges(cells, depth, wet, bed, rough, direction):
    events, steps, rows, cols = depth.shape
    sides = 2 if lax.axis_size("row") > 2 else 1
    _, count = plan(events, steps)
    vmem, anywhere = pl.BlockSpec(memory_space=pltpu.VMEM), pl.BlockSpec(memory_space=pl.ANY)
    ins = (depth, wet, bed, rough, direction)
    shapes = [(events, cols // LANES, rows, LANES)] + [(rows, LANES)] * 2
    shapes += [(count * SUB, cols)] * sides + [(SUB, LANES)] * (2 * sides)
    return pl.pallas_call(
        functools.partial(edge_kernel, sides),
        in_specs=[anywhere] * 6,
        out_specs=[vmem] * len(shapes),
        out_shape=[jax.ShapeDtypeStruct(x, jnp.float32) for x in shapes],
        scratch_shapes=[pltpu.VMEM((*x.shape[:-2], SUB, cols), x.dtype) for x in ins] * sides
        + [pltpu.VMEM((*x.shape[:-1], LANES), x.dtype) for x in ins] * 2
        + [pltpu.VMEM(cells.shape, cells.dtype), pltpu.SemaphoreType.DMA((sides + 2, 6))],
        compiler_params=pltpu.CompilerParams(vmem_limit_bytes=58 * 1024 * 1024),
        name="edges",
    )(cells, *ins)


def diagonal(x, first_row, first_col):
    count = lax.axis_size("col")
    perm = [
        (a * count + c, b * count + d)
        for a, b in pairs(lax.axis_size("row"), first_row)
        for c, d in pairs(count, first_col)
    ]
    return lax.ppermute(x, ("row", "col"), perm)


def rim_kernel(sides, events, steps, *refs):
    rims_in = refs[:sides]
    rim_top, rim_bottom = refs[sides:]
    cols = rim_top.shape[-1]
    even_row = lax.axis_index("row") % 2 == 0
    sub = lax.broadcasted_iota(jnp.int32, (SUB, cols), 0)
    slots, _ = plan(events, steps)
    nothing = jnp.zeros((SUB, cols), jnp.float32)

    def field(ref, n, slot):
        x = nothing
        for i in range(slot // SUB, (slot + n - 1) // SUB + 1):
            low, high = slot - i * SUB, slot + n - i * SUB
            y = ref[i * SUB : (i + 1) * SUB]
            y = pltpu.roll(y, -low % SUB, 0) if low % SUB else y
            x = jnp.where((sub >= -low) & (sub < min(n, SUB - low)) & (sub >= max(0, -low)), y, x)
        return x

    for f, (n, slot) in enumerate(slots):
        x = field(rims_in[0], n, slot)
        y = field(rims_in[1], n, slot) if sides > 1 else nothing
        rim_bottom[f] = jnp.where(even_row, x, y)
        rim_top[f] = pltpu.roll(jnp.where(even_row, y, x), SUB - n, 0)


def row_rims(rims, events, steps):
    vmem = pl.BlockSpec(memory_space=pltpu.VMEM)
    rim = jax.ShapeDtypeStruct((events * (steps + 2) + 3, SUB, rims[0].shape[-1]), jnp.float32)
    return pl.pallas_call(
        functools.partial(rim_kernel, len(rims), events, steps),
        in_specs=[vmem] * len(rims),
        out_specs=[vmem] * 2,
        out_shape=[rim] * 2,
        compiler_params=pltpu.CompilerParams(vmem_limit_bytes=4 * 1024 * 1024),
        name="row_rims",
    )(*rims)


def up(x):
    return pltpu.roll(x, SUB - 1, 0)


def down(x):
    return pltpu.roll(x, 1, 0)


def sublanes():
    return lax.broadcasted_iota(jnp.int32, (SUB, LANES), 0)


def to_right(x, nxt):
    last = lanes_of((SUB, LANES)) == LANES - 1
    return jnp.where(last, pltpu.roll(nxt, LANES - 1, 1), pltpu.roll(x, LANES - 1, 1))


def right(xs):
    last = lanes_of((SUB, LANES)) == LANES - 1
    r = [pltpu.roll(x, LANES - 1, 1) for x in xs]
    return [jnp.where(last, r[(j + 1) % len(xs)], r[j]) for j in range(len(xs))]


def left(xs):
    first = lanes_of((SUB, LANES)) == 0
    r = [pltpu.roll(x, 1, 1) for x in xs]
    return [jnp.where(first, r[j - 1], r[j]) for j in range(len(xs))]


def at_lanes(j):
    return slice(j * LANES, (j + 1) * LANES)


def get(ref, *at):
    return [ref[(*at, slice(None), at_lanes(j))] for j in range(ref.shape[-1] // LANES)]


def put(xs, ref, *at):
    for j, x in enumerate(xs):
        ref[(*at, slice(None), at_lanes(j))] = x


def followers(first, below, above):
    last = sublanes() == SUB - 1
    f, b, a = up(first), up(below), up(above)
    return jnp.where(last, b, f), b, jnp.where(last, f, a)


def follow(ref, *at):
    deep = ref.shape[-3] - 5
    sets = zip(get(ref, *at, 0), get(ref, *at, deep), get(ref, *at, deep + 1))
    for k, xs in enumerate(zip(*[followers(*x) for x in sets])):
        put(xs, ref, *at, deep + 2 + k)


def preceding(ref, deep, passed):
    first = sublanes() == 0
    last, below, above = get(ref, deep), get(ref, deep + 1), get(ref, deep + 2)
    return (
        [jnp.where(first, down(a), down(l)) for a, l in zip(above, last)],
        [jnp.where(first, down(l), down(b)) - l for b, l in zip(below, last)],
        [down(a) - b for a, b in zip(above, below)],
    )


def face(h, h_k, sb, cond, inv):
    hs = h + h_k
    s = (h_k - h) + sb
    x = s * s + slope_floor
    y = lax.rsqrt(x)
    p = cond * (jnp.exp2((2.0 / 3.0 / LN2) * jnp.log(hs)) * (y * lax.rsqrt(y)))
    ps = p * s
    t = p * hs
    A = (5.0 / 3.0) * ps
    B = t * (0.5 + (0.5 * slope_floor) * (y * y))
    return A - B, A + B, (ps * hs) * inv


scale = time_step * 2.0 ** (-2.0 / 3.0)


def inner_kernel(
    depth, wet, bed, rough, direction,
    prim, a_x, b_x, c_x, a_y, b_y, c_y, q_x, q_y,
    nat, sb_x, sb_y, inv_x, inv_y, cond_x, cond_y,
):
    events, steps, rows, cols = depth.shape
    deep, count = rows // SUB, cols // LANES
    fields = [bed, rough, direction] + [wet.at[e] for e in range(events)]
    fields += [depth.at[e, t] for e in range(events) for t in range(steps)]
    for k, x in enumerate(fields):
        for j in range(count):
            nat[k, j] = x[:, at_lanes(j)].astype(jnp.float32)

    @pl.loop(0, deep, unroll=4)
    def _(i):
        spread = lambda k: [nat[k, j, pl.ds(i, SUB, stride=deep), :] for j in range(count)]
        m = [jnp.exp(x) for x in spread(1)]
        put(spread(0), prim, 0, i)
        put(m, prim, 1, i)
        put([x * y for x, y in zip(m, spread(2))], prim, 2, i)
        for k in range(3, 3 + events * (steps + 1)):
            put(spread(k), prim, k, i)

    for k in range(3 + events * (steps + 1)):
        put([up(x) for x in get(prim, k, 0)], prim, k, deep)

    @pl.loop(0, deep, unroll=4)
    def _(i):
        b, m, q = (get(prim, k, i) for k in range(3))
        put([y - x for x, y in zip(b, right(b))], sb_x, i)
        put([y - x for x, y in zip(b, get(prim, 0, i + 1))], sb_y, i)
        ix = [1.0 / (x + y) for x, y in zip(m, right(m))]
        iy = [1.0 / (x + y) for x, y in zip(m, get(prim, 1, i + 1))]
        put([-x for x in ix], inv_x, i)
        put([-x for x in iy], inv_y, i)
        put([x + y for x, y in zip(q, right(q))], q_x, i)
        put([x + y for x, y in zip(q, get(prim, 2, i + 1))], q_y, i)
        for e in range(events):
            w = get(prim, 3 + e, i)
            put([(scale * z) * (x * y) for x, y, z in zip(w, right(w), ix)], cond_x, e, i)
            put([(scale * z) * (x * y) for x, y, z in zip(w, get(prim, 3 + e, i + 1), iy)], cond_y, e, i)

    @pl.loop(0, events)
    def _(e):
        for t in range(steps):

            @pl.loop(0, deep, unroll=deep)
            def _(i):
                k = 3 + events + e * steps + t
                h = get(prim, k, i)
                h_r, h_d = right(h), get(prim, k, i + 1)
                for j in range(count):
                    J = at_lanes(j)
                    for h_k, sb, cond, inv, a, b, c in (
                        (h_r, sb_x, cond_x, inv_x, a_x, b_x, c_x),
                        (h_d, sb_y, cond_y, inv_y, a_y, b_y, c_y),
                    ):
                        A, B, C = face(h[j], h_k[j], sb[i, :, J], cond[e, i, :, J], inv[i, :, J])
                        c[e, t, i, :, J] = C
                        if t:
                            a[e, t - 1, i, :, J] = A
                            b[e, t - 1, i, :, J] = B


def inner(depth, wet, bed, rough, direction):
    events, steps, rows, cols = depth.shape
    deep = rows // SUB
    shape = lambda *lead: (*lead, deep, SUB, cols)
    vm = lambda *lead: pltpu.VMEM(shape(*lead), jnp.float32)
    out = lambda *lead: jax.ShapeDtypeStruct(shape(*lead), jnp.float32)
    vmem = pl.BlockSpec(memory_space=pltpu.VMEM)
    fields = 3 + events * (steps + 1)
    return pl.pallas_call(
        inner_kernel,
        in_specs=[vmem] * 5,
        out_specs=[vmem] * 9,
        out_shape=[
            jax.ShapeDtypeStruct((fields, deep + 1, SUB, cols), jnp.float32),
            *[out(events, steps - 1), out(events, steps - 1), out(events, steps)] * 2,
            out(),
            out(),
        ],
        scratch_shapes=[
            pltpu.VMEM((fields, cols // LANES, rows, LANES), jnp.float32),
            *[vm()] * 4,
            *[vm(events)] * 2,
        ],
        compiler_params=pltpu.CompilerParams(vmem_limit_bytes=12 * 1024 * 1024),
        cost_estimate=pl.CostEstimate(flops=100000000, bytes_accessed=16000000, transcendentals=0),
        name="inner",
    )(depth, wet, bed, rough, direction)


def tangent_kernel(
    prim, cnt, ia_x, ib_x, ic_x, ia_y, ib_y, ic_y, iq_x, iq_y, rim_top, rim_bottom, side_a, side_b,
    corner_aa, corner_ab, corner_ba, corner_bb, curve_ref, source, a_x, b_x, c_x, a_y, b_y, c_y,
    nat, ext, xcnt, sb_x, sb_y, q_x, q_y, inv_x, inv_y, cond_x, cond_y, tan_a, tan_b, flow,
):
    events, steps, deep, _, cols = ic_x.shape
    rows, tiles = deep * SUB, cols // LANES
    count, tall = tiles + 1, rows + 2 * SUB
    even_col = lax.axis_index("col") % 2 == 0
    lane_t = lanes_of((tall, LANES))
    even_row = lax.axis_index("row") % 2 == 0

    def whole_side(side, corner_a, corner_b):
        above = jnp.where(even_row, corner_b[...], corner_a[...])
        below = jnp.where(even_row, corner_a[...], corner_b[...])
        return jnp.concatenate([above, side[...], below], axis=0)

    full_a, full_b = whole_side(side_a, corner_aa, corner_ba), whole_side(side_b, corner_ab, corner_bb)
    right_rim = jnp.where(even_col, full_a, full_b)
    left_rim = jnp.where(even_col, full_b, full_a)
    J = [at_lanes(j) for j in range(count)]
    zero = jnp.zeros((SUB, LANES), jnp.float32)
    below, above = deep, deep + 1
    fields = prim.shape[0]

    place_in = [events * (steps + 1) + k for k in range(3)]
    place_in += [events * steps + e for e in range(events)]
    place_in += [e * steps + t for e in range(events) for t in range(steps)]
    place_in += [events * (steps + 1) + 3 + e for e in range(events)]
    for k, f in enumerate(place_in):
        place = f * REACH
        r = pltpu.roll(right_rim, (LANES - place) % LANES, 1) if place else right_rim
        l = pltpu.roll(left_rim, (LANES - REACH - place) % LANES, 1)
        x = jnp.where(lane_t < REACH, r, jnp.where(lane_t >= LANES - REACH, l, 0.0))
        if k == 1:
            m_side = x = jnp.exp(x)
        if k == 2:
            x = m_side * x
        nat[k] = x
        to, n = (ext, k) if k < fields else (xcnt, k - fields)
        for i in range(deep):
            to[n, i, :, J[tiles]] = nat[k, pl.ds(SUB + i, SUB, stride=deep), :]
        for i, rim, at in ((below, rim_bottom, SUB + rows), (above, rim_top, 0)):
            xs = get(rim, f)
            if k == 1:
                xs = [jnp.exp(x) for x in xs]
            if k == 2:
                xs = [x * y for x, y in zip(xs, get(ext, 1, i))]
            put(xs, to, n, i)
            to[n, i, :, J[tiles]] = nat[k, at : at + SUB, :]

    def value(k, i, j):
        return ext[k, i, :, J[j]] if j == tiles or (isinstance(i, int) and i >= deep) else prim[k, i, :, J[j]]

    def next_rows(k, j):
        return followers(value(k, 0, j), value(k, below, j), value(k, above, j))

    for k in range(fields):
        ext[k, deep + 2, :, J[tiles]] = next_rows(k, tiles)[0]

    def derive(i, j, along, k_of):
        sb, inv, q, cond = (sb_x, inv_x, q_x, cond_x) if along else (sb_y, inv_y, q_y, cond_y)
        x, y = k_of(0)
        sb[i, :, J[j]] = y - x
        x, y = k_of(1)
        z = 1.0 / (x + y)
        inv[i, :, J[j]] = -z
        x, y = k_of(2)
        q[i, :, J[j]] = x + y
        for e in range(events):
            x, y = k_of(3 + e)
            cond[e, i, :, J[j]] = (scale * z) * (x * y)

    def across(i, j):
        return lambda k: (value(k, i, j), to_right(value(k, i, j), value(k, i, (j + 1) % count)))

    @pl.loop(0, deep, unroll=4)
    def _(i):
        for j in (tiles - 1, tiles):
            derive(i, j, True, across(i, j))
        n = jnp.where(i == deep - 1, deep + 2, i + 1)
        derive(i, tiles, False, lambda k: (value(k, i, tiles), ext[k, n, :, J[tiles]]))

    for i in (below, above):
        for j in range(count):
            derive(i, j, True, across(i, j))
    for n, i in enumerate((deep - 1, below, above)):
        for j in range(tiles if n == 0 else count):
            derive(i, j, False, lambda k: (value(k, i, j), next_rows(k, j)[n]))

    curve_ref[...] = jnp.zeros(curve_ref.shape, jnp.float32)
    put([zero] * count, flow, 0)

    @pl.loop(0, events)
    def _(e):
        for t in range(steps):
            old, new = (tan_a, tan_b) if t % 2 else (tan_b, tan_a)
            k = 3 + events + e * steps + t

            def row(i):
                static = isinstance(i, int)
                rim = static and i >= deep
                nxt = i + 3 if static and i >= deep - 1 else i + 1
                if t:
                    d = get(old, i)
                    d_r, d_d = right(d), get(old, nxt)
                fx, fy = [], []
                here = lambda j: ext[k, i, :, J[j]] if rim or j == tiles else prim[k, i, :, J[j]]
                for j in range(count):
                    inside = not rim and j < tiles - 1
                    if inside:
                        A, B = (ia_x[e, t - 1, i, :, J[j]], ib_x[e, t - 1, i, :, J[j]]) if t else (None, None)
                        C = ic_x[e, t, i, :, J[j]]
                        f = C * iq_x[i, :, J[j]]
                    else:
                        h = here(j)
                        A, B, C = face(
                            h, to_right(h, here((j + 1) % count)),
                            sb_x[i, :, J[j]], cond_x[e, i, :, J[j]], inv_x[i, :, J[j]],
                        )
                        f = C * q_x[i, :, J[j]]
                    c_x[e, t, i, :, J[j]] = C
                    if t:
                        a_x[e, t - 1, i, :, J[j]] = A
                        b_x[e, t - 1, i, :, J[j]] = B
                        f += A * d[j] + B * d_r[j]
                    fx.append(f)
                    inside = not (static and i >= deep - 1) and j < tiles
                    if inside:
                        A, B = (ia_y[e, t - 1, i, :, J[j]], ib_y[e, t - 1, i, :, J[j]]) if t else (None, None)
                        C = ic_y[e, t, i, :, J[j]]
                        f = C * iq_y[i, :, J[j]]
                    else:
                        h = here(j)
                        if static and i >= deep - 1:
                            first = ext[k, 0, :, J[j]] if j == tiles else prim[k, 0, :, J[j]]
                            h_d = followers(first, ext[k, below, :, J[j]], ext[k, above, :, J[j]])[i - deep + 1]
                        else:
                            h_d = ext[k, i + 1, :, J[j]]
                        A, B, C = face(h, h_d, sb_y[i, :, J[j]], cond_y[e, i, :, J[j]], inv_y[i, :, J[j]])
                        f = C * q_y[i, :, J[j]]
                    c_y[e, t, i, :, J[j]] = C
                    if t:
                        a_y[e, t - 1, i, :, J[j]] = A
                        b_y[e, t - 1, i, :, J[j]] = B
                        f += A * d[j] + B * d_d[j]
                    fy.append(f)
                put(fy, flow, i + 1)
                before = get(flow, i)
                fl = left(fx)
                for j in range(count):
                    r = (fx[j] - fl[j]) + (fy[j] - before[j])
                    new[i, :, J[j]] = d[j] + r if t else r

            main = deep - 2
            pl.loop(0, main, unroll=3 if main % 3 == 0 else 1)(row)
            for i in range(main, deep + 2):
                row(i)
            for i, lack in zip((0, below, above), preceding(flow, deep, zero)):
                put([x - y for x, y in zip(get(new, i), lack)], new, i)
            follow(new)

        old = tan_a if steps % 2 else tan_b
        total = zero
        for i in range(deep + 2):
            for j in range(count):
                own = i < deep and j < tiles
                n = cnt[e, j, pl.ds(i, SUB, stride=deep), :] if own else xcnt[e, i, :, J[j]]
                r = old[i, :, J[j]]
                s = (gauge_weight * n) * r
                source[e, i, :, J[j]] = s
                if own:
                    total += s * r
        curve_ref[...] += total
        follow(source, e)


def tangents(prim, cnt, *more_inputs):
    fields, _, _, cols = prim.shape
    events, deep = cnt.shape[0], prim.shape[1] - 1
    steps = more_inputs[2].shape[1]
    wide = cols + LANES
    regs = deep + 2
    vm = lambda *lead: pltpu.VMEM((*lead, regs, SUB, wide), jnp.float32)
    more = lambda *lead: pltpu.VMEM((*lead, regs + 3, SUB, wide), jnp.float32)
    out = lambda *lead: jax.ShapeDtypeStruct((*lead, regs, SUB, wide), jnp.float32)
    vmem = pl.BlockSpec(memory_space=pltpu.VMEM)
    return pl.pallas_call(
        tangent_kernel,
        in_specs=[vmem] * (2 + len(more_inputs)),
        out_specs=[vmem] * 8,
        out_shape=[
            jax.ShapeDtypeStruct((SUB, LANES), jnp.float32),
            jax.ShapeDtypeStruct((events, regs + 3, SUB, wide), jnp.float32),
            *[out(events, steps - 1), out(events, steps - 1), out(events, steps)] * 2,
        ],
        scratch_shapes=[
            pltpu.VMEM((fields + events, deep * SUB + 2 * SUB, LANES), jnp.float32),
            more(fields),
            vm(events),
            *[vm()] * 6,
            *[vm(events)] * 2,
            *[more()] * 3,
        ],
        compiler_params=pltpu.CompilerParams(vmem_limit_bytes=16 * 1024 * 1024),
        name="tangents",
    )(prim, cnt, *more_inputs)


def adjoint_kernel(first_event, last_event, m_c, source, a_x, b_x, c_x, a_y, b_y, c_y, *refs):
    sums = () if first_event else refs[:2]
    outs = refs[len(sums) : len(sums) + (1 if last_event else 2)]
    nat, adj_a, adj_b, flow, *own = refs[len(sums) + len(outs) :]
    g_x, g_y = own if last_event else outs
    steps, regs, _, wide = c_x.shape
    deep = regs - 2
    count = wide // LANES
    J = [at_lanes(j) for j in range(count)]
    zero = jnp.zeros((SUB, LANES), jnp.float32)
    put([zero] * count, flow, 0)

    for t in range(steps - 1, -1, -1):
        old, new = (adj_a, adj_b) if t % 2 else (adj_b, adj_a)
        if t == steps - 1:
            old = source
            base_x, base_y = sums if sums else (None, None)
        else:
            base_x, base_y = g_x, g_y

        @pl.loop(0, regs, unroll=5 if regs % 5 == 0 else 1)
        def _(i):
            l = get(old, i)
            l_r, l_d = right(l), get(old, jnp.where(i < deep - 1, i + 1, i + 3))
            acc, kx, ky = [], [], []
            for j in range(count):
                p = l[j] - l_r[j]
                g = c_x[t, i, :, J[j]] * p
                g_x[i, :, J[j]] = g + base_x[i, :, J[j]] if base_x is not None else g
                if t:
                    a = l[j] + a_x[t - 1, i, :, J[j]] * p
                    kx.append(b_x[t - 1, i, :, J[j]] * p)
                p = l[j] - l_d[j]
                g = c_y[t, i, :, J[j]] * p
                g_y[i, :, J[j]] = g + base_y[i, :, J[j]] if base_y is not None else g
                if t:
                    acc.append(a + a_y[t - 1, i, :, J[j]] * p)
                    ky.append(b_y[t - 1, i, :, J[j]] * p)
            if t:
                put(ky, flow, i + 1)
                before = get(flow, i)
                kl = left(kx)
                for j in range(count):
                    new[i, :, J[j]] = acc[j] + (kl[j] + before[j])

        if t:
            for i, lack in zip((0, deep, deep + 1), preceding(flow, deep, zero)):
                put([x + y for x, y in zip(get(new, i), lack)], new, i)
            follow(new)

    if last_event:
        (grad_ref,) = outs
        tiles = grad_ref.shape[-1] // LANES
        first = sublanes() == 0
        put(
            [jnp.where(first, down(a), down(l)) for a, l in zip(get(g_y, deep + 1), get(g_y, deep - 1))],
            flow,
            0,
        )

        @pl.loop(0, deep, unroll=4)
        def _(i):
            x, y = get(g_x, i), get(g_y, i)
            put(y, flow, i + 1)
            xl, yl = left(x), get(flow, i)
            for j in range(tiles):
                g = m_c[i, :, J[j]] * ((x[j] + xl[j]) + (y[j] + yl[j]))
                nat[j, pl.ds(i, SUB, stride=deep), :] = g

        for j in range(tiles):
            grad_ref[:, J[j]] = nat[j]


def gradient(e, sums, prim, source, *coefficients):
    events, entries, _, wide = source.shape
    cols, regs = prim.shape[-1], entries - 3
    rows = (regs - 2) * SUB
    first, last = e == 0, e == events - 1
    vm = (regs, SUB, wide)
    more = pltpu.VMEM((entries, SUB, wide), jnp.float32)
    own = lambda x: pl.BlockSpec((None, *x.shape[1:]), lambda i: (e,) + (0,) * (x.ndim - 1))
    whole = lambda shape: pl.BlockSpec(shape, lambda i: (0,) * len(shape))
    return pl.pallas_call(
        functools.partial(adjoint_kernel, first, last),
        grid=(1,),
        in_specs=[pl.BlockSpec((None, *prim.shape[1:]), lambda i: (1, 0, 0, 0)), own(source)]
        + [own(x) for x in coefficients]
        + [whole(vm)] * len(sums),
        out_specs=whole((rows, cols)) if last else [whole(vm)] * 2,
        out_shape=jax.ShapeDtypeStruct((rows, cols), jnp.float32)
        if last
        else [jax.ShapeDtypeStruct(vm, jnp.float32)] * 2,
        scratch_shapes=[pltpu.VMEM((cols // LANES, rows, LANES), jnp.float32), more, more, more]
        + [pltpu.VMEM(vm, jnp.float32)] * (2 if last else 0),
        compiler_params=pltpu.CompilerParams(vmem_limit_bytes=16 * 1024 * 1024),
        cost_estimate=pl.CostEstimate(flops=40000000, bytes_accessed=12000000, transcendentals=0),
        name="gradient",
    )(prim, source, *coefficients, *sums)


def hops_over(axis):
    count, hop, out = lax.axis_size(axis), 1, []
    while hop < count:
        out.append((axis, hop))
        hop *= 2
    return out


def from_hop(x, axis, hop):
    return lax.ppermute(x, axis, [(i, i ^ hop) for i in range(lax.axis_size(axis))])


def hop_sum(x, axis, hop):
    return x + from_hop(x, axis, hop)


def finish_kernel(grad, arrived, curve, curve_arrived, hess, total):
    hess[...] = grad[...] + arrived[...]
    total[...] = jnp.sum(curve[...] + curve_arrived[...], keepdims=True)


def finish(grad, arrived, curve, curve_arrived):
    vmem = pl.BlockSpec(memory_space=pltpu.VMEM)
    hess, total = pl.pallas_call(
        finish_kernel,
        in_specs=[vmem] * 4,
        out_specs=[vmem] * 2,
        out_shape=[jax.ShapeDtypeStruct(grad.shape, grad.dtype), jax.ShapeDtypeStruct((1, 1), curve.dtype)],
        compiler_params=pltpu.CompilerParams(vmem_limit_bytes=4 * 1024 * 1024),
        name="finish",
    )(grad, arrived, curve, curve_arrived)
    return (hess, total.reshape(()))


def local(depth, wet, bed, rough, direction, gauge_cells):
    events, steps, rows, cols = depth.shape
    cells = gauge_cells.reshape(events, 1, -1)
    sides = 2 if lax.axis_size("row") > 2 else 1
    counts, send_a, send_b, *more = edges_and_gauges(cells, depth, wet, bed, rough, direction)
    rims = [exchange(x, "row", k) for k, x in enumerate(more[:sides])]
    side_a = exchange(send_a, "col", 0)
    side_b = exchange(send_b, "col", 1)
    corners = [diagonal(x, k // 2, k % 2) for k, x in enumerate(more[sides:])]
    block = inner(depth, wet, bed, rough, direction)
    rims, side_a, side_b, corners, block = lax.optimization_barrier((rims, side_a, side_b, corners, block))
    if sides == 1:
        corners = corners + [jnp.zeros_like(x) for x in corners]
    rim_top, rim_bottom = row_rims(rims, events, steps)
    curve, *coefficients = tangents(block[0], counts, *block[1:], rim_top, rim_bottom, side_a, side_b, *corners)
    hops = hops_over("event") + hops_over("row") + hops_over("col")
    sums = ()
    for e in range(events):
        sums = gradient(e, sums, block[0], *coefficients)
        if hops:
            curve = hop_sum(curve, *hops.pop(0))
            sums, curve = lax.optimization_barrier((sums, curve))
    grad, arrived = sums, None
    for axis, hop in hops_over("event"):
        if arrived is not None:
            grad = grad + arrived
            if hops:
                curve = hop_sum(curve, *hops.pop(0))
                grad, curve = lax.optimization_barrier((grad, curve))
        arrived = from_hop(grad, axis, hop)
    while len(hops) > 1:
        curve = hop_sum(curve, *hops.pop(0))
    return finish(grad, arrived, curve, from_hop(curve, *hops[0]))


def solution(mesh):
    placed = (
        P("event", None, "row", "col"),
        P("event", "row", "col"),
        P("row", "col"),
        P("row", "col"),
        P("row", "col"),
        P("event", "row", "col", None),
    )
    return jax.shard_map(
        local, mesh=mesh, in_specs=placed, out_specs=(P("row", "col"), P()), check_vma=False
    )
```

```python
import functools

import jax
import jax.numpy as jnp
from jax import lax
from jax.experimental import pallas as pl
from jax.experimental.pallas import tpu as pltpu
from jax.sharding import PartitionSpec as P

time_step = 0.035
slope_floor = 0.01
gauge_weight = 100.0
REACH = 6
LANES = 128
LN2 = 0.6931471805599453
SUB = 8


def pairs(count, first):
    out = []
    for i in range(first, count - 1, 2):
        out += [(i, i + 1), (i + 1, i)]
    return out


def exchange(x, axis, first):
    perm = pairs(lax.axis_size(axis), first)
    return lax.ppermute(x, axis, perm) if perm else None


def lanes_of(shape):
    return lax.broadcasted_iota(jnp.int32, shape, 1)


def plan(events, steps):
    out, slot = [], 0
    for n in [REACH - t for _ in range(events) for t in range(steps)] + [REACH] * (events + 3) + [REACH // 2] * events:
        out.append((n, slot))
        slot += n
    return out, -(-slot // SUB)


def one_hot(hit):
    return jnp.where(hit, 1.0, 0.0).astype(jnp.bfloat16)


def tally_of(row, col, rows, cols):
    gauges = row.shape[-1]
    tall = rows * (cols // 256)
    inside = (row >= 0) & (row < rows)
    high = jnp.where(inside, (col // 256) * rows + row, -1)
    hits = lax.dot_general(
        one_hot(lax.broadcasted_iota(jnp.int32, (tall, gauges), 0) == high),
        one_hot(lax.broadcasted_iota(jnp.int32, (256, gauges), 0) == col % 256),
        (((1,), (1,)), ((), ())),
        preferred_element_type=jnp.float32,
    )
    return [hits[b * rows : (b + 1) * rows] for b in range(cols // 256)]


def edge_kernel(sides, *refs):
    ins, outs, rest = refs[1:6], refs[6 : 9 + 3 * sides], refs[9 + 3 * sides :]
    cnt, pay_a, pay_b, *more = outs
    pays, corners = more[:sides], more[sides:]
    cells, sems = rest[-2:]
    events, steps, rows, cols = ins[0].shape
    even = lax.axis_index("row") % 2 == 0
    even_col = lax.axis_index("col") % 2 == 0
    slots, count = plan(events, steps)
    sub = lax.broadcasted_iota(jnp.int32, (SUB, cols), 0)
    copies = [pltpu.make_async_copy(refs[0], cells, sems.at[0, 5])]
    edges = []
    for k in range(sides):
        sends_last = even if k == 0 else jnp.logical_not(even)
        edge = pl.multiple_of(jnp.where(sends_last, rows - SUB, 0), SUB)
        edges.append((sends_last, edge))
        for i, x in enumerate(ins):
            lead = (slice(None),) * (len(x.shape) - 2)
            at = x.at[(*lead, pl.ds(edge, SUB), slice(None))]
            copies.append(pltpu.make_async_copy(at, rest[5 * k + i], sems.at[k, i]))
    columns = (rest[5 * sides : 5 * sides + 5], rest[5 * sides + 5 : 5 * sides + 10])
    for k in range(2):
        for i, x in enumerate(ins):
            lead = (slice(None),) * (len(x.shape) - 1)
            at = x.at[(*lead, slice(0, LANES) if k == 0 else slice(cols - LANES, cols))]
            copies.append(pltpu.make_async_copy(at, columns[k][i], sems.at[sides + k, i]))
    for copy in copies:
        copy.start()
    copies[0].wait()
    for e in range(events):
        g = cells[e]
        for b, x in enumerate(tally_of(g // cols, g % cols, rows, cols)):
            for j in range(256 // LANES):
                cnt[e, b * (256 // LANES) + j] = x[:, j * LANES : (j + 1) * LANES]
    for copy in copies[1:]:
        copy.wait()

    for k, pay in enumerate(pays):
        d, w, b, r, v = rest[5 * k : 5 * k + 5]
        fields = [d[e, t] for e in range(events) for t in range(steps)]
        fields += [w[e].astype(jnp.float32) for e in range(events)] + [b[...], r[...], v[...]]
        fields += [
            jnp.concatenate([cnt[e, j, pl.ds(edges[k][1], SUB), :] for j in range(cols // LANES)], axis=1)
            for e in range(events)
        ]
        tiles = [jnp.zeros((SUB, cols), jnp.float32)] * count
        for x, (n, slot) in zip(fields, slots):
            if 1 < n < SUB:
                x = jnp.where(edges[k][0], pltpu.roll(x, n, 0), x)
            for i in range(slot // SUB, (slot + n - 1) // SUB + 1):
                low, high = slot - i * SUB, slot + n - i * SUB
                y = pltpu.roll(x, low % SUB, 0) if low % SUB else x
                tiles[i] = jnp.where((sub >= low) & (sub < high), y, tiles[i])
        for i in range(count):
            pay[i * SUB : (i + 1) * SUB] = tiles[i]

    lane = lanes_of((rows, LANES))
    packs = []
    for side in range(2):
        d, w, b, r, v = columns[side]
        pack = jnp.zeros((rows, LANES), jnp.float32)
        xs = [d[e, t] for e in range(events) for t in range(steps)]
        xs += [w[e].astype(jnp.float32) for e in range(events)]
        xs += [b[...], r[...], v[...]]
        xs += [cnt[e, 0 if side == 0 else cols // LANES - 1] for e in range(events)]
        for f, x in enumerate(xs):
            place = f * REACH
            shift = (place + REACH if side == 1 else place) % LANES
            if shift:
                x = pltpu.roll(x, shift, 1)
            pack = jnp.where((lane >= place) & (lane < place + REACH), x, pack)
        packs.append(pack)
    pay_a[...] = jnp.where(even_col, packs[1], packs[0])
    pay_b[...] = jnp.where(even_col, packs[0], packs[1])
    for k in range(sides):
        corners[2 * k][...] = pay_a[pl.ds(edges[k][1], SUB), :]
        corners[2 * k + 1][...] = pay_b[pl.ds(edges[k][1], SUB), :]


def edges_and_gauges(cells, depth, wet, bed, rough, direction):
    events, steps, rows, cols = depth.shape
    sides = 2 if lax.axis_size("row") > 2 else 1
    _, count = plan(events, steps)
    vmem, anywhere = pl.BlockSpec(memory_space=pltpu.VMEM), pl.BlockSpec(memory_space=pl.ANY)
    ins = (depth, wet, bed, rough, direction)
    shapes = [(events, cols // LANES, rows, LANES)] + [(rows, LANES)] * 2
    shapes += [(count * SUB, cols)] * sides + [(SUB, LANES)] * (2 * sides)
    return pl.pallas_call(
        functools.partial(edge_kernel, sides),
        in_specs=[anywhere] * 6,
        out_specs=[vmem] * len(shapes),
        out_shape=[jax.ShapeDtypeStruct(x, jnp.float32) for x in shapes],
        scratch_shapes=[pltpu.VMEM((*x.shape[:-2], SUB, cols), x.dtype) for x in ins] * sides
        + [pltpu.VMEM((*x.shape[:-1], LANES), x.dtype) for x in ins] * 2
        + [pltpu.VMEM(cells.shape, cells.dtype), pltpu.SemaphoreType.DMA((sides + 2, 6))],
        compiler_params=pltpu.CompilerParams(vmem_limit_bytes=58 * 1024 * 1024),
        name="edges",
    )(cells, *ins)


def diagonal(x, first_row, first_col):
    count = lax.axis_size("col")
    perm = [
        (a * count + c, b * count + d)
        for a, b in pairs(lax.axis_size("row"), first_row)
        for c, d in pairs(count, first_col)
    ]
    return lax.ppermute(x, ("row", "col"), perm)


def rim_kernel(sides, events, steps, *refs):
    rims_in = refs[:sides]
    rim_top, rim_bottom = refs[sides:]
    cols = rim_top.shape[-1]
    even_row = lax.axis_index("row") % 2 == 0
    sub = lax.broadcasted_iota(jnp.int32, (SUB, cols), 0)
    slots, _ = plan(events, steps)
    nothing = jnp.zeros((SUB, cols), jnp.float32)

    def field(ref, n, slot):
        x = nothing
        for i in range(slot // SUB, (slot + n - 1) // SUB + 1):
            low, high = slot - i * SUB, slot + n - i * SUB
            y = ref[i * SUB : (i + 1) * SUB]
            y = pltpu.roll(y, -low % SUB, 0) if low % SUB else y
            x = jnp.where((sub >= -low) & (sub < min(n, SUB - low)) & (sub >= max(0, -low)), y, x)
        return x

    for f, (n, slot) in enumerate(slots):
        x = field(rims_in[0], n, slot)
        y = field(rims_in[1], n, slot) if sides > 1 else nothing
        rim_bottom[f] = jnp.where(even_row, x, y)
        rim_top[f] = pltpu.roll(jnp.where(even_row, y, x), SUB - n, 0)


def row_rims(rims, events, steps):
    vmem = pl.BlockSpec(memory_space=pltpu.VMEM)
    rim = jax.ShapeDtypeStruct((events * (steps + 2) + 3, SUB, rims[0].shape[-1]), jnp.float32)
    return pl.pallas_call(
        functools.partial(rim_kernel, len(rims), events, steps),
        in_specs=[vmem] * len(rims),
        out_specs=[vmem] * 2,
        out_shape=[rim] * 2,
        compiler_params=pltpu.CompilerParams(vmem_limit_bytes=4 * 1024 * 1024),
        name="row_rims",
    )(*rims)


def up(x):
    return pltpu.roll(x, SUB - 1, 0)


def down(x):
    return pltpu.roll(x, 1, 0)


def sublanes():
    return lax.broadcasted_iota(jnp.int32, (SUB, LANES), 0)


def to_right(x, nxt):
    last = lanes_of((SUB, LANES)) == LANES - 1
    return jnp.where(last, pltpu.roll(nxt, LANES - 1, 1), pltpu.roll(x, LANES - 1, 1))


def right(xs):
    last = lanes_of((SUB, LANES)) == LANES - 1
    r = [pltpu.roll(x, LANES - 1, 1) for x in xs]
    return [jnp.where(last, r[(j + 1) % len(xs)], r[j]) for j in range(len(xs))]


def left(xs):
    first = lanes_of((SUB, LANES)) == 0
    r = [pltpu.roll(x, 1, 1) for x in xs]
    return [jnp.where(first, r[j - 1], r[j]) for j in range(len(xs))]


def at_lanes(j):
    return slice(j * LANES, (j + 1) * LANES)


def get(ref, *at):
    return [ref[(*at, slice(None), at_lanes(j))] for j in range(ref.shape[-1] // LANES)]


def put(xs, ref, *at):
    for j, x in enumerate(xs):
        ref[(*at, slice(None), at_lanes(j))] = x


def followers(first, below, above):
    last = sublanes() == SUB - 1
    f, b, a = up(first), up(below), up(above)
    return jnp.where(last, b, f), b, jnp.where(last, f, a)


def follow(ref, *at):
    deep = ref.shape[-3] - 5
    sets = zip(get(ref, *at, 0), get(ref, *at, deep), get(ref, *at, deep + 1))
    for k, xs in enumerate(zip(*[followers(*x) for x in sets])):
        put(xs, ref, *at, deep + 2 + k)


def preceding(ref, deep, passed):
    first = sublanes() == 0
    last, below, above = get(ref, deep), get(ref, deep + 1), get(ref, deep + 2)
    return (
        [jnp.where(first, down(a), down(l)) for a, l in zip(above, last)],
        [jnp.where(first, down(l), down(b)) - l for b, l in zip(below, last)],
        [down(a) - b for a, b in zip(above, below)],
    )


def face(h, h_k, sb, cond, inv):
    hs = h + h_k
    s = (h_k - h) + sb
    x = s * s + slope_floor
    y = lax.rsqrt(x)
    p = cond * (jnp.exp2((2.0 / 3.0 / LN2) * jnp.log(hs)) * (y * lax.rsqrt(y)))
    ps = p * s
    t = p * hs
    B = t * (0.3 + (0.3 * slope_floor) * (y * y))
    return ps - B, ps + B, (t * s) * inv


scale = (5.0 / 3.0) * time_step * 2.0 ** (-2.0 / 3.0)


def inner_kernel(
    depth, wet, bed, rough, direction,
    prim, a_x, b_x, c_x, a_y, b_y, c_y, q_x, q_y,
    nat, sb_x, sb_y, inv_x, inv_y, cond_x, cond_y,
):
    events, steps, rows, cols = depth.shape
    deep, count = rows // SUB, cols // LANES
    fields = [bed, rough, direction] + [wet.at[e] for e in range(events)]
    fields += [depth.at[e, t] for e in range(events) for t in range(steps)]
    for k, x in enumerate(fields):
        for j in range(count):
            nat[k, j] = x[:, at_lanes(j)].astype(jnp.float32)

    @pl.loop(0, deep, unroll=4)
    def _(i):
        spread = lambda k: [nat[k, j, pl.ds(i, SUB, stride=deep), :] for j in range(count)]
        m = [jnp.exp(x) for x in spread(1)]
        put(spread(0), prim, 0, i)
        put(m, prim, 1, i)
        put([x * y for x, y in zip(m, spread(2))], prim, 2, i)
        for k in range(3, 3 + events * (steps + 1)):
            put(spread(k), prim, k, i)

    for k in range(3 + events * (steps + 1)):
        put([up(x) for x in get(prim, k, 0)], prim, k, deep)

    @pl.loop(0, deep, unroll=4)
    def _(i):
        b, m, q = (get(prim, k, i) for k in range(3))
        put([y - x for x, y in zip(b, right(b))], sb_x, i)
        put([y - x for x, y in zip(b, get(prim, 0, i + 1))], sb_y, i)
        ix = [1.0 / (x + y) for x, y in zip(m, right(m))]
        iy = [1.0 / (x + y) for x, y in zip(m, get(prim, 1, i + 1))]
        put([-0.6 * x for x in ix], inv_x, i)
        put([-0.6 * x for x in iy], inv_y, i)
        put([x + y for x, y in zip(q, right(q))], q_x, i)
        put([x + y for x, y in zip(q, get(prim, 2, i + 1))], q_y, i)
        for e in range(events):
            w = get(prim, 3 + e, i)
            put([(scale * z) * (x * y) for x, y, z in zip(w, right(w), ix)], cond_x, e, i)
            put([(scale * z) * (x * y) for x, y, z in zip(w, get(prim, 3 + e, i + 1), iy)], cond_y, e, i)

    @pl.loop(0, events)
    def _(e):
        for t in range(steps):

            @pl.loop(0, deep, unroll=deep)
            def _(i):
                k = 3 + events + e * steps + t
                h = get(prim, k, i)
                h_r, h_d = right(h), get(prim, k, i + 1)
                for j in range(count):
                    J = at_lanes(j)
                    for h_k, sb, cond, inv, a, b, c in (
                        (h_r, sb_x, cond_x, inv_x, a_x, b_x, c_x),
                        (h_d, sb_y, cond_y, inv_y, a_y, b_y, c_y),
                    ):
                        A, B, C = face(h[j], h_k[j], sb[i, :, J], cond[e, i, :, J], inv[i, :, J])
                        c[e, t, i, :, J] = C
                        if t:
                            a[e, t - 1, i, :, J] = A
                            b[e, t - 1, i, :, J] = B


def inner(depth, wet, bed, rough, direction):
    events, steps, rows, cols = depth.shape
    deep = rows // SUB
    shape = lambda *lead: (*lead, deep, SUB, cols)
    vm = lambda *lead: pltpu.VMEM(shape(*lead), jnp.float32)
    out = lambda *lead: jax.ShapeDtypeStruct(shape(*lead), jnp.float32)
    vmem = pl.BlockSpec(memory_space=pltpu.VMEM)
    fields = 3 + events * (steps + 1)
    return pl.pallas_call(
        inner_kernel,
        in_specs=[vmem] * 5,
        out_specs=[vmem] * 9,
        out_shape=[
            jax.ShapeDtypeStruct((fields, deep + 1, SUB, cols), jnp.float32),
            *[out(events, steps - 1), out(events, steps - 1), out(events, steps)] * 2,
            out(),
            out(),
        ],
        scratch_shapes=[
            pltpu.VMEM((fields, cols // LANES, rows, LANES), jnp.float32),
            *[vm()] * 4,
            *[vm(events)] * 2,
        ],
        compiler_params=pltpu.CompilerParams(vmem_limit_bytes=12 * 1024 * 1024),
        cost_estimate=pl.CostEstimate(flops=100000000, bytes_accessed=16000000, transcendentals=0),
        name="inner",
    )(depth, wet, bed, rough, direction)


def tangent_kernel(
    prim, cnt, ia_x, ib_x, ic_x, ia_y, ib_y, ic_y, iq_x, iq_y, rim_top, rim_bottom, side_a, side_b,
    corner_aa, corner_ab, corner_ba, corner_bb, curve_ref, source, a_x, b_x, c_x, a_y, b_y, c_y,
    nat, ext, xcnt, sb_x, sb_y, q_x, q_y, inv_x, inv_y, cond_x, cond_y, tan_a, tan_b, flow,
):
    events, steps, deep, _, cols = ic_x.shape
    rows, tiles = deep * SUB, cols // LANES
    count, tall = tiles + 1, rows + 2 * SUB
    even_col = lax.axis_index("col") % 2 == 0
    lane_t = lanes_of((tall, LANES))
    even_row = lax.axis_index("row") % 2 == 0

    def whole_side(side, corner_a, corner_b):
        above = jnp.where(even_row, corner_b[...], corner_a[...])
        below = jnp.where(even_row, corner_a[...], corner_b[...])
        return jnp.concatenate([above, side[...], below], axis=0)

    full_a, full_b = whole_side(side_a, corner_aa, corner_ba), whole_side(side_b, corner_ab, corner_bb)
    right_rim = jnp.where(even_col, full_a, full_b)
    left_rim = jnp.where(even_col, full_b, full_a)
    J = [at_lanes(j) for j in range(count)]
    zero = jnp.zeros((SUB, LANES), jnp.float32)
    below, above = deep, deep + 1
    fields = prim.shape[0]

    place_in = [events * (steps + 1) + k for k in range(3)]
    place_in += [events * steps + e for e in range(events)]
    place_in += [e * steps + t for e in range(events) for t in range(steps)]
    place_in += [events * (steps + 1) + 3 + e for e in range(events)]
    for k, f in enumerate(place_in):
        place = f * REACH
        r = pltpu.roll(right_rim, (LANES - place) % LANES, 1) if place else right_rim
        l = pltpu.roll(left_rim, (LANES - REACH - place) % LANES, 1)
        x = jnp.where(lane_t < REACH, r, jnp.where(lane_t >= LANES - REACH, l, 0.0))
        if k == 1:
            m_side = x = jnp.exp(x)
        if k == 2:
            x = m_side * x
        nat[k] = x
        to, n = (ext, k) if k < fields else (xcnt, k - fields)
        for i in range(deep):
            to[n, i, :, J[tiles]] = nat[k, pl.ds(SUB + i, SUB, stride=deep), :]
        for i, rim, at in ((below, rim_bottom, SUB + rows), (above, rim_top, 0)):
            xs = get(rim, f)
            if k == 1:
                xs = [jnp.exp(x) for x in xs]
            if k == 2:
                xs = [x * y for x, y in zip(xs, get(ext, 1, i))]
            put(xs, to, n, i)
            to[n, i, :, J[tiles]] = nat[k, at : at + SUB, :]

    def value(k, i, j):
        return ext[k, i, :, J[j]] if j == tiles or (isinstance(i, int) and i >= deep) else prim[k, i, :, J[j]]

    def next_rows(k, j):
        return followers(value(k, 0, j), value(k, below, j), value(k, above, j))

    for k in range(fields):
        ext[k, deep + 2, :, J[tiles]] = next_rows(k, tiles)[0]

    def derive(i, j, along, k_of):
        sb, inv, q, cond = (sb_x, inv_x, q_x, cond_x) if along else (sb_y, inv_y, q_y, cond_y)
        x, y = k_of(0)
        sb[i, :, J[j]] = y - x
        x, y = k_of(1)
        z = 1.0 / (x + y)
        inv[i, :, J[j]] = -0.6 * z
        x, y = k_of(2)
        q[i, :, J[j]] = x + y
        for e in range(events):
            x, y = k_of(3 + e)
            cond[e, i, :, J[j]] = (scale * z) * (x * y)

    def across(i, j):
        return lambda k: (value(k, i, j), to_right(value(k, i, j), value(k, i, (j + 1) % count)))

    @pl.loop(0, deep, unroll=4)
    def _(i):
        for j in (tiles - 1, tiles):
            derive(i, j, True, across(i, j))
        n = jnp.where(i == deep - 1, deep + 2, i + 1)
        derive(i, tiles, False, lambda k: (value(k, i, tiles), ext[k, n, :, J[tiles]]))

    for i in (below, above):
        for j in range(count):
            derive(i, j, True, across(i, j))
    for n, i in enumerate((deep - 1, below, above)):
        for j in range(tiles if n == 0 else count):
            derive(i, j, False, lambda k: (value(k, i, j), next_rows(k, j)[n]))

    curve_ref[...] = jnp.zeros(curve_ref.shape, jnp.float32)
    put([zero] * count, flow, 0)

    @pl.loop(0, events)
    def _(e):
        for t in range(steps):
            old, new = (tan_a, tan_b) if t % 2 else (tan_b, tan_a)
            k = 3 + events + e * steps + t

            def row(i):
                static = isinstance(i, int)
                rim = static and i >= deep
                nxt = i + 3 if static and i >= deep - 1 else i + 1
                if t:
                    d = get(old, i)
                    d_r, d_d = right(d), get(old, nxt)
                fx, fy = [], []
                here = lambda j: ext[k, i, :, J[j]] if rim or j == tiles else prim[k, i, :, J[j]]
                for j in range(count):
                    inside = not rim and j < tiles - 1
                    if inside:
                        A, B = (ia_x[e, t - 1, i, :, J[j]], ib_x[e, t - 1, i, :, J[j]]) if t else (None, None)
                        C = ic_x[e, t, i, :, J[j]]
                        f = C * iq_x[i, :, J[j]]
                    else:
                        h = here(j)
                        A, B, C = face(
                            h, to_right(h, here((j + 1) % count)),
                            sb_x[i, :, J[j]], cond_x[e, i, :, J[j]], inv_x[i, :, J[j]],
                        )
                        f = C * q_x[i, :, J[j]]
                    c_x[e, t, i, :, J[j]] = C
                    if t:
                        a_x[e, t - 1, i, :, J[j]] = A
                        b_x[e, t - 1, i, :, J[j]] = B
                        f += A * d[j] + B * d_r[j]
                    fx.append(f)
                    inside = not (static and i >= deep - 1) and j < tiles
                    if inside:
                        A, B = (ia_y[e, t - 1, i, :, J[j]], ib_y[e, t - 1, i, :, J[j]]) if t else (None, None)
                        C = ic_y[e, t, i, :, J[j]]
                        f = C * iq_y[i, :, J[j]]
                    else:
                        h = here(j)
                        if static and i >= deep - 1:
                            first = ext[k, 0, :, J[j]] if j == tiles else prim[k, 0, :, J[j]]
                            h_d = followers(first, ext[k, below, :, J[j]], ext[k, above, :, J[j]])[i - deep + 1]
                        else:
                            h_d = ext[k, i + 1, :, J[j]]
                        A, B, C = face(h, h_d, sb_y[i, :, J[j]], cond_y[e, i, :, J[j]], inv_y[i, :, J[j]])
                        f = C * q_y[i, :, J[j]]
                    c_y[e, t, i, :, J[j]] = C
                    if t:
                        a_y[e, t - 1, i, :, J[j]] = A
                        b_y[e, t - 1, i, :, J[j]] = B
                        f += A * d[j] + B * d_d[j]
                    fy.append(f)
                put(fy, flow, i + 1)
                before = get(flow, i)
                fl = left(fx)
                for j in range(count):
                    r = (fx[j] - fl[j]) + (fy[j] - before[j])
                    new[i, :, J[j]] = d[j] + r if t else r

            main = deep - 2
            pl.loop(0, main, unroll=3 if main % 3 == 0 else 1)(row)
            for i in range(main, deep + 2):
                row(i)
            for i, lack in zip((0, below, above), preceding(flow, deep, zero)):
                put([x - y for x, y in zip(get(new, i), lack)], new, i)
            follow(new)

        old = tan_a if steps % 2 else tan_b
        total = zero
        for i in range(deep + 2):
            for j in range(count):
                own = i < deep and j < tiles
                n = cnt[e, j, pl.ds(i, SUB, stride=deep), :] if own else xcnt[e, i, :, J[j]]
                r = old[i, :, J[j]]
                s = (gauge_weight * n) * r
                source[e, i, :, J[j]] = s
                if own:
                    total += s * r
        curve_ref[...] += total
        follow(source, e)


def tangents(prim, cnt, *more_inputs):
    fields, _, _, cols = prim.shape
    events, deep = cnt.shape[0], prim.shape[1] - 1
    steps = more_inputs[2].shape[1]
    wide = cols + LANES
    regs = deep + 2
    vm = lambda *lead: pltpu.VMEM((*lead, regs, SUB, wide), jnp.float32)
    more = lambda *lead: pltpu.VMEM((*lead, regs + 3, SUB, wide), jnp.float32)
    out = lambda *lead: jax.ShapeDtypeStruct((*lead, regs, SUB, wide), jnp.float32)
    vmem = pl.BlockSpec(memory_space=pltpu.VMEM)
    return pl.pallas_call(
        tangent_kernel,
        in_specs=[vmem] * (2 + len(more_inputs)),
        out_specs=[vmem] * 8,
        out_shape=[
            jax.ShapeDtypeStruct((SUB, LANES), jnp.float32),
            jax.ShapeDtypeStruct((events, regs + 3, SUB, wide), jnp.float32),
            *[out(events, steps - 1), out(events, steps - 1), out(events, steps)] * 2,
        ],
        scratch_shapes=[
            pltpu.VMEM((fields + events, deep * SUB + 2 * SUB, LANES), jnp.float32),
            more(fields),
            vm(events),
            *[vm()] * 6,
            *[vm(events)] * 2,
            *[more()] * 3,
        ],
        compiler_params=pltpu.CompilerParams(vmem_limit_bytes=16 * 1024 * 1024),
        name="tangents",
    )(prim, cnt, *more_inputs)


def adjoint_kernel(first_event, last_event, m_c, source, a_x, b_x, c_x, a_y, b_y, c_y, *refs):
    sums = () if first_event else refs[:2]
    outs = refs[len(sums) : len(sums) + (1 if last_event else 2)]
    nat, adj_a, adj_b, flow, *own = refs[len(sums) + len(outs) :]
    g_x, g_y = own if last_event else outs
    steps, regs, _, wide = c_x.shape
    deep = regs - 2
    count = wide // LANES
    J = [at_lanes(j) for j in range(count)]
    zero = jnp.zeros((SUB, LANES), jnp.float32)
    put([zero] * count, flow, 0)

    for t in range(steps - 1, -1, -1):
        old, new = (adj_a, adj_b) if t % 2 else (adj_b, adj_a)
        if t == steps - 1:
            old = source
            base_x, base_y = sums if sums else (None, None)
        else:
            base_x, base_y = g_x, g_y

        @pl.loop(0, regs, unroll=5 if regs % 5 == 0 else 1)
        def _(i):
            l = get(old, i)
            l_r, l_d = right(l), get(old, jnp.where(i < deep - 1, i + 1, i + 3))
            acc, kx, ky = [], [], []
            for j in range(count):
                p = l[j] - l_r[j]
                g = c_x[t, i, :, J[j]] * p
                g_x[i, :, J[j]] = g + base_x[i, :, J[j]] if base_x is not None else g
                if t:
                    a = l[j] + a_x[t - 1, i, :, J[j]] * p
                    kx.append(b_x[t - 1, i, :, J[j]] * p)
                p = l[j] - l_d[j]
                g = c_y[t, i, :, J[j]] * p
                g_y[i, :, J[j]] = g + base_y[i, :, J[j]] if base_y is not None else g
                if t:
                    acc.append(a + a_y[t - 1, i, :, J[j]] * p)
                    ky.append(b_y[t - 1, i, :, J[j]] * p)
            if t:
                put(ky, flow, i + 1)
                before = get(flow, i)
                kl = left(kx)
                for j in range(count):
                    new[i, :, J[j]] = acc[j] + (kl[j] + before[j])

        if t:
            for i, lack in zip((0, deep, deep + 1), preceding(flow, deep, zero)):
                put([x + y for x, y in zip(get(new, i), lack)], new, i)
            follow(new)

    if last_event:
        (grad_ref,) = outs
        tiles = grad_ref.shape[-1] // LANES
        first = sublanes() == 0
        put(
            [jnp.where(first, down(a), down(l)) for a, l in zip(get(g_y, deep + 1), get(g_y, deep - 1))],
            flow,
            0,
        )

        @pl.loop(0, deep, unroll=4)
        def _(i):
            x, y = get(g_x, i), get(g_y, i)
            put(y, flow, i + 1)
            xl, yl = left(x), get(flow, i)
            for j in range(tiles):
                g = m_c[i, :, J[j]] * ((x[j] + xl[j]) + (y[j] + yl[j]))
                nat[j, pl.ds(i, SUB, stride=deep), :] = g

        for j in range(tiles):
            grad_ref[:, J[j]] = nat[j]


def gradient(e, sums, prim, source, *coefficients):
    events, entries, _, wide = source.shape
    cols, regs = prim.shape[-1], entries - 3
    rows = (regs - 2) * SUB
    first, last = e == 0, e == events - 1
    vm = (regs, SUB, wide)
    more = pltpu.VMEM((entries, SUB, wide), jnp.float32)
    own = lambda x: pl.BlockSpec((None, *x.shape[1:]), lambda i: (e,) + (0,) * (x.ndim - 1))
    whole = lambda shape: pl.BlockSpec(shape, lambda i: (0,) * len(shape))
    return pl.pallas_call(
        functools.partial(adjoint_kernel, first, last),
        grid=(1,),
        in_specs=[pl.BlockSpec((None, *prim.shape[1:]), lambda i: (1, 0, 0, 0)), own(source)]
        + [own(x) for x in coefficients]
        + [whole(vm)] * len(sums),
        out_specs=whole((rows, cols)) if last else [whole(vm)] * 2,
        out_shape=jax.ShapeDtypeStruct((rows, cols), jnp.float32)
        if last
        else [jax.ShapeDtypeStruct(vm, jnp.float32)] * 2,
        scratch_shapes=[pltpu.VMEM((cols // LANES, rows, LANES), jnp.float32), more, more, more]
        + [pltpu.VMEM(vm, jnp.float32)] * (2 if last else 0),
        compiler_params=pltpu.CompilerParams(vmem_limit_bytes=16 * 1024 * 1024),
        cost_estimate=pl.CostEstimate(flops=40000000, bytes_accessed=12000000, transcendentals=0),
        name="gradient",
    )(prim, source, *coefficients, *sums)


def hops_over(axis):
    count, hop, out = lax.axis_size(axis), 1, []
    while hop < count:
        out.append((axis, hop))
        hop *= 2
    return out


def from_hop(x, axis, hop):
    return lax.ppermute(x, axis, [(i, i ^ hop) for i in range(lax.axis_size(axis))])


def hop_sum(x, axis, hop):
    return x + from_hop(x, axis, hop)


def finish_kernel(grad, arrived, curve, curve_arrived, hess, total):
    hess[...] = grad[...] + arrived[...]
    total[...] = jnp.sum(curve[...] + curve_arrived[...], keepdims=True)


def finish(grad, arrived, curve, curve_arrived):
    vmem = pl.BlockSpec(memory_space=pltpu.VMEM)
    hess, total = pl.pallas_call(
        finish_kernel,
        in_specs=[vmem] * 4,
        out_specs=[vmem] * 2,
        out_shape=[jax.ShapeDtypeStruct(grad.shape, grad.dtype), jax.ShapeDtypeStruct((1, 1), curve.dtype)],
        compiler_params=pltpu.CompilerParams(vmem_limit_bytes=4 * 1024 * 1024),
        name="finish",
    )(grad, arrived, curve, curve_arrived)
    return (hess, total.reshape(()))


def local(depth, wet, bed, rough, direction, gauge_cells):
    events, steps, rows, cols = depth.shape
    cells = gauge_cells.reshape(events, 1, -1)
    sides = 2 if lax.axis_size("row") > 2 else 1
    counts, send_a, send_b, *more = edges_and_gauges(cells, depth, wet, bed, rough, direction)
    rims = [exchange(x, "row", k) for k, x in enumerate(more[:sides])]
    side_a = exchange(send_a, "col", 0)
    side_b = exchange(send_b, "col", 1)
    corners = [diagonal(x, k // 2, k % 2) for k, x in enumerate(more[sides:])]
    block = inner(depth, wet, bed, rough, direction)
    rims, side_a, side_b, corners, block = lax.optimization_barrier((rims, side_a, side_b, corners, block))
    if sides == 1:
        corners = corners + [jnp.zeros_like(x) for x in corners]
    rim_top, rim_bottom = row_rims(rims, events, steps)
    curve, *coefficients = tangents(block[0], counts, *block[1:], rim_top, rim_bottom, side_a, side_b, *corners)
    hops = hops_over("event") + hops_over("row") + hops_over("col")
    sums = ()
    for e in range(events):
        sums = gradient(e, sums, block[0], *coefficients)
        if hops:
            curve = hop_sum(curve, *hops.pop(0))
            sums, curve = lax.optimization_barrier((sums, curve))
    grad, arrived = sums, None
    for axis, hop in hops_over("event"):
        if arrived is not None:
            grad = grad + arrived
            if hops:
                curve = hop_sum(curve, *hops.pop(0))
                grad, curve = lax.optimization_barrier((grad, curve))
        arrived = from_hop(grad, axis, hop)
    while len(hops) > 1:
        curve = hop_sum(curve, *hops.pop(0))
    return finish(grad, arrived, curve, from_hop(curve, *hops[0]))


def solution(mesh):
    placed = (
        P("event", None, "row", "col"),
        P("event", "row", "col"),
        P("row", "col"),
        P("row", "col"),
        P("row", "col"),
        P("event", "row", "col", None),
    )
    return jax.shard_map(
        local, mesh=mesh, in_specs=placed, out_specs=(P("row", "col"), P()), check_vma=False
    )
```

```python
import functools

import jax
import jax.numpy as jnp
from jax import lax
from jax.experimental import pallas as pl
from jax.experimental.pallas import tpu as pltpu
from jax.sharding import PartitionSpec as P

time_step = 0.035
slope_floor = 0.01
gauge_weight = 100.0
REACH = 6
LANES = 128
LN2 = 0.6931471805599453
SUB = 8


def pairs(count, first):
    out = []
    for i in range(first, count - 1, 2):
        out += [(i, i + 1), (i + 1, i)]
    return out


def exchange(x, axis, first):
    perm = pairs(lax.axis_size(axis), first)
    return lax.ppermute(x, axis, perm) if perm else None


def lanes_of(shape):
    return lax.broadcasted_iota(jnp.int32, shape, 1)


def plan(events, steps):
    out, slot = [], 0
    for n in [REACH - t for _ in range(events) for t in range(steps)] + [REACH] * (events + 3) + [REACH // 2] * events:
        out.append((n, slot))
        slot += n
    return out, -(-slot // SUB)


def one_hot(hit):
    return jnp.where(hit, 1.0, 0.0).astype(jnp.bfloat16)


def tally_of(row, col, rows, cols):
    gauges = row.shape[-1]
    tall = rows * (cols // 256)
    inside = (row >= 0) & (row < rows)
    high = jnp.where(inside, (col // 256) * rows + row, -1)
    hits = lax.dot_general(
        one_hot(lax.broadcasted_iota(jnp.int32, (tall, gauges), 0) == high),
        one_hot(lax.broadcasted_iota(jnp.int32, (256, gauges), 0) == col % 256),
        (((1,), (1,)), ((), ())),
        preferred_element_type=jnp.float32,
    )
    return [hits[b * rows : (b + 1) * rows] for b in range(cols // 256)]


def edge_kernel(sides, *refs):
    ins, outs, rest = refs[1:6], refs[6 : 9 + 3 * sides], refs[9 + 3 * sides :]
    cnt, pay_a, pay_b, *more = outs
    pays, corners = more[:sides], more[sides:]
    cells, sems = rest[-2:]
    events, steps, rows, cols = ins[0].shape
    even = lax.axis_index("row") % 2 == 0
    even_col = lax.axis_index("col") % 2 == 0
    slots, count = plan(events, steps)
    sub = lax.broadcasted_iota(jnp.int32, (SUB, cols), 0)
    copies = [pltpu.make_async_copy(refs[0], cells, sems.at[0, 5])]
    edges = []
    for k in range(sides):
        sends_last = even if k == 0 else jnp.logical_not(even)
        edge = pl.multiple_of(jnp.where(sends_last, rows - SUB, 0), SUB)
        edges.append((sends_last, edge))
        for i, x in enumerate(ins):
            lead = (slice(None),) * (len(x.shape) - 2)
            at = x.at[(*lead, pl.ds(edge, SUB), slice(None))]
            copies.append(pltpu.make_async_copy(at, rest[5 * k + i], sems.at[k, i]))
    columns = (rest[5 * sides : 5 * sides + 5], rest[5 * sides + 5 : 5 * sides + 10])
    for k in range(2):
        for i, x in enumerate(ins):
            lead = (slice(None),) * (len(x.shape) - 1)
            at = x.at[(*lead, slice(0, LANES) if k == 0 else slice(cols - LANES, cols))]
            copies.append(pltpu.make_async_copy(at, columns[k][i], sems.at[sides + k, i]))
    for copy in copies:
        copy.start()
    copies[0].wait()
    for e in range(events):
        g = cells[e]
        for b, x in enumerate(tally_of(g // cols, g % cols, rows, cols)):
            for j in range(256 // LANES):
                cnt[e, b * (256 // LANES) + j] = x[:, j * LANES : (j + 1) * LANES]
    for copy in copies[1:]:
        copy.wait()

    for k, pay in enumerate(pays):
        d, w, b, r, v = rest[5 * k : 5 * k + 5]
        fields = [d[e, t] for e in range(events) for t in range(steps)]
        fields += [w[e].astype(jnp.float32) for e in range(events)] + [b[...], r[...], v[...]]
        fields += [
            jnp.concatenate([cnt[e, j, pl.ds(edges[k][1], SUB), :] for j in range(cols // LANES)], axis=1)
            for e in range(events)
        ]
        tiles = [jnp.zeros((SUB, cols), jnp.float32)] * count
        for x, (n, slot) in zip(fields, slots):
            if 1 < n < SUB:
                x = jnp.where(edges[k][0], pltpu.roll(x, n, 0), x)
            for i in range(slot // SUB, (slot + n - 1) // SUB + 1):
                low, high = slot - i * SUB, slot + n - i * SUB
                y = pltpu.roll(x, low % SUB, 0) if low % SUB else x
                tiles[i] = jnp.where((sub >= low) & (sub < high), y, tiles[i])
        for i in range(count):
            pay[i * SUB : (i + 1) * SUB] = tiles[i]

    lane = lanes_of((rows, LANES))
    packs = []
    for side in range(2):
        d, w, b, r, v = columns[side]
        pack = jnp.zeros((rows, LANES), jnp.float32)
        xs = [d[e, t] for e in range(events) for t in range(steps)]
        xs += [w[e].astype(jnp.float32) for e in range(events)]
        xs += [b[...], r[...], v[...]]
        xs += [cnt[e, 0 if side == 0 else cols // LANES - 1] for e in range(events)]
        for f, x in enumerate(xs):
            place = f * REACH
            shift = (place + REACH if side == 1 else place) % LANES
            if shift:
                x = pltpu.roll(x, shift, 1)
            pack = jnp.where((lane >= place) & (lane < place + REACH), x, pack)
        packs.append(pack)
    pay_a[...] = jnp.where(even_col, packs[1], packs[0])
    pay_b[...] = jnp.where(even_col, packs[0], packs[1])
    for k in range(sides):
        corners[2 * k][...] = pay_a[pl.ds(edges[k][1], SUB), :]
        corners[2 * k + 1][...] = pay_b[pl.ds(edges[k][1], SUB), :]


def edges_and_gauges(cells, depth, wet, bed, rough, direction):
    events, steps, rows, cols = depth.shape
    sides = 2 if lax.axis_size("row") > 2 else 1
    _, count = plan(events, steps)
    vmem, anywhere = pl.BlockSpec(memory_space=pltpu.VMEM), pl.BlockSpec(memory_space=pl.ANY)
    ins = (depth, wet, bed, rough, direction)
    shapes = [(events, cols // LANES, rows, LANES)] + [(rows, LANES)] * 2
    shapes += [(count * SUB, cols)] * sides + [(SUB, LANES)] * (2 * sides)
    return pl.pallas_call(
        functools.partial(edge_kernel, sides),
        in_specs=[anywhere] * 6,
        out_specs=[vmem] * len(shapes),
        out_shape=[jax.ShapeDtypeStruct(x, jnp.float32) for x in shapes],
        scratch_shapes=[pltpu.VMEM((*x.shape[:-2], SUB, cols), x.dtype) for x in ins] * sides
        + [pltpu.VMEM((*x.shape[:-1], LANES), x.dtype) for x in ins] * 2
        + [pltpu.VMEM(cells.shape, cells.dtype), pltpu.SemaphoreType.DMA((sides + 2, 6))],
        compiler_params=pltpu.CompilerParams(vmem_limit_bytes=58 * 1024 * 1024),
        name="edges",
    )(cells, *ins)


def diagonal(x, first_row, first_col):
    count = lax.axis_size("col")
    perm = [
        (a * count + c, b * count + d)
        for a, b in pairs(lax.axis_size("row"), first_row)
        for c, d in pairs(count, first_col)
    ]
    return lax.ppermute(x, ("row", "col"), perm)


def rim_kernel(sides, events, steps, *refs):
    rims_in = refs[:sides]
    rim_top, rim_bottom = refs[sides:]
    cols = rim_top.shape[-1]
    even_row = lax.axis_index("row") % 2 == 0
    sub = lax.broadcasted_iota(jnp.int32, (SUB, cols), 0)
    slots, _ = plan(events, steps)
    nothing = jnp.zeros((SUB, cols), jnp.float32)

    def field(ref, n, slot):
        x = nothing
        for i in range(slot // SUB, (slot + n - 1) // SUB + 1):
            low, high = slot - i * SUB, slot + n - i * SUB
            y = ref[i * SUB : (i + 1) * SUB]
            y = pltpu.roll(y, -low % SUB, 0) if low % SUB else y
            x = jnp.where((sub >= -low) & (sub < min(n, SUB - low)) & (sub >= max(0, -low)), y, x)
        return x

    for f, (n, slot) in enumerate(slots):
        x = field(rims_in[0], n, slot)
        y = field(rims_in[1], n, slot) if sides > 1 else nothing
        rim_bottom[f] = jnp.where(even_row, x, y)
        rim_top[f] = pltpu.roll(jnp.where(even_row, y, x), SUB - n, 0)


def row_rims(rims, events, steps):
    vmem = pl.BlockSpec(memory_space=pltpu.VMEM)
    rim = jax.ShapeDtypeStruct((events * (steps + 2) + 3, SUB, rims[0].shape[-1]), jnp.float32)
    return pl.pallas_call(
        functools.partial(rim_kernel, len(rims), events, steps),
        in_specs=[vmem] * len(rims),
        out_specs=[vmem] * 2,
        out_shape=[rim] * 2,
        compiler_params=pltpu.CompilerParams(vmem_limit_bytes=4 * 1024 * 1024),
        name="row_rims",
    )(*rims)


def up(x):
    return pltpu.roll(x, SUB - 1, 0)


def down(x):
    return pltpu.roll(x, 1, 0)


def sublanes():
    return lax.broadcasted_iota(jnp.int32, (SUB, LANES), 0)


def to_right(x, nxt):
    last = lanes_of((SUB, LANES)) == LANES - 1
    return jnp.where(last, pltpu.roll(nxt, LANES - 1, 1), pltpu.roll(x, LANES - 1, 1))


def right(xs):
    last = lanes_of((SUB, LANES)) == LANES - 1
    r = [pltpu.roll(x, LANES - 1, 1) for x in xs]
    return [jnp.where(last, r[(j + 1) % len(xs)], r[j]) for j in range(len(xs))]


def left(xs):
    first = lanes_of((SUB, LANES)) == 0
    r = [pltpu.roll(x, 1, 1) for x in xs]
    return [jnp.where(first, r[j - 1], r[j]) for j in range(len(xs))]


def at_lanes(j):
    return slice(j * LANES, (j + 1) * LANES)


def get(ref, *at):
    return [ref[(*at, slice(None), at_lanes(j))] for j in range(ref.shape[-1] // LANES)]


def put(xs, ref, *at):
    for j, x in enumerate(xs):
        ref[(*at, slice(None), at_lanes(j))] = x


def followers(first, below, above):
    last = sublanes() == SUB - 1
    f, b, a = up(first), up(below), up(above)
    return jnp.where(last, b, f), b, jnp.where(last, f, a)


def follow(ref, *at):
    deep = ref.shape[-3] - 5
    sets = zip(get(ref, *at, 0), get(ref, *at, deep), get(ref, *at, deep + 1))
    for k, xs in enumerate(zip(*[followers(*x) for x in sets])):
        put(xs, ref, *at, deep + 2 + k)


def preceding(ref, deep, passed):
    first = sublanes() == 0
    last, below, above = get(ref, deep), get(ref, deep + 1), get(ref, deep + 2)
    return (
        [jnp.where(first, down(a), down(l)) for a, l in zip(above, last)],
        [jnp.where(first, down(l), down(b)) - l for b, l in zip(below, last)],
        [down(a) - b for a, b in zip(above, below)],
    )


def face(h, h_k, sb, cond, inv):
    hs = h + h_k
    s = (h_k - h) + sb
    x = s * s + slope_floor
    y = lax.rsqrt(x)
    p = cond * (jnp.exp2((2.0 / 3.0 / LN2) * jnp.log(hs)) * (y * lax.rsqrt(y)))
    ps = p * s
    t = p * hs
    B = t * (0.3 + (0.3 * slope_floor) * (y * y))
    return ps - B, ps + B, (t * s) * inv


scale = (5.0 / 3.0) * time_step * 2.0 ** (-2.0 / 3.0)


def inner_kernel(
    depth, wet, bed, rough, direction,
    prim, a_x, b_x, c_x, a_y, b_y, c_y, q_x, q_y,
    nat, sb_x, sb_y, inv_x, inv_y, cond_x, cond_y,
):
    events, steps, rows, cols = depth.shape
    deep, count = rows // SUB, cols // LANES
    fields = [bed, rough, direction] + [wet.at[e] for e in range(events)]
    fields += [depth.at[e, t] for e in range(events) for t in range(steps)]
    for k, x in enumerate(fields):
        for j in range(count):
            nat[k, j] = x[:, at_lanes(j)].astype(jnp.float32)

    @pl.loop(0, deep, unroll=deep)
    def _(i):
        spread = lambda k: [nat[k, j, pl.ds(i, SUB, stride=deep), :] for j in range(count)]
        m = [jnp.exp(x) for x in spread(1)]
        put(spread(0), prim, 0, i)
        put(m, prim, 1, i)
        put([x * y for x, y in zip(m, spread(2))], prim, 2, i)
        for k in range(3, 3 + events * (steps + 1)):
            put(spread(k), prim, k, i)

    for k in range(3 + events * (steps + 1)):
        put([up(x) for x in get(prim, k, 0)], prim, k, deep)

    @pl.loop(0, deep, unroll=deep)
    def _(i):
        b, m, q = (get(prim, k, i) for k in range(3))
        put([y - x for x, y in zip(b, right(b))], sb_x, i)
        put([y - x for x, y in zip(b, get(prim, 0, i + 1))], sb_y, i)
        ix = [1.0 / (x + y) for x, y in zip(m, right(m))]
        iy = [1.0 / (x + y) for x, y in zip(m, get(prim, 1, i + 1))]
        put([-0.6 * x for x in ix], inv_x, i)
        put([-0.6 * x for x in iy], inv_y, i)
        put([x + y for x, y in zip(q, right(q))], q_x, i)
        put([x + y for x, y in zip(q, get(prim, 2, i + 1))], q_y, i)
        for e in range(events):
            w = get(prim, 3 + e, i)
            put([(scale * z) * (x * y) for x, y, z in zip(w, right(w), ix)], cond_x, e, i)
            put([(scale * z) * (x * y) for x, y, z in zip(w, get(prim, 3 + e, i + 1), iy)], cond_y, e, i)

    @pl.loop(0, events)
    def _(e):
        for t in range(steps):

            @pl.loop(0, deep, unroll=deep)
            def _(i):
                k = 3 + events + e * steps + t
                h = get(prim, k, i)
                h_r, h_d = right(h), get(prim, k, i + 1)
                for j in range(count):
                    J = at_lanes(j)
                    for h_k, sb, cond, inv, a, b, c in (
                        (h_r, sb_x, cond_x, inv_x, a_x, b_x, c_x),
                        (h_d, sb_y, cond_y, inv_y, a_y, b_y, c_y),
                    ):
                        A, B, C = face(h[j], h_k[j], sb[i, :, J], cond[e, i, :, J], inv[i, :, J])
                        c[e, t, i, :, J] = C
                        if t:
                            a[e, t - 1, i, :, J] = A
                            b[e, t - 1, i, :, J] = B


def inner(depth, wet, bed, rough, direction):
    events, steps, rows, cols = depth.shape
    deep = rows // SUB
    shape = lambda *lead: (*lead, deep, SUB, cols)
    vm = lambda *lead: pltpu.VMEM(shape(*lead), jnp.float32)
    out = lambda *lead: jax.ShapeDtypeStruct(shape(*lead), jnp.float32)
    vmem = pl.BlockSpec(memory_space=pltpu.VMEM)
    fields = 3 + events * (steps + 1)
    return pl.pallas_call(
        inner_kernel,
        in_specs=[vmem] * 5,
        out_specs=[vmem] * 9,
        out_shape=[
            jax.ShapeDtypeStruct((fields, deep + 1, SUB, cols), jnp.float32),
            *[out(events, steps - 1), out(events, steps - 1), out(events, steps)] * 2,
            out(),
            out(),
        ],
        scratch_shapes=[
            pltpu.VMEM((fields, cols // LANES, rows, LANES), jnp.float32),
            *[vm()] * 4,
            *[vm(events)] * 2,
        ],
        compiler_params=pltpu.CompilerParams(vmem_limit_bytes=12 * 1024 * 1024),
        cost_estimate=pl.CostEstimate(flops=100000000, bytes_accessed=16000000, transcendentals=0),
        name="inner",
    )(depth, wet, bed, rough, direction)


def tangent_kernel(
    prim, cnt, ia_x, ib_x, ic_x, ia_y, ib_y, ic_y, iq_x, iq_y, rim_top, rim_bottom, side_a, side_b,
    corner_aa, corner_ab, corner_ba, corner_bb, curve_ref, source, a_x, b_x, c_x, a_y, b_y, c_y,
    nat, ext, xcnt, sb_x, sb_y, q_x, q_y, inv_x, inv_y, cond_x, cond_y, tan_a, tan_b, flow,
):
    events, steps, deep, _, cols = ic_x.shape
    rows, tiles = deep * SUB, cols // LANES
    count, tall = tiles + 1, rows + 2 * SUB
    even_col = lax.axis_index("col") % 2 == 0
    lane_t = lanes_of((tall, LANES))
    even_row = lax.axis_index("row") % 2 == 0

    def whole_side(side, corner_a, corner_b):
        above = jnp.where(even_row, corner_b[...], corner_a[...])
        below = jnp.where(even_row, corner_a[...], corner_b[...])
        return jnp.concatenate([above, side[...], below], axis=0)

    full_a, full_b = whole_side(side_a, corner_aa, corner_ba), whole_side(side_b, corner_ab, corner_bb)
    right_rim = jnp.where(even_col, full_a, full_b)
    left_rim = jnp.where(even_col, full_b, full_a)
    J = [at_lanes(j) for j in range(count)]
    zero = jnp.zeros((SUB, LANES), jnp.float32)
    below, above = deep, deep + 1
    fields = prim.shape[0]

    place_in = [events * (steps + 1) + k for k in range(3)]
    place_in += [events * steps + e for e in range(events)]
    place_in += [e * steps + t for e in range(events) for t in range(steps)]
    place_in += [events * (steps + 1) + 3 + e for e in range(events)]
    for k, f in enumerate(place_in):
        place = f * REACH
        r = pltpu.roll(right_rim, (LANES - place) % LANES, 1) if place else right_rim
        l = pltpu.roll(left_rim, (LANES - REACH - place) % LANES, 1)
        x = jnp.where(lane_t < REACH, r, jnp.where(lane_t >= LANES - REACH, l, 0.0))
        if k == 1:
            m_side = x = jnp.exp(x)
        if k == 2:
            x = m_side * x
        nat[k] = x
        to, n = (ext, k) if k < fields else (xcnt, k - fields)
        for i in range(deep):
            to[n, i, :, J[tiles]] = nat[k, pl.ds(SUB + i, SUB, stride=deep), :]
        for i, rim, at in ((below, rim_bottom, SUB + rows), (above, rim_top, 0)):
            xs = get(rim, f)
            if k == 1:
                xs = [jnp.exp(x) for x in xs]
            if k == 2:
                xs = [x * y for x, y in zip(xs, get(ext, 1, i))]
            put(xs, to, n, i)
            to[n, i, :, J[tiles]] = nat[k, at : at + SUB, :]

    def value(k, i, j):
        return ext[k, i, :, J[j]] if j == tiles or (isinstance(i, int) and i >= deep) else prim[k, i, :, J[j]]

    def next_rows(k, j):
        return followers(value(k, 0, j), value(k, below, j), value(k, above, j))

    for k in range(fields):
        ext[k, deep + 2, :, J[tiles]] = next_rows(k, tiles)[0]

    def derive(i, j, along, k_of):
        sb, inv, q, cond = (sb_x, inv_x, q_x, cond_x) if along else (sb_y, inv_y, q_y, cond_y)
        x, y = k_of(0)
        sb[i, :, J[j]] = y - x
        x, y = k_of(1)
        z = 1.0 / (x + y)
        inv[i, :, J[j]] = -0.6 * z
        x, y = k_of(2)
        q[i, :, J[j]] = x + y
        for e in range(events):
            x, y = k_of(3 + e)
            cond[e, i, :, J[j]] = (scale * z) * (x * y)

    def across(i, j):
        return lambda k: (value(k, i, j), to_right(value(k, i, j), value(k, i, (j + 1) % count)))

    @pl.loop(0, deep, unroll=4)
    def _(i):
        for j in (tiles - 1, tiles):
            derive(i, j, True, across(i, j))
        n = jnp.where(i == deep - 1, deep + 2, i + 1)
        derive(i, tiles, False, lambda k: (value(k, i, tiles), ext[k, n, :, J[tiles]]))

    for i in (below, above):
        for j in range(count):
            derive(i, j, True, across(i, j))
    for n, i in enumerate((deep - 1, below, above)):
        for j in range(tiles if n == 0 else count):
            derive(i, j, False, lambda k: (value(k, i, j), next_rows(k, j)[n]))

    curve_ref[...] = jnp.zeros(curve_ref.shape, jnp.float32)
    put([zero] * count, flow, 0)

    @pl.loop(0, events)
    def _(e):
        for t in range(steps):
            old, new = (tan_a, tan_b) if t % 2 else (tan_b, tan_a)
            k = 3 + events + e * steps + t

            def row(i):
                static = isinstance(i, int)
                rim = static and i >= deep
                nxt = i + 3 if static and i >= deep - 1 else i + 1
                if t:
                    d = get(old, i)
                    d_r, d_d = right(d), get(old, nxt)
                fx, fy = [], []
                here = lambda j: ext[k, i, :, J[j]] if rim or j == tiles else prim[k, i, :, J[j]]
                for j in range(count):
                    inside = not rim and j < tiles - 1
                    if inside:
                        A, B = (ia_x[e, t - 1, i, :, J[j]], ib_x[e, t - 1, i, :, J[j]]) if t else (None, None)
                        C = ic_x[e, t, i, :, J[j]]
                        f = C * iq_x[i, :, J[j]]
                    else:
                        h = here(j)
                        A, B, C = face(
                            h, to_right(h, here((j + 1) % count)),
                            sb_x[i, :, J[j]], cond_x[e, i, :, J[j]], inv_x[i, :, J[j]],
                        )
                        f = C * q_x[i, :, J[j]]
                    c_x[e, t, i, :, J[j]] = C
                    if t:
                        a_x[e, t - 1, i, :, J[j]] = A
                        b_x[e, t - 1, i, :, J[j]] = B
                        f += A * d[j] + B * d_r[j]
                    fx.append(f)
                    inside = not (static and i >= deep - 1) and j < tiles
                    if inside:
                        A, B = (ia_y[e, t - 1, i, :, J[j]], ib_y[e, t - 1, i, :, J[j]]) if t else (None, None)
                        C = ic_y[e, t, i, :, J[j]]
                        f = C * iq_y[i, :, J[j]]
                    else:
                        h = here(j)
                        if static and i >= deep - 1:
                            first = ext[k, 0, :, J[j]] if j == tiles else prim[k, 0, :, J[j]]
                            h_d = followers(first, ext[k, below, :, J[j]], ext[k, above, :, J[j]])[i - deep + 1]
                        else:
                            h_d = ext[k, i + 1, :, J[j]]
                        A, B, C = face(h, h_d, sb_y[i, :, J[j]], cond_y[e, i, :, J[j]], inv_y[i, :, J[j]])
                        f = C * q_y[i, :, J[j]]
                    c_y[e, t, i, :, J[j]] = C
                    if t:
                        a_y[e, t - 1, i, :, J[j]] = A
                        b_y[e, t - 1, i, :, J[j]] = B
                        f += A * d[j] + B * d_d[j]
                    fy.append(f)
                put(fy, flow, i + 1)
                before = get(flow, i)
                fl = left(fx)
                for j in range(count):
                    r = (fx[j] - fl[j]) + (fy[j] - before[j])
                    new[i, :, J[j]] = d[j] + r if t else r

            main = deep - 2
            pl.loop(0, main, unroll=3 if main % 3 == 0 else 1)(row)
            for i in range(main, deep + 2):
                row(i)
            for i, lack in zip((0, below, above), preceding(flow, deep, zero)):
                put([x - y for x, y in zip(get(new, i), lack)], new, i)
            follow(new)

        old = tan_a if steps % 2 else tan_b
        total = zero
        for i in range(deep + 2):
            for j in range(count):
                own = i < deep and j < tiles
                n = cnt[e, j, pl.ds(i, SUB, stride=deep), :] if own else xcnt[e, i, :, J[j]]
                r = old[i, :, J[j]]
                s = (gauge_weight * n) * r
                source[e, i, :, J[j]] = s
                if own:
                    total += s * r
        curve_ref[...] += total
        follow(source, e)


def tangents(prim, cnt, *more_inputs):
    fields, _, _, cols = prim.shape
    events, deep = cnt.shape[0], prim.shape[1] - 1
    steps = more_inputs[2].shape[1]
    wide = cols + LANES
    regs = deep + 2
    vm = lambda *lead: pltpu.VMEM((*lead, regs, SUB, wide), jnp.float32)
    more = lambda *lead: pltpu.VMEM((*lead, regs + 3, SUB, wide), jnp.float32)
    out = lambda *lead: jax.ShapeDtypeStruct((*lead, regs, SUB, wide), jnp.float32)
    vmem = pl.BlockSpec(memory_space=pltpu.VMEM)
    return pl.pallas_call(
        tangent_kernel,
        in_specs=[vmem] * (2 + len(more_inputs)),
        out_specs=[vmem] * 8,
        out_shape=[
            jax.ShapeDtypeStruct((SUB, LANES), jnp.float32),
            jax.ShapeDtypeStruct((events, regs + 3, SUB, wide), jnp.float32),
            *[out(events, steps - 1), out(events, steps - 1), out(events, steps)] * 2,
        ],
        scratch_shapes=[
            pltpu.VMEM((fields + events, deep * SUB + 2 * SUB, LANES), jnp.float32),
            more(fields),
            vm(events),
            *[vm()] * 6,
            *[vm(events)] * 2,
            *[more()] * 3,
        ],
        compiler_params=pltpu.CompilerParams(vmem_limit_bytes=16 * 1024 * 1024),
        name="tangents",
    )(prim, cnt, *more_inputs)


def adjoint_kernel(first_event, last_event, m_c, source, a_x, b_x, c_x, a_y, b_y, c_y, *refs):
    sums = () if first_event else refs[:2]
    outs = refs[len(sums) : len(sums) + (1 if last_event else 2)]
    nat, adj_a, adj_b, flow, *own = refs[len(sums) + len(outs) :]
    g_x, g_y = own if last_event else outs
    steps, regs, _, wide = c_x.shape
    deep = regs - 2
    count = wide // LANES
    J = [at_lanes(j) for j in range(count)]
    zero = jnp.zeros((SUB, LANES), jnp.float32)
    put([zero] * count, flow, 0)

    for t in range(steps - 1, -1, -1):
        old, new = (adj_a, adj_b) if t % 2 else (adj_b, adj_a)
        if t == steps - 1:
            old = source
            base_x, base_y = sums if sums else (None, None)
        else:
            base_x, base_y = g_x, g_y

        @pl.loop(0, regs, unroll=5 if regs % 5 == 0 else 1)
        def _(i):
            l = get(old, i)
            l_r, l_d = right(l), get(old, jnp.where(i < deep - 1, i + 1, i + 3))
            acc, kx, ky = [], [], []
            for j in range(count):
                p = l[j] - l_r[j]
                g = c_x[t, i, :, J[j]] * p
                g_x[i, :, J[j]] = g + base_x[i, :, J[j]] if base_x is not None else g
                if t:
                    a = l[j] + a_x[t - 1, i, :, J[j]] * p
                    kx.append(b_x[t - 1, i, :, J[j]] * p)
                p = l[j] - l_d[j]
                g = c_y[t, i, :, J[j]] * p
                g_y[i, :, J[j]] = g + base_y[i, :, J[j]] if base_y is not None else g
                if t:
                    acc.append(a + a_y[t - 1, i, :, J[j]] * p)
                    ky.append(b_y[t - 1, i, :, J[j]] * p)
            if t:
                put(ky, flow, i + 1)
                before = get(flow, i)
                kl = left(kx)
                for j in range(count):
                    new[i, :, J[j]] = acc[j] + (kl[j] + before[j])

        if t:
            for i, lack in zip((0, deep, deep + 1), preceding(flow, deep, zero)):
                put([x + y for x, y in zip(get(new, i), lack)], new, i)
            follow(new)

    if last_event:
        (grad_ref,) = outs
        tiles = grad_ref.shape[-1] // LANES
        first = sublanes() == 0
        put(
            [jnp.where(first, down(a), down(l)) for a, l in zip(get(g_y, deep + 1), get(g_y, deep - 1))],
            flow,
            0,
        )

        @pl.loop(0, deep, unroll=4)
        def _(i):
            x, y = get(g_x, i), get(g_y, i)
            put(y, flow, i + 1)
            xl, yl = left(x), get(flow, i)
            for j in range(tiles):
                g = m_c[i, :, J[j]] * ((x[j] + xl[j]) + (y[j] + yl[j]))
                nat[j, pl.ds(i, SUB, stride=deep), :] = g

        for j in range(tiles):
            grad_ref[:, J[j]] = nat[j]


def gradient(e, sums, prim, source, *coefficients):
    events, entries, _, wide = source.shape
    cols, regs = prim.shape[-1], entries - 3
    rows = (regs - 2) * SUB
    first, last = e == 0, e == events - 1
    vm = (regs, SUB, wide)
    more = pltpu.VMEM((entries, SUB, wide), jnp.float32)
    own = lambda x: pl.BlockSpec((None, *x.shape[1:]), lambda i: (e,) + (0,) * (x.ndim - 1))
    whole = lambda shape: pl.BlockSpec(shape, lambda i: (0,) * len(shape))
    return pl.pallas_call(
        functools.partial(adjoint_kernel, first, last),
        grid=(1,),
        in_specs=[pl.BlockSpec((None, *prim.shape[1:]), lambda i: (1, 0, 0, 0)), own(source)]
        + [own(x) for x in coefficients]
        + [whole(vm)] * len(sums),
        out_specs=whole((rows, cols)) if last else [whole(vm)] * 2,
        out_shape=jax.ShapeDtypeStruct((rows, cols), jnp.float32)
        if last
        else [jax.ShapeDtypeStruct(vm, jnp.float32)] * 2,
        scratch_shapes=[pltpu.VMEM((cols // LANES, rows, LANES), jnp.float32), more, more, more]
        + [pltpu.VMEM(vm, jnp.float32)] * (2 if last else 0),
        compiler_params=pltpu.CompilerParams(vmem_limit_bytes=16 * 1024 * 1024),
        cost_estimate=pl.CostEstimate(flops=40000000, bytes_accessed=12000000, transcendentals=0),
        name="gradient",
    )(prim, source, *coefficients, *sums)


def hops_over(axis):
    count, hop, out = lax.axis_size(axis), 1, []
    while hop < count:
        out.append((axis, hop))
        hop *= 2
    return out


def from_hop(x, axis, hop):
    return lax.ppermute(x, axis, [(i, i ^ hop) for i in range(lax.axis_size(axis))])


def hop_sum(x, axis, hop):
    return x + from_hop(x, axis, hop)


def finish_kernel(grad, arrived, curve, curve_arrived, hess, total):
    hess[...] = grad[...] + arrived[...]
    total[...] = jnp.sum(curve[...] + curve_arrived[...], keepdims=True)


def finish(grad, arrived, curve, curve_arrived):
    vmem = pl.BlockSpec(memory_space=pltpu.VMEM)
    hess, total = pl.pallas_call(
        finish_kernel,
        in_specs=[vmem] * 4,
        out_specs=[vmem] * 2,
        out_shape=[jax.ShapeDtypeStruct(grad.shape, grad.dtype), jax.ShapeDtypeStruct((1, 1), curve.dtype)],
        compiler_params=pltpu.CompilerParams(vmem_limit_bytes=4 * 1024 * 1024),
        name="finish",
    )(grad, arrived, curve, curve_arrived)
    return (hess, total.reshape(()))


def local(depth, wet, bed, rough, direction, gauge_cells):
    events, steps, rows, cols = depth.shape
    cells = gauge_cells.reshape(events, 1, -1)
    sides = 2 if lax.axis_size("row") > 2 else 1
    counts, send_a, send_b, *more = edges_and_gauges(cells, depth, wet, bed, rough, direction)
    rims = [exchange(x, "row", k) for k, x in enumerate(more[:sides])]
    side_a = exchange(send_a, "col", 0)
    side_b = exchange(send_b, "col", 1)
    corners = [diagonal(x, k // 2, k % 2) for k, x in enumerate(more[sides:])]
    block = inner(depth, wet, bed, rough, direction)
    rims, side_a, side_b, corners, block = lax.optimization_barrier((rims, side_a, side_b, corners, block))
    if sides == 1:
        corners = corners + [jnp.zeros_like(x) for x in corners]
    rim_top, rim_bottom = row_rims(rims, events, steps)
    curve, *coefficients = tangents(block[0], counts, *block[1:], rim_top, rim_bottom, side_a, side_b, *corners)
    hops = hops_over("event") + hops_over("row") + hops_over("col")
    sums = ()
    for e in range(events):
        sums = gradient(e, sums, block[0], *coefficients)
        if hops:
            curve = hop_sum(curve, *hops.pop(0))
            sums, curve = lax.optimization_barrier((sums, curve))
    grad, arrived = sums, None
    for axis, hop in hops_over("event"):
        if arrived is not None:
            grad = grad + arrived
            if hops:
                curve = hop_sum(curve, *hops.pop(0))
                grad, curve = lax.optimization_barrier((grad, curve))
        arrived = from_hop(grad, axis, hop)
    while len(hops) > 1:
        curve = hop_sum(curve, *hops.pop(0))
    return finish(grad, arrived, curve, from_hop(curve, *hops[0]))


def solution(mesh):
    placed = (
        P("event", None, "row", "col"),
        P("event", "row", "col"),
        P("row", "col"),
        P("row", "col"),
        P("row", "col"),
        P("event", "row", "col", None),
    )
    return jax.shard_map(
        local, mesh=mesh, in_specs=placed, out_specs=(P("row", "col"), P()), check_vma=False
    )
```
